32 devices in a mesh: groups: 2 (over y), tm: 4 (over z), height: 2 (over x), chan: 2 (over core).
Axes of the slice: x: 2, y: 2, z: 4, core: 2. Of those that a mesh axis runs over, the one named last changes fastest.
Arguments:
- clip_video: bfloat16 [64, 32, 16, 256], P(('groups', 'tm'), 'height', None, 'chan'), parts along dimension 0, may hold values from -60 to 60
- norm_gain: float32 [256], P('chan'), may hold values from 0.25 to 1.75
- norm_bias: float32 [256], P('chan'), may hold values from -3 to 3
- conv_weight: bfloat16 [3, 3, 3, 256, 256], replicated, may hold values from -0.078125 to 0.078125
- clip_lengths: int32 [16], P('groups'), parts along dimension 0, may hold values from 1 to 24, 32 in all
- packed_frame: int32 [64], P(('groups', 'tm')), parts along dimension 0, may hold values from 0 to 31, as said below
- packed_grad: bfloat16 [64, 32, 16, 256], P(('groups', 'tm'), 'height', None, 'chan'), parts along dimension 0, may hold values from -6 to 6
Outputs:
- block_out: bfloat16 [64, 32, 16, 256], P(('groups', 'tm'), 'height', None, 'chan'), parts along dimension 0
- video_grad: bfloat16 [64, 32, 16, 256], P(('groups', 'tm'), 'height', None, 'chan'), parts along dimension 0
- weight_grad: float32 [6, 3, 3, 256, 256], P('groups', None, None, ('tm', 'height'), 'chan'), parts along dimension 0
- gain_grad: float32 [512], P(('groups', 'chan')), parts along dimension 0
- bias_grad: float32 [512], P(('groups', 'chan')), parts along dimension 0
The draws below stay inside these ranges and needn't reach their ends.
There are 2 independent parts, one for each index of `groups`. The reference program is written for one: setup_inputs(seed, part) draws one part's arguments, and reference() takes and returns one part's arrays. A program takes and returns all parts, laid end to end along the dimension named above; an argument that names none is the same for every part. Nothing has to cross between parts.
Inputs may be any that keep to these rules, and one draw needn't show every extreme that they name: `packed_frame`: A permutation of the 32 frames. Each aligned block of 8 packed slots holds frames of exactly 4 time slabs of 8 frames, the same count 2 from each of them, and no frame of the other slabs. `clip_lengths`: the lengths sum to 32; the longest clip has exactly 24 frames.
All inputs are finite; a program needn't handle non-finite values.
Results may differ from the reference program's by a relative error of at most 0.0017.
Values may be sent and summed in bfloat16 or wider, within the bound.
No kernel may reach another device: no remote copies, remote signals or barrier semaphores. Data moves between devices by JAX's collectives and lax.ppermute only.
A program may use at most 128 MiB of HBM per device.

```python
import math
import jax
import jax.numpy as jnp
import numpy as np
from jax import lax

C = 256
GROUPS = 32
TD = 8
WD = 16
NCLIPS = 8
FRAMES = 32
HEIGHT = 32
MOST = 24
N_TM = 4


def draw_clip_video(key, part):
    subkeys = jax.random.split(key, 4)
    full_shape = (FRAMES, HEIGHT, WD, C)
    channel_scale = jnp.exp(jax.random.uniform(subkeys[0], (C,), jnp.float32, math.log(0.2), math.log(2.0)))
    channel_mean = 2.0 * jnp.clip(jax.random.normal(subkeys[1], (C,), jnp.float32), -2.0, 2.0)
    frame_scale = 3.0 ** (jnp.arange(FRAMES, dtype=jnp.float32) / FRAMES)
    frame_scale = frame_scale * jax.random.uniform(subkeys[2], (FRAMES,), jnp.float32, 0.7, 1.2)
    base_value = jnp.clip(jax.random.normal(subkeys[3], full_shape, jnp.float32), -4.0, 4.0)
    values = (base_value + channel_mean) * channel_scale * frame_scale[:, None, None, None]
    return values.astype(jnp.bfloat16)


def draw_packed_grad(key, part):
    subkeys = jax.random.split(key, 2)
    full_shape = (FRAMES, HEIGHT, WD, C)
    channel_offset = jnp.clip(jax.random.normal(subkeys[0], (C,), jnp.float32), -2.0, 2.0)
    noise_value = jnp.clip(jax.random.normal(subkeys[1], full_shape, jnp.float32), -4.0, 4.0)
    values = noise_value + channel_offset
    return values.astype(jnp.bfloat16)


def draw_packed_frame(key, part):
    capacity = max(1, TD // N_TM)
    piece_count = TD // capacity
    shift_key, order_key = jax.random.split(key)
    shifts = jax.random.permutation(shift_key, N_TM)[:piece_count]
    slot_index = jnp.arange(TD, dtype=jnp.int32)
    target_block = jnp.arange(N_TM, dtype=jnp.int32)
    owner_slab = (target_block[:, None] - shifts[slot_index // capacity][None, :]) % N_TM
    frame_number = owner_slab * TD + slot_index[None, :]
    order_keys = jax.random.split(order_key, N_TM)
    orders = jax.vmap(lambda one_key: jax.random.permutation(one_key, TD))(order_keys)
    inverse = jnp.argsort(orders, axis=1)
    packed = jnp.take_along_axis(frame_number, inverse, axis=1)
    return packed.reshape(-1).astype(jnp.int32)


def level_of(stream_key, shape, cuts, smallest, largest):
    loudness, own = 1.0, jax.random.fold_in(stream_key, 6)
    for dim, blocks in cuts:
        draws = jnp.exp(jax.random.uniform(jax.random.fold_in(own, dim), (blocks,), jnp.float32, smallest / len(cuts), largest / len(cuts)))
        loudness = loudness * jnp.repeat(draws, shape[dim] // blocks).reshape([-1 if axis == dim else 1 for axis in range(len(shape))])
    return loudness


def split_up(count, total, reach, lean):
    portions = [(1 << 20) // math.isqrt(rank ** lean) + 1 for rank in range(2, count + 1)]
    surplus, given = total - reach - (count - 1), [1] * (count - 1)
    while surplus > 0:
        candidates = [i for i in range(count - 1) if given[i] < reach]
        whole, left = sum([portions[i] for i in candidates]), surplus
        for i in candidates:
            extra = min(reach - given[i], max(1, left * portions[i] // whole), surplus)
            given[i] = given[i] + extra
            surplus = surplus - extra
    return np.array([reach] + given)


def uneven(stream_key, number_of, total, limit, skew):
    if number_of == 2:
        one = jax.random.randint(stream_key, (), max(1, total - limit), min(limit, total - 1) + 1)
        return jnp.stack([one, total - one])
    tallies = jnp.asarray(split_up(number_of, total, limit, skew), jnp.int32)
    couples = (number_of - 1) // 2
    giver, taker = tallies[1:1 + 2 * couples:2], tallies[2:2 + 2 * couples:2]
    slack = jnp.minimum(giver - 1, limit - taker)
    moved = jax.random.randint(jax.random.fold_in(stream_key, 1), (couples,), 0, 1 << 20) % (slack + 1)
    tallies = tallies.at[1:1 + 2 * couples:2].set(giver - moved).at[2:2 + 2 * couples:2].set(taker + moved)
    return tallies[jax.random.permutation(jax.random.fold_in(stream_key, 2), number_of)]


def gaussian(stream_key, shape, scale, limit, cuts=(), kind=jnp.bfloat16):
    drawn = jax.random.normal(stream_key, shape, jnp.float32) * scale
    if len(cuts) > 0:
        drawn = level_of(stream_key, shape, cuts, -0.22, 0.18) * drawn
    return jnp.clip(drawn, min=-limit, max=limit).astype(kind)


def setup_inputs(seed: int = 0, part: int = 0) -> dict:
    keys = jax.random.split(jax.random.key(seed), 8)
    part_keys = jax.random.split(jax.random.fold_in(keys[7], part), 8)
    clip_video = draw_clip_video(jax.random.fold_in(jax.random.fold_in(keys[7], part), 71), part)
    norm_gain = jnp.clip(1.0 + 0.15 * jax.random.normal(keys[1], (C,), jnp.float32), 0.25, 1.75)
    norm_bias = gaussian(keys[2], (C,), 0.5, 3.0, ((0, 2),), jnp.float32)
    conv_weight = gaussian(keys[3], (3, 3, 3, C, C), (27 * C) ** -0.5, 0.078125)
    clip_lengths = uneven(part_keys[4], NCLIPS, FRAMES, MOST, 2).astype(jnp.int32)
    packed_frame = draw_packed_frame(jax.random.fold_in(jax.random.fold_in(keys[7], part), 71), part)
    packed_grad = draw_packed_grad(jax.random.fold_in(jax.random.fold_in(keys[7], part), 71), part)
    return {"clip_video": clip_video, "norm_gain": norm_gain, "norm_bias": norm_bias, "conv_weight": conv_weight, "clip_lengths": clip_lengths, "packed_frame": packed_frame, "packed_grad": packed_grad}


def clip_layout(clip_lengths, frame_count):
    frame_index = jnp.arange(frame_count, dtype=jnp.int32)
    clip_ends = jnp.cumsum(clip_lengths).astype(jnp.int32)
    passed = clip_ends[None, :] <= frame_index[:, None]
    clip_number = lax.optimization_barrier(jnp.sum(passed.astype(jnp.int32), axis=1))
    clip_start = lax.optimization_barrier(jnp.sum(jnp.where(passed, clip_lengths[None, :], 0), axis=1)).astype(jnp.int32)
    member = (clip_number[None, :] == jnp.arange(NCLIPS, dtype=jnp.int32)[:, None]).astype(jnp.float32)
    return (frame_index, clip_start, member)

def reference(clip_video, norm_gain, norm_bias, conv_weight, clip_lengths, packed_frame, packed_grad):
    frame_count, height, width, channels = clip_video.shape
    group_size = channels // GROUPS
    highest = lax.Precision.HIGHEST
    frame_index, clip_start, member = clip_layout(clip_lengths, frame_count)
    counts = clip_lengths.astype(jnp.float32) * (height * width * group_size)

    def totals(terms):
        return jnp.dot(member, terms, precision=highest)

    def spread(per_clip):
        return jnp.dot(member.T, per_clip, precision=highest)[:, None, None, :, None]
    grouped = clip_video.astype(jnp.float32).reshape(frame_count, height, width, GROUPS, group_size)
    mean = totals(lax.optimization_barrier(jnp.sum(grouped, axis=(1, 2, 4)))) / counts[:, None]
    centered = grouped - spread(mean)
    variance = totals(lax.optimization_barrier(jnp.sum(centered * centered, axis=(1, 2, 4)))) / counts[:, None]
    inv_std = spread(lax.rsqrt(variance + 1e-06))
    normal_hat5 = centered * inv_std
    normal_hat = normal_hat5.reshape(frame_count, height, width, channels)
    normed = normal_hat * norm_gain + norm_bias
    activ = jax.nn.silu(normed).astype(jnp.bfloat16)
    padded = jnp.pad(activ, ((0, 0), (1, 1), (1, 1), (0, 0)))
    sources = [jnp.maximum(frame_index - (2 - tap_time), clip_start) for tap_time in range(3)]
    upstream = jnp.zeros_like(packed_grad).at[packed_frame].set(packed_grad)
    flat_up = upstream.reshape(-1, channels)
    mixed = jnp.zeros((frame_count * height * width, channels), jnp.float32)
    grad_terms = []
    activ_grad = jnp.zeros((frame_count, height, width, channels), jnp.float32)
    for tap_time in range(3):
        taken = padded[sources[tap_time]]
        spatial = jnp.zeros((frame_count, height + 2, width + 2, channels), jnp.float32)
        for tap_row in range(3):
            for tap_col in range(3):
                window = taken[:, tap_row:tap_row + height, tap_col:tap_col + width, :].reshape(-1, channels)
                kernel = conv_weight[tap_time, tap_row, tap_col]
                mixed = mixed + jnp.dot(window, kernel, preferred_element_type=jnp.float32)
                grad_terms.append(jnp.dot(window.T, flat_up, preferred_element_type=jnp.float32))
                back = jnp.dot(flat_up, kernel.T, preferred_element_type=jnp.float32)
                spatial = spatial.at[:, tap_row:tap_row + height, tap_col:tap_col + width, :].add(back.reshape(frame_count, height, width, channels))
        activ_grad = activ_grad.at[sources[tap_time]].add(spatial[:, 1:-1, 1:-1, :])
    block_out = (clip_video.astype(jnp.float32).reshape(-1, channels) + mixed).astype(jnp.bfloat16)
    block_out = block_out.reshape(clip_video.shape)
    weight_grad = jnp.stack(grad_terms).reshape(3, 3, 3, channels, channels)
    sigmoid_value = jax.nn.sigmoid(normed)
    normed_grad = activ_grad * sigmoid_value * (1.0 + normed * (1.0 - sigmoid_value))
    gain_grad = lax.optimization_barrier(jnp.sum(normed_grad * normal_hat, axis=(0, 1, 2)))
    bias_grad = lax.optimization_barrier(jnp.sum(normed_grad, axis=(0, 1, 2)))
    scaled = (normed_grad * norm_gain).reshape(frame_count, height, width, GROUPS, group_size)
    first = totals(lax.optimization_barrier(jnp.sum(scaled, axis=(1, 2, 4)))) / counts[:, None]
    second = totals(lax.optimization_barrier(jnp.sum(scaled * normal_hat5, axis=(1, 2, 4)))) / counts[:, None]
    input_part = inv_std * (scaled - spread(first) - normal_hat5 * spread(second))
    video_grad = (upstream.astype(jnp.float32) + input_part.reshape(frame_count, height, width, channels)).astype(jnp.bfloat16)
    return (block_out, video_grad, weight_grad, gain_grad, bias_grad)
```

```python
import functools
import jax
import jax.numpy as jnp
from jax import lax
from jax.experimental import pallas as pl
from jax.experimental.pallas import tpu as pltpu
from jax.sharding import PartitionSpec as P

GROUPS = 32
NCLIPS = 8
F32 = jnp.float32
BF16 = jnp.bfloat16
HIGHEST = lax.Precision.HIGHEST
VM = pl.BlockSpec(memory_space=pltpu.VMEM)
SM = pl.BlockSpec(memory_space=pltpu.SMEM)


def call(body, out_shape, in_specs, scratch=(), flops=0, nbytes=0, name=None):
    return pl.pallas_call(
        body,
        out_shape=out_shape,
        in_specs=in_specs,
        out_specs=jax.tree.map(lambda _: VM, out_shape),
        scratch_shapes=list(scratch),
        compiler_params=pltpu.CompilerParams(vmem_limit_bytes=56 * 2**20),
        cost_estimate=pl.CostEstimate(flops=flops, bytes_accessed=nbytes, transcendentals=0),
        name=name,
    )


def fdot(a, b):
    return jnp.dot(a, b, precision=HIGHEST, preferred_element_type=F32)


def bdot(a, b):
    return jnp.dot(a, b, preferred_element_type=F32)


def ring(peers, by):
    return [(i, (i + by) % peers) for i in range(peers)]


def sibling(value):
    return lax.ppermute(value, "chan", ring(2, 1))


def sigmoid(v):
    return 1.0 / (1.0 + jnp.exp(-v))


def pack_body(peers, cap, pos, frames, grad, *outs):
    slots = frames.shape[0]
    slab_frames = slots
    tm = pos[0]
    number = [frames[i] for i in range(slots)]
    step = [lax.rem(n // slab_frames - tm + peers, peers) for n in number]
    rank = []
    for i in range(slots):
        r = jnp.int32(0)
        for j in range(i):
            r = r + jnp.where(step[j] == step[i], 1, 0)
        rank.append(r)
    rows = grad.shape[1]
    for k in range(peers):
        for j in range(cap):
            index = jnp.int32(0)
            local = jnp.int32(-1)
            for i in range(slots):
                hit = jnp.logical_and(step[i] == k, rank[i] == j)
                index = jnp.where(hit, i, index)
                local = jnp.where(hit, lax.rem(number[i], slab_frames), local)
            outs[k][j, :rows] = grad[index]
            outs[k][j, rows:] = jnp.full((1,) + grad.shape[2:], local.astype(F32), F32).astype(BF16)


def stat_body(video, gain, bias, average, out):
    frames, rows, cols, chans = video.shape
    cells = rows * cols
    sums = [
        jnp.sum(video[t].astype(F32).reshape(cells, chans), axis=0, keepdims=True)
        for t in range(frames)
    ]
    mean = fdot(jnp.concatenate(sums, axis=0) * (1.0 / cells), average[...])
    squares = []
    for t in range(frames):
        apart = video[t].astype(F32).reshape(cells, chans) - mean[t : t + 1]
        squares.append(jnp.sum(apart * apart, axis=0, keepdims=True))
    var = fdot(jnp.concatenate(squares, axis=0) * (1.0 / cells), average[...])
    rest = jnp.concatenate(
        [gain[...], bias[...], jnp.zeros((6, chans), F32)], axis=0
    )
    whole = jnp.concatenate([mean, var, rest], axis=0)
    for i in range(out.shape[0]):
        out[i] = whole


def table_body(got, same, picked, out):
    peers, bands = got.shape[:2]
    frames = (got.shape[3] - 8) // 2
    for c in range(2):
        mean = [
            jnp.concatenate([got[t, h, c, :frames] for t in range(peers)], axis=0)
            for h in range(bands)
        ]
        var = [
            jnp.concatenate([got[t, h, c, frames : 2 * frames] for t in range(peers)], axis=0)
            for h in range(bands)
        ]
        average = sum(mean[1:], mean[0]) * (1.0 / bands)
        clip_mean = fdot(same[...], average)
        spread = jnp.zeros_like(average)
        for h in range(bands):
            apart = mean[h] - clip_mean
            spread = spread + (var[h] + apart * apart)
        out[c, :16] = fdot(picked[...], average)
        out[c, 16:32] = lax.rsqrt(fdot(picked[...], spread * (1.0 / bands)) + 1e-06)
        out[c, 32:] = got[0, 0, c, 2 * frames :]


def shifts(value):
    length = value.shape[0]
    column = lax.rem(lax.broadcasted_iota(jnp.int32, value.shape, 0), 16)
    before = jnp.where(column == 0, 0.0, pltpu.roll(value, 1, 0))
    after = jnp.where(column == 15, 0.0, pltpu.roll(value, length - 1, 0))
    return before, after


def weight_body(peers, bands, cap, block, *refs):
    refs = list(refs)
    pos, source, table, pick_own, pick_sib = [refs.pop(0) for _ in range(5)]
    take = lambda n: [refs.pop(0) for _ in range(n)]
    own, sib, prev_own, prev_sib = take(bands), take(bands), take(bands), take(bands)
    ups = [take(peers) for _ in range(bands)]
    outs = take(peers)
    active, upright = refs
    frames, rows, cols, chans = own[0].shape
    cells = rows * cols
    width = peers * block
    c = pos[1]
    h = pos[2]
    band = [lax.rem(h - m + bands, bands) for m in range(bands)]
    lookup = fdot(table[c], pick_own[...].astype(F32)) + fdot(
        table[1 - c], pick_sib[...].astype(F32)
    )
    mean, inv = lookup[:16], lookup[16:32]
    scale = inv * lookup[32:33]
    bias = lookup[33:34]
    active[:, 0] = jnp.zeros((active.shape[0], cols, 3 * width), BF16)
    active[:, bands * rows + 1] = jnp.zeros((active.shape[0], cols, 3 * width), BF16)
    for f in range(frames + 2):
        for m in range(bands):
            if f < 2:
                a, b = prev_own[m][f], prev_sib[m][f]
            else:
                a, b = own[m][f - 2], sib[m][f - 2]
            x = bdot(a.reshape(cells, chans), pick_own[...]) + bdot(
                b.reshape(cells, chans), pick_sib[...]
            )
            v = (x - mean[f : f + 1]) * scale[f : f + 1] + bias
            v = v * sigmoid(v)
            before, after = shifts(v)
            at = pl.ds(band[m] * rows + 1, rows)
            active[f, at, :, :width] = before.astype(BF16).reshape(rows, cols, width)
            active[f, at, :, width : 2 * width] = v.astype(BF16).reshape(rows, cols, width)
            active[f, at, :, 2 * width :] = after.astype(BF16).reshape(rows, cols, width)
    for k in range(peers):
        for j in range(cap):
            local = jnp.max(ups[0][k][j, rows].astype(F32)).astype(jnp.int32)

            @pl.when(local >= 0)
            def _():
                for m in range(bands):
                    u = ups[m][k][j, :rows].reshape(cells, chans)
                    upright[local, m] = u.T

    def tap(i, carry):
        a = i // 3
        b = lax.rem(i, 3)
        total = jnp.zeros((chans, 3 * width), F32)
        for t in range(frames):
            s = source[t * 3 + a]
            for m in range(bands):
                patch = active[s, pl.ds(band[m] * rows + b, rows)].reshape(cells, 3 * width)
                total = total + bdot(upright[t, m], patch)
        for col in range(3):
            piece = total[:, col * width : (col + 1) * width].T
            for k in range(peers):
                outs[k][i * 3 + col] = piece[k * block : (k + 1) * block].astype(outs[k].dtype)
        return carry

    lax.fori_loop(0, 9, tap, 0)


def forward_body(bands, *refs):
    pos, source, table, weight, own, sib, prev_own, prev_sib, up_own, up_sib, dn_own, dn_sib = refs[:12]
    out, active = refs[12:]
    frames, rows, cols, chans = own.shape
    cells = rows * cols
    c = pos[1]
    h = pos[2]
    line = lax.broadcasted_iota(jnp.int32, (cells + 2 * cols, chans), 0)
    inside = jnp.logical_and(
        jnp.logical_or(line >= cols, h > 0),
        jnp.logical_or(line < cells + cols, h < bands - 1),
    )

    def one(f, current_own, current_sib, edges):
        parts = []
        for value, (top, bottom) in ((current_own, edges[0]), (current_sib, edges[1])):
            parts.append(
                jnp.concatenate(
                    [top, value.reshape(cells, chans), bottom], axis=0
                ).astype(F32)
            )
        halves = [jnp.where(c == 0, parts[0], parts[1]), jnp.where(c == 0, parts[1], parts[0])]
        for side in range(2):
            mean = table[side, pl.ds(f, 1)]
            scale = table[side, pl.ds(16 + f, 1)] * table[side, 32:33]
            v = (halves[side] - mean) * scale + table[side, 33:34]
            v = jnp.where(inside, v * sigmoid(v), 0.0)
            before, after = shifts(v)
            for n, w in enumerate((before, v, after)):
                at = n * 2 * chans + side * chans
                active[f, :, :, at : at + chans] = w.astype(BF16).reshape(rows + 2, cols, chans)

    for f in range(2):
        one(
            f,
            prev_own[f],
            prev_sib[f],
            (
                (up_own[frames + f], dn_own[frames + f]),
                (up_sib[frames + f], dn_sib[frames + f]),
            ),
        )

    def body(t, carry):
        one(
            t + 2,
            own[t],
            sib[t],
            ((up_own[t], dn_own[t]), (up_sib[t], dn_sib[t])),
        )
        return carry

    lax.fori_loop(0, frames, body, 0)

    def frame(t, carry):
        total = own[t].reshape(cells, chans).astype(F32)
        mixed = jnp.zeros((cells, chans), F32)
        for a in range(3):
            s = source[t * 3 + a]
            for b in range(3):
                patch = active[s, b : b + rows].reshape(cells, 6 * chans)
                mixed = mixed + bdot(patch, weight[a * 3 + b])
        out[t] = (total + mixed).astype(BF16).reshape(rows, cols, chans)
        return carry

    lax.fori_loop(0, frames, frame, 0)


def order_body(peers, bands, cap, pos, *refs):
    own, above, below = refs[:peers], refs[peers : 2 * peers], refs[2 * peers : 3 * peers]
    out, first = refs[3 * peers :]
    rows = own[0].shape[1] - 1
    h = pos[2]
    for k in range(peers):
        for j in range(cap):
            local = jnp.max(own[k][j, rows].astype(F32)).astype(jnp.int32)

            @pl.when(local >= 0)
            def _():
                out[local, 1 : rows + 1] = own[k][j, :rows]
                top = above[k][j, rows - 1].astype(F32)
                bottom = below[k][j, 0].astype(F32)
                out[local, 0] = jnp.where(h > 0, top, 0.0).astype(BF16)
                out[local, rows + 1] = jnp.where(h < bands - 1, bottom, 0.0).astype(BF16)

    first[...] = out[:2]


def backward_body(pos, target, table, member, weight, video, own, sib, next_own, next_sib, out, sums, spatial, total):
    frames, rows, cols, chans = video.shape
    cells = rows * cols
    c = pos[1]

    def fill(f, a, b):
        a = a.reshape(cells + 2 * cols, chans).astype(F32)
        b = b.reshape(cells + 2 * cols, chans).astype(F32)
        for side, v in enumerate((jnp.where(c == 0, a, b), jnp.where(c == 0, b, a))):
            before, after = shifts(v)
            for n, w in enumerate((after, v, before)):
                at = n * 2 * chans + side * chans
                spatial[f, :, :, at : at + chans] = w.astype(BF16).reshape(rows + 2, cols, chans)

    def body(t, carry):
        fill(t, own[t], sib[t])
        total[t] = jnp.zeros((cells, chans), F32)
        return carry

    lax.fori_loop(0, frames, body, 0)
    for f in range(2):
        fill(frames + f, next_own[f], next_sib[f])

    def frame(t, carry):
        for a in range(3):
            s = target[t * 3 + a]

            @pl.when(jnp.logical_and(s >= 0, s < frames))
            def _():
                grad = jnp.zeros((cells, chans), F32)
                for b in range(3):
                    patch = spatial[t, 2 - b : 2 - b + rows].reshape(cells, 6 * chans)
                    grad = grad + bdot(patch, weight[a * 3 + b])
                total[s] += grad

        return carry

    lax.fori_loop(0, frames + 2, frame, 0)
    firsts, seconds = [], []
    for t in range(frames):
        x = video[t].reshape(cells, chans).astype(F32)
        hat = (x - table[c, t + 2 : t + 3]) * table[c, t + 18 : t + 19]
        v = hat * table[c, 32:33] + table[c, 33:34]
        s = sigmoid(v)
        grad = total[t] * s * (1.0 + v * (1.0 - s))
        out[t] = grad
        firsts.append(jnp.sum(grad, axis=0, keepdims=True))
        seconds.append(jnp.sum(grad * hat, axis=0, keepdims=True))
    whole = jnp.concatenate(
        [
            fdot(member[...], jnp.concatenate(firsts, axis=0)),
            fdot(member[...], jnp.concatenate(seconds, axis=0)),
        ],
        axis=0,
    )
    for i in range(sums.shape[0]):
        sums[i] = whole


def finish_body(pos, table, group, spread, got, video, grad, up, out, small):
    frames, rows, cols, chans = video.shape
    cells = rows * cols
    c = pos[1]
    whole = jnp.sum(got[...], axis=0)
    gain = table[c, 32:33]
    small[0:1] = jnp.sum(whole[NCLIPS:], axis=0, keepdims=True)
    small[1:2] = jnp.sum(whole[:NCLIPS], axis=0, keepdims=True)
    small[2:] = jnp.zeros((6, chans), F32)
    first = fdot(spread[...], fdot(whole[:NCLIPS] * gain, group[...]))
    second = fdot(spread[...], fdot(whole[NCLIPS:] * gain, group[...]))
    for t in range(frames):
        inv = table[c, t + 18 : t + 19]
        x = video[t].reshape(cells, chans).astype(F32)
        hat = (x - table[c, t + 2 : t + 3]) * inv
        part = inv * (grad[t] * gain - first[t : t + 1] - hat * second[t : t + 1])
        u = up[t, 1 : rows + 1].reshape(cells, chans).astype(F32)
        out[t] = (u + part).astype(BF16).reshape(rows, cols, chans)


def per_device(
    clip_video, norm_gain, norm_bias, conv_weight, clip_lengths, packed_frame, packed_grad
):
    frames, rows, cols, chans = clip_video.shape
    full = conv_weight.shape[3]
    peers = lax.axis_size("tm")
    bands = lax.axis_size("height")
    tm = lax.axis_index("tm")
    h = lax.axis_index("height")
    c = lax.axis_index("chan")
    group_size = full // GROUPS
    cap = max(1, frames // peers)
    block = full // (peers * bands)
    width = peers * block
    cells = rows * cols
    everyone = ("tm", "height", "chan")
    i32 = jnp.int32
    sds = jax.ShapeDtypeStruct
    pos = jnp.stack([tm, c, h]).astype(i32)

    piece = sds((cap, rows + 1, cols, chans), BF16)
    pieces = call(
        functools.partial(pack_body, peers, cap), [piece] * peers, [SM, SM, VM],
        nbytes=2**20, name="pack",
    )(pos, packed_frame, packed_grad)
    ups = [[pieces[0]] + [lax.ppermute(pieces[k], "tm", ring(peers, k)) for k in range(1, peers)]]

    last = clip_video[frames - 2 :]
    own = [clip_video]
    prev_own = []
    for m in range(bands):
        if m > 0:
            own.append(lax.ppermute(clip_video, "height", ring(bands, m)))
        pairs = [
            (t * bands + b, (t + 1) * bands + (b + m) % bands)
            for t in range(peers - 1)
            for b in range(bands)
        ]
        prev_own.append(lax.ppermute(last, ("tm", "height"), pairs))
    sib = [sibling(v) for v in own]
    prev_sib = [sibling(v) for v in prev_own]
    for m in range(1, bands):
        ups.append([lax.ppermute(v, "height", ring(bands, m)) for v in ups[0]])

    lane = jnp.arange(chans, dtype=i32)
    group = (lane[:, None] // group_size == lane[None, :] // group_size).astype(F32)
    devices = peers * bands * 2
    stats = call(
        stat_body, sds((devices, 2 * frames + 8, chans), F32), [VM, VM, VM, VM],
        nbytes=2**20, name="stat",
    )(clip_video, norm_gain[None], norm_bias[None], group * (1.0 / group_size))
    got = lax.all_to_all(stats, everyone, 0, 0)
    got = got.reshape(peers, bands, 2, 2 * frames + 8, chans)

    clip = jnp.arange(NCLIPS, dtype=i32)
    ends = jnp.sum(jnp.where(clip[None, :] <= clip[:, None], clip_lengths[None, :], 0), axis=1)

    def start_of(frame):
        passed = ends[None, :] <= frame[:, None]
        return jnp.sum(jnp.where(passed, clip_lengths[None, :], 0), axis=1)

    def member_of(frame):
        passed = ends[None, :] <= frame[:, None]
        return jnp.sum(passed.astype(i32), axis=1)

    first_frame = tm * frames
    near = first_frame - 2 + jnp.arange(frames + 8, dtype=i32)
    near = jnp.clip(near, 0, peers * frames - 1)
    every = jnp.arange(peers * frames, dtype=i32)

    def one_hot(index):
        return (index[:, None] == clip[None, :]).astype(F32)

    every_member = one_hot(member_of(every))
    near_member = one_hot(member_of(near))
    over = every_member / clip_lengths.astype(F32)[None, :]
    same = jnp.dot(every_member, over.T, precision=HIGHEST)
    picked = jnp.dot(near_member, over.T, precision=HIGHEST)
    table = call(
        table_body, sds((2, 40, chans), F32), [VM, VM, VM], nbytes=2**18, name="table"
    )(got, same, picked)
    tap = jnp.arange(3, dtype=i32)
    ahead = first_frame + jnp.arange(frames + 2, dtype=i32)
    reach = jnp.maximum(ahead[:, None] - 2 + tap[None, :], start_of(ahead)[:, None])
    source = (reach[:frames] - (first_frame - 2)).reshape(-1)
    target = (reach - first_frame).reshape(-1)

    wanted = jnp.arange(width, dtype=i32)
    holder = lax.rem(tm + wanted // block, peers)
    wanted = (holder * bands + h) * block + lax.rem(wanted, block)
    pick_own = (c * chans + lane[:, None] == wanted[None, :]).astype(BF16)
    pick_sib = ((1 - c) * chans + lane[:, None] == wanted[None, :]).astype(BF16)
    grads = call(
        functools.partial(weight_body, peers, bands, cap, block),
        [sds((27, block, chans), F32)] + [sds((27, block, chans), BF16)] * (peers - 1),
        [SM, SM] + [VM] * (3 + 4 * bands + peers * bands),
        [
            pltpu.VMEM((frames + 2, bands * rows + 2, cols, 3 * width), BF16),
            pltpu.VMEM((frames, bands, chans, cells), BF16),
        ],
        flops=8 * 10**9, nbytes=6 * 2**20, name="weight",
    )(
        pos, source, table, pick_own, pick_sib, *own, *sib, *prev_own, *prev_sib,
        *[v for band in ups for v in band],
    )
    weight_grad = grads[0]
    for k in range(1, peers):
        weight_grad = weight_grad + lax.ppermute(grads[k], "tm", ring(peers, k)).astype(F32)
    weight_grad = weight_grad.reshape(3, 3, 3, block, chans)

    def edge(values, row):
        return jnp.concatenate([v[:, row] for v in values], axis=0)

    far = bands - 1
    weight_out = lax.dynamic_slice_in_dim(conv_weight, c * chans, chans, 4)
    weight_out = weight_out.reshape(9, 3 * full, chans)
    block_out = call(
        functools.partial(forward_body, bands),
        sds(clip_video.shape, BF16),
        [SM, SM] + [VM] * 10,
        [pltpu.VMEM((frames + 2, rows + 2, cols, 6 * chans), BF16)],
        flops=8 * 10**9, nbytes=6 * 2**20, name="forward",
    )(
        pos, source, table, weight_out, own[0], sib[0], prev_own[0], prev_sib[0],
        edge([own[1], prev_own[1]], rows - 1), edge([sib[1], prev_sib[1]], rows - 1),
        edge([own[far], prev_own[far]], 0), edge([sib[far], prev_sib[far]], 0),
    )

    up, up_first = call(
        functools.partial(order_body, peers, bands, cap),
        [sds((frames, rows + 2, cols, chans), BF16), sds((2, rows + 2, cols, chans), BF16)],
        [SM] + [VM] * (3 * peers),
        nbytes=2 * 2**20, name="order",
    )(pos, *ups[0], *ups[1], *ups[far])
    up_sib = sibling(up)
    next_own = lax.ppermute(up_first, "tm", [(t + 1, t) for t in range(peers - 1)])
    next_sib = sibling(next_own)
    weight_back = lax.dynamic_slice_in_dim(conv_weight, c * chans, chans, 3)
    weight_back = jnp.transpose(weight_back, (0, 1, 2, 4, 3)).reshape(9, 3 * full, chans)
    slab_member = near_member[2 : frames + 2]
    parts = peers * bands
    scaled, sums = call(
        backward_body,
        [sds((frames, cells, chans), F32), sds((parts, 2 * NCLIPS, chans), F32)],
        [SM, SM] + [VM] * 8,
        [
            pltpu.VMEM((frames + 2, rows + 2, cols, 6 * chans), BF16),
            pltpu.VMEM((frames, cells, chans), F32),
        ],
        flops=8 * 10**9, nbytes=6 * 2**20, name="backward",
    )(pos, target, table, slab_member.T, weight_back, clip_video, up, up_sib, next_own, next_sib)
    totals = lax.all_to_all(sums, ("tm", "height"), 0, 0)
    counts = clip_lengths.astype(F32) * (rows * bands * cols * group_size)
    video_grad, small = call(
        finish_body,
        [sds(clip_video.shape, BF16), sds((8, chans), F32)],
        [SM] + [VM] * 7,
        nbytes=3 * 2**20, name="finish",
    )(pos, table, group, slab_member / counts[None, :], totals, clip_video, scaled, up)
    return (block_out, video_grad, weight_grad, small[0], small[1])


def solution(mesh):
    placed = (
        P(("groups", "tm"), "height", None, "chan"),
        P("chan"),
        P("chan"),
        P(),
        P("groups"),
        P(("groups", "tm")),
        P(("groups", "tm"), "height", None, "chan"),
    )
    return jax.shard_map(
        per_device,
        mesh=mesh,
        in_specs=placed,
        out_specs=(
            P(("groups", "tm"), "height", None, "chan"),
            P(("groups", "tm"), "height", None, "chan"),
            P("groups", None, None, ("tm", "height"), "chan"),
            P(("groups", "chan")),
            P(("groups", "chan")),
        ),
        check_vma=False,
    )
```

```python
import functools
import jax
import jax.numpy as jnp
from jax import lax
from jax.experimental import pallas as pl
from jax.experimental.pallas import tpu as pltpu
from jax.sharding import PartitionSpec as P

GROUPS = 32
NCLIPS = 8
F32 = jnp.float32
BF16 = jnp.bfloat16
HIGHEST = lax.Precision.HIGHEST
VM = pl.BlockSpec(memory_space=pltpu.VMEM)
SM = pl.BlockSpec(memory_space=pltpu.SMEM)


ANY = pl.BlockSpec(memory_space=pl.ANY)


def call(body, out_shape, in_specs, scratch=(), flops=0, nbytes=0, name=None):
    return pl.pallas_call(
        body,
        out_shape=out_shape,
        in_specs=in_specs,
        out_specs=jax.tree.map(lambda _: VM, out_shape),
        scratch_shapes=list(scratch),
        compiler_params=pltpu.CompilerParams(vmem_limit_bytes=56 * 2**20),
        cost_estimate=pl.CostEstimate(flops=flops, bytes_accessed=nbytes, transcendentals=0),
        name=name,
    )


def fdot(a, b):
    return jnp.dot(a, b, precision=HIGHEST, preferred_element_type=F32)


def bdot(a, b):
    return jnp.dot(a, b, preferred_element_type=F32)


def ring(peers, by):
    return [(i, (i + by) % peers) for i in range(peers)]


def sibling(value):
    return lax.ppermute(value, "chan", ring(2, 1))


def sigmoid(v):
    return 1.0 / (1.0 + jnp.exp(-v))


def start_of(lengths, frame):
    begin = jnp.int32(0)
    end = jnp.int32(0)
    for k in range(NCLIPS):
        end = end + lengths[k]
        begin = jnp.where(end <= frame, end, begin)
    return begin


def clip_of(lengths, frame):
    number = jnp.zeros(frame.shape, jnp.int32)
    end = jnp.int32(0)
    for k in range(NCLIPS):
        end = end + lengths[k]
        number = number + jnp.where(end <= frame, 1, 0)
    return number


def per_clip(lengths, clip, scale):
    inverse = jnp.zeros(clip.shape, F32)
    for k in range(NCLIPS):
        length = jnp.full(clip.shape, lengths[k].astype(F32) * scale, F32)
        inverse = jnp.where(clip == k, 1.0 / length, inverse)
    return inverse


def iota(shape, dim):
    return lax.broadcasted_iota(jnp.int32, shape, dim)


def group_matrix(chans, size):
    return (iota((chans, chans), 0) // size == iota((chans, chans), 1) // size).astype(F32)


def pack_body(peers, cap, frames, grad, video, last, *outs):
    outs, sem = outs[:-1], outs[-1]
    slots = frames.shape[0]
    copy = pltpu.make_async_copy(video.at[pl.ds(slots - 2, 2)], last, sem)
    copy.start()
    tm = lax.axis_index("tm")
    number = [frames[i] for i in range(slots)]
    step = [lax.rem(lax.div(n, slots) - tm + peers, peers) for n in number]
    rank = []
    for i in range(slots):
        r = jnp.int32(0)
        for j in range(i):
            r = r + jnp.where(step[j] == step[i], 1, 0)
        rank.append(r)
    rows = grad.shape[1]
    for k in range(peers):
        for j in range(cap):
            index = jnp.int32(0)
            local = jnp.int32(-1)
            for i in range(slots):
                hit = jnp.logical_and(step[i] == k, rank[i] == j)
                index = jnp.where(hit, i, index)
                local = jnp.where(hit, lax.rem(number[i], slots), local)
            outs[k][j, :rows] = grad[index]
            outs[k][j, rows:] = jnp.full((1,) + grad.shape[2:], local.astype(F32), F32).astype(BF16)
    copy.wait()


def stat_body(size, video, gain, bias, out):
    frames, rows, cols, chans = video.shape
    cells = rows * cols
    average = group_matrix(chans, size) * (1.0 / size)
    sums = [
        jnp.sum(video[t].astype(F32).reshape(cells, chans), axis=0, keepdims=True)
        for t in range(frames)
    ]
    mean = fdot(jnp.concatenate(sums, axis=0) * (1.0 / cells), average)
    squares = []
    for t in range(frames):
        apart = video[t].astype(F32).reshape(cells, chans) - mean[t : t + 1]
        squares.append(jnp.sum(apart * apart, axis=0, keepdims=True))
    var = fdot(jnp.concatenate(squares, axis=0) * (1.0 / cells), average)
    rest = jnp.concatenate(
        [gain[...], bias[...], jnp.zeros((6, chans), F32)], axis=0
    )
    whole = jnp.concatenate([mean, var, rest], axis=0)
    for i in range(out.shape[0]):
        out[i] = whole


def turn_body(weight, out):
    for i in range(9):
        for col in range(3):
            out[i, col * 256 : (col + 1) * 256] = weight[i, col * 256 : (col + 1) * 256].T


def table_body(lengths, got, out):
    peers, bands = got.shape[:2]
    frames = (got.shape[3] - 8) // 2
    first = lax.axis_index("tm") * frames
    count = peers * frames
    clip = clip_of(lengths, iota((count, count), 1))
    inverse = per_clip(lengths, clip, 1.0)
    same = jnp.where(clip_of(lengths, iota((count, count), 0)) == clip, inverse, 0.0)
    near = jnp.clip(first - 2 + iota((16, count), 0), 0, count - 1)
    clip = clip_of(lengths, iota((16, count), 1))
    inverse = per_clip(lengths, clip, 1.0)
    picked = jnp.where(clip_of(lengths, near) == clip, inverse, 0.0)
    for c in range(2):
        mean = [
            jnp.concatenate([got[t, h, c, :frames] for t in range(peers)], axis=0)
            for h in range(bands)
        ]
        var = [
            jnp.concatenate([got[t, h, c, frames : 2 * frames] for t in range(peers)], axis=0)
            for h in range(bands)
        ]
        average = sum(mean[1:], mean[0]) * (1.0 / bands)
        clip_mean = fdot(same, average)
        spread = jnp.zeros_like(average)
        for h in range(bands):
            apart = mean[h] - clip_mean
            spread = spread + (var[h] + apart * apart)
        out[c, :16] = fdot(picked, average)
        out[c, 16:32] = lax.rsqrt(fdot(picked, spread * (1.0 / bands)) + 1e-06)
        out[c, 32:] = got[0, 0, c, 2 * frames :]


def shifts(value):
    length = value.shape[0]
    column = lax.rem(iota(value.shape, 0), 16)
    before = jnp.where(column == 0, 0.0, pltpu.roll(value, 1, 0))
    after = jnp.where(column == 15, 0.0, pltpu.roll(value, length - 1, 0))
    return before, after


def weight_body(peers, bands, cap, block, *refs):
    refs = list(refs)
    lengths, table = refs.pop(0), refs.pop(0)
    take = lambda n: [refs.pop(0) for _ in range(n)]
    own, sib, prev_own, prev_sib = take(bands), take(bands), take(bands), take(bands)
    ups = [take(peers) for _ in range(bands)]
    outs = take(peers)
    active, upright = refs
    frames, rows, cols, chans = own[0].shape
    cells = rows * cols
    width = peers * block
    tm, h, c = lax.axis_index("tm"), lax.axis_index("height"), lax.axis_index("chan")
    first = tm * frames
    band = [lax.rem(h - m + bands, bands) for m in range(bands)]
    place = iota((chans, width), 1)
    wanted = (lax.rem(tm + lax.div(place, block), peers) * bands + h) * block + lax.rem(place, block)
    channel = iota((chans, width), 0)
    pick_own = (c * chans + channel == wanted).astype(F32)
    pick_sib = ((1 - c) * chans + channel == wanted).astype(F32)
    lookup = fdot(table[c], pick_own) + fdot(table[1 - c], pick_sib)
    pick_own, pick_sib = pick_own.astype(BF16), pick_sib.astype(BF16)
    mean, inv = lookup[:16], lookup[16:32]
    scale = inv * lookup[32:33]
    bias = lookup[33:34]
    active[:, 0] = jnp.zeros((active.shape[0], cols, 3 * width), BF16)
    active[:, bands * rows + 1] = jnp.zeros((active.shape[0], cols, 3 * width), BF16)
    for f in range(frames + 2):
        for m in range(bands):
            if f < 2:
                a, b = prev_own[m][f], prev_sib[m][f]
            else:
                a, b = own[m][f - 2], sib[m][f - 2]
            x = bdot(a.reshape(cells, chans), pick_own) + bdot(b.reshape(cells, chans), pick_sib)
            v = (x - mean[f : f + 1]) * scale[f : f + 1] + bias
            v = v * sigmoid(v)
            before, after = shifts(v)
            at = pl.ds(band[m] * rows + 1, rows)
            active[f, at, :, :width] = before.astype(BF16).reshape(rows, cols, width)
            active[f, at, :, width : 2 * width] = v.astype(BF16).reshape(rows, cols, width)
            active[f, at, :, 2 * width :] = after.astype(BF16).reshape(rows, cols, width)
    for k in range(peers):
        for j in range(cap):
            local = jnp.max(ups[0][k][j, rows].astype(F32)).astype(jnp.int32)

            @pl.when(local >= 0)
            def _():
                for m in range(bands):
                    u = ups[m][k][j, :rows].reshape(cells, chans)
                    upright[local, m] = u.T

    begin = [start_of(lengths, first + t) for t in range(frames)]

    def tap(i, carry):
        a = lax.div(i, 3)
        b = lax.rem(i, 3)
        total = jnp.zeros((chans, 3 * width), F32)
        for t in range(frames):
            s = jnp.maximum(first + t - 2 + a, begin[t]) - (first - 2)
            for m in range(bands):
                patch = active[s, pl.ds(band[m] * rows + b, rows)].reshape(cells, 3 * width)
                total = total + bdot(upright[t, m], patch)
        for col in range(3):
            piece = total[:, col * width : (col + 1) * width].T
            for k in range(peers):
                outs[k][i * 3 + col] = piece[k * block : (k + 1) * block].astype(outs[k].dtype)
        return carry

    lax.fori_loop(0, 9, tap, 0)


def forward_body(bands, lengths, table, weight, own, sib, prev_own, prev_sib, *refs):
    above_own, above_sib, below_own, below_sib = refs[:4]
    far_prev = refs[4:8]
    keep, give, active = refs[8:]
    frames, rows, cols, chans = own.shape
    half = rows // 2
    tm, h, c = lax.axis_index("tm"), lax.axis_index("height"), lax.axis_index("chan")
    first = tm * frames
    outer = jnp.logical_or(
        jnp.logical_and(c == 0, h > 0), jnp.logical_and(c == 1, h < bands - 1)
    )
    begin = [start_of(lengths, first + t) for t in range(frames)]

    def put(f, at, lines, value_own, value_sib, ok):
        a, b = value_own.astype(F32), value_sib.astype(F32)
        for side, x in enumerate((jnp.where(c == 0, a, b), jnp.where(c == 0, b, a))):
            mean = table[side, f : f + 1]
            scale = table[side, 16 + f : 17 + f] * table[side, 32:33]
            v = (x - mean) * scale + table[side, 33:34]
            v = v * sigmoid(v)
            if ok is not None:
                v = jnp.where(ok, v, 0.0)
            before, after = shifts(v)
            for n, w in enumerate((before, v, after)):
                lane = n * 2 * chans + side * chans
                active[f, at, :, lane : lane + chans] = w.astype(BF16).reshape(lines, cols, chans)

    def edge(up, down, f):
        return jnp.where(c == 0, up[f, rows - 1].astype(F32), down[f, 0].astype(F32))

    for f in range(frames + 2):
        if f < 2:
            here = (prev_own, prev_sib, f)
            there = far_prev
        else:
            here = (own, sib, f - 2)
            there = (above_own, above_sib, below_own, below_sib)
        g = here[2]
        near = pl.ds((half - 1) * c, half + 1)
        put(
            f, pl.ds(1 - c, half + 1), half + 1,
            here[0][g, near].reshape((half + 1) * cols, chans),
            here[1][g, near].reshape((half + 1) * cols, chans),
            None,
        )
        put(
            f, pl.ds((half + 1) * c, 1), 1,
            edge(there[0], there[2], g), edge(there[1], there[3], g), outer,
        )
    batch = 4
    for t0 in range(0, frames, batch):
        mixed = [jnp.zeros((half * cols, 2 * chans), F32) for _ in range(batch)]
        for a in range(3):
            for b in range(3):
                w = weight[a * 3 + b]
                for q in range(batch):
                    t = t0 + q
                    s = jnp.maximum(first + t - 2 + a, begin[t]) - (first - 2)
                    patch = active[s, b : b + half].reshape(half * cols, 6 * chans)
                    mixed[q] = mixed[q] + bdot(patch, w)
        for q in range(batch):
            t = t0 + q
            mine = pl.ds(c * half, half)
            left, right = mixed[q][:, :chans], mixed[q][:, chans:]
            shape = (half, cols, chans)
            for out, value, x in (
                (keep, jnp.where(c == 0, left, right), own[t, mine]),
                (give, jnp.where(c == 0, right, left), sib[t, mine]),
            ):
                x = x.reshape(half * cols, chans).astype(F32)
                out[t] = (x + value).astype(BF16).reshape(shape)


def order_body(peers, bands, cap, *refs):
    own, above, below = refs[:peers], refs[peers : 2 * peers], refs[2 * peers : 3 * peers]
    out, first = refs[3 * peers :]
    rows = own[0].shape[1] - 1
    h = lax.axis_index("height")
    for k in range(peers):
        for j in range(cap):
            local = jnp.max(own[k][j, rows].astype(F32)).astype(jnp.int32)

            @pl.when(local >= 0)
            def _():
                out[local, 1 : rows + 1] = own[k][j, :rows]
                top = above[k][j, rows - 1].astype(F32)
                bottom = below[k][j, 0].astype(F32)
                out[local, 0] = jnp.where(h > 0, top, 0.0).astype(BF16)
                out[local, rows + 1] = jnp.where(h < bands - 1, bottom, 0.0).astype(BF16)

    first[...] = out[:2]


def backward_body(peers, lengths, table, weight, own, sib, up, up_sib, next_own, next_sib, *refs):
    keep, give, sums, spatial, total = refs
    frames, rows, cols, chans = own.shape
    half = rows // 2
    cells = half * cols
    tm, c = lax.axis_index("tm"), lax.axis_index("chan")
    first = tm * frames
    for f in range(frames + 2):
        a, b, g = (up, up_sib, f) if f < frames else (next_own, next_sib, f - frames)
        a = a[g, pl.ds(c * half, half + 2)].reshape(cells + 2 * cols, chans).astype(F32)
        b = b[g, pl.ds(c * half, half + 2)].reshape(cells + 2 * cols, chans).astype(F32)
        for side, v in enumerate((jnp.where(c == 0, a, b), jnp.where(c == 0, b, a))):
            before, after = shifts(v)
            for n, w in enumerate((after, v, before)):
                at = n * 2 * chans + side * chans
                spatial[f, :, :, at : at + chans] = w.astype(BF16).reshape(half + 2, cols, chans)
    total[...] = jnp.zeros_like(total)

    def frame(t, carry):
        begin = start_of(lengths, first + t)
        for a in range(3):
            s = jnp.maximum(first + t - 2 + a, begin) - first

            @pl.when(jnp.logical_and(s >= 0, s < frames))
            def _():
                grad = jnp.zeros((cells, 2 * chans), F32)
                for b in range(3):
                    patch = spatial[t, 2 - b : 2 - b + half].reshape(cells, 6 * chans)
                    grad = grad + bdot(patch, weight[a * 3 + b])
                total[s] += grad

        return carry

    lax.fori_loop(0, frames + 2, frame, 0)
    mine = pl.ds(c * half, half)
    member = (
        clip_of(lengths, first + iota((NCLIPS, frames), 1)) == iota((NCLIPS, frames), 0)
    ).astype(F32)
    for side in range(2):
        firsts, seconds = [], []
        for t in range(frames):
            a, b = own[t, mine].astype(F32), sib[t, mine].astype(F32)
            x = jnp.where((c == 0) == (side == 0), a, b).reshape(cells, chans)
            hat = (x - table[side, t + 2 : t + 3]) * table[side, t + 18 : t + 19]
            v = hat * table[side, 32:33] + table[side, 33:34]
            s = sigmoid(v)
            grad = total[t, :, side * chans : (side + 1) * chans] * s * (1.0 + v * (1.0 - s))
            total[t, :, side * chans : (side + 1) * chans] = grad
            firsts.append(jnp.sum(grad, axis=0, keepdims=True))
            seconds.append(jnp.sum(grad * hat, axis=0, keepdims=True))
        whole = jnp.concatenate(
            [
                fdot(member, jnp.concatenate(firsts, axis=0)),
                fdot(member, jnp.concatenate(seconds, axis=0)),
            ],
            axis=0,
        )
        for i in range(sums.shape[0] // 2):
            sums[2 * i + side] = whole
    for t in range(frames):
        left, right = total[t, :, :chans], total[t, :, chans:]
        keep[t] = jnp.where(c == 0, left, right)
        give[t] = jnp.where(c == 0, right, left)


def finish_body(size, bands, lengths, table, got, video, keep, other, up, out, small):
    frames, rows, cols, chans = video.shape
    half = rows // 2
    cells = half * cols
    tm, c = lax.axis_index("tm"), lax.axis_index("chan")
    first_frame = tm * frames
    whole = jnp.sum(got[...], axis=0)
    gain = table[c, 32:33]
    small[0:1] = jnp.sum(whole[NCLIPS:], axis=0, keepdims=True)
    small[1:2] = jnp.sum(whole[:NCLIPS], axis=0, keepdims=True)
    small[2:] = jnp.zeros((6, chans), F32)
    group = group_matrix(chans, size)
    clip = iota((frames, NCLIPS), 1)
    inverse = per_clip(lengths, clip, float(rows * bands * cols * size))
    spread = jnp.where(clip_of(lengths, first_frame + iota((frames, NCLIPS), 0)) == clip, inverse, 0.0)
    first = fdot(spread, fdot(whole[:NCLIPS] * gain, group))
    second = fdot(spread, fdot(whole[NCLIPS:] * gain, group))
    for t in range(frames):
        inv = table[c, t + 18 : t + 19]
        for grads, at in ((keep, c * half), (other, (1 - c) * half)):
            x = video[t, pl.ds(at, half)].reshape(cells, chans).astype(F32)
            hat = (x - table[c, t + 2 : t + 3]) * inv
            part = inv * (grads[t] * gain - first[t : t + 1] - hat * second[t : t + 1])
            u = up[t, pl.ds(at + 1, half)].reshape(cells, chans).astype(F32)
            out[t, pl.ds(at, half)] = (u + part).astype(BF16).reshape(half, cols, chans)


def per_device(
    clip_video, norm_gain, norm_bias, conv_weight, clip_lengths, packed_frame, packed_grad
):
    frames, rows, cols, chans = clip_video.shape
    full = conv_weight.shape[3]
    peers = lax.axis_size("tm")
    bands = lax.axis_size("height")
    c = lax.axis_index("chan")
    size = full // GROUPS
    cap = max(1, frames // peers)
    block = full // (peers * bands)
    width = peers * block
    half = rows // 2
    everyone = ("tm", "height", "chan")
    devices = peers * bands * 2
    sds = jax.ShapeDtypeStruct

    piece = sds((cap, rows + 1, cols, chans), BF16)
    last, *pieces = call(
        functools.partial(pack_body, peers, cap),
        [sds((2, rows, cols, chans), BF16)] + [piece] * peers,
        [SM, VM, ANY],
        [pltpu.SemaphoreType.DMA],
        nbytes=2**20, name="pack",
    )(packed_frame, packed_grad, clip_video)
    ups = [[pieces[0]] + [lax.ppermute(pieces[k], "tm", ring(peers, k)) for k in range(1, peers)]]

    own = [clip_video]
    prev_own = []
    for m in range(bands):
        if m > 0:
            own.append(lax.ppermute(clip_video, "height", ring(bands, m)))
        pairs = [
            (t * bands + b, (t + 1) * bands + (b + m) % bands)
            for t in range(peers - 1)
            for b in range(bands)
        ]
        prev_own.append(lax.ppermute(last, ("tm", "height"), pairs))
    sib = [sibling(v) for v in own]
    prev_sib = [sibling(v) for v in prev_own]
    for m in range(1, bands):
        ups.append([lax.ppermute(v, "height", ring(bands, m)) for v in ups[0]])

    stats = call(
        functools.partial(stat_body, size),
        sds((devices, 2 * frames + 8, chans), F32), [VM, VM, VM],
        nbytes=2**20, name="stat",
    )(clip_video, norm_gain[None], norm_bias[None])
    got = lax.all_to_all(stats, everyone, 0, 0)
    got = got.reshape(peers, bands, 2, 2 * frames + 8, chans)
    table = call(
        table_body, sds((2, 40, chans), F32), [SM, VM], nbytes=2**18, name="table"
    )(clip_lengths, got)
    weight = conv_weight.reshape(9, 3 * full, full)
    turned = call(
        turn_body, sds(weight.shape, BF16), [VM], nbytes=8 * 2**20, name="turn"
    )(weight)

    grads = call(
        functools.partial(weight_body, peers, bands, cap, block),
        [sds((27, block, chans), F32)] + [sds((27, block, chans), BF16)] * (peers - 1),
        [SM] + [VM] * (1 + 4 * bands + peers * bands),
        [
            pltpu.VMEM((frames + 2, bands * rows + 2, cols, 3 * width), BF16),
            pltpu.VMEM((frames, bands, chans, rows * cols), BF16),
        ],
        flops=8 * 10**9, nbytes=6 * 2**20, name="weight",
    )(
        clip_lengths, table, *own, *sib, *prev_own, *prev_sib,
        *[v for band in ups for v in band],
    )
    weight_grad = grads[0]
    for k in range(1, peers):
        weight_grad = weight_grad + lax.ppermute(grads[k], "tm", ring(peers, k)).astype(F32)
    weight_grad = weight_grad.reshape(3, 3, 3, block, chans)

    far = bands - 1
    up, up_first = call(
        functools.partial(order_body, peers, bands, cap),
        [sds((frames, rows + 2, cols, chans), BF16), sds((2, rows + 2, cols, chans), BF16)],
        [VM] * (3 * peers),
        nbytes=2 * 2**20, name="order",
    )(*ups[0], *ups[1], *ups[far])
    up_sib = sibling(up)
    next_own = lax.ppermute(up_first, "tm", [(t + 1, t) for t in range(peers - 1)])
    next_sib = sibling(next_own)
    part = sds((frames, half * cols, chans), F32)
    keep, give, sums = call(
        functools.partial(backward_body, peers),
        [part, part, sds((devices, 2 * NCLIPS, chans), F32)],
        [SM] + [VM] * 8,
        [
            pltpu.VMEM((frames + 2, half + 2, cols, 6 * chans), BF16),
            pltpu.VMEM((frames, half * cols, 2 * chans), F32),
        ],
        flops=8 * 10**9, nbytes=6 * 2**20, name="backward",
    )(clip_lengths, table, turned, clip_video, sib[0], up, up_sib, next_own, next_sib)
    totals = lax.all_to_all(sums, everyone, 0, 0)
    other = sibling(give)

    part = sds((frames, half, cols, chans), BF16)
    block_keep, block_give = call(
        functools.partial(forward_body, bands),
        [part, part],
        [SM] + [VM] * 14,
        [pltpu.VMEM((frames + 2, half + 2, cols, 6 * chans), BF16)],
        flops=8 * 10**9, nbytes=6 * 2**20, name="forward",
    )(
        clip_lengths, table, weight, clip_video, sib[0], prev_own[0], prev_sib[0],
        own[1], sib[1], own[far], sib[far],
        prev_own[1], prev_sib[1], prev_own[far], prev_sib[far],
    )
    block_other = sibling(block_give)
    block_out = jnp.where(
        c == 0,
        jnp.concatenate([block_keep, block_other], axis=1),
        jnp.concatenate([block_other, block_keep], axis=1),
    )

    video_grad, small = call(
        functools.partial(finish_body, size, bands),
        [sds(clip_video.shape, BF16), sds((8, chans), F32)],
        [SM] + [VM] * 6,
        nbytes=3 * 2**20, name="finish",
    )(clip_lengths, table, totals, clip_video, keep, other, up)
    return (block_out, video_grad, weight_grad, small[0], small[1])


def solution(mesh):
    placed = (
        P(("groups", "tm"), "height", None, "chan"),
        P("chan"),
        P("chan"),
        P(),
        P("groups"),
        P(("groups", "tm")),
        P(("groups", "tm"), "height", None, "chan"),
    )
    return jax.shard_map(
        per_device,
        mesh=mesh,
        in_specs=placed,
        out_specs=(
            P(("groups", "tm"), "height", None, "chan"),
            P(("groups", "tm"), "height", None, "chan"),
            P("groups", None, None, ("tm", "height"), "chan"),
            P(("groups", "chan")),
            P(("groups", "chan")),
        ),
        check_vma=False,
    )
```

```python
import functools
import jax
import jax.numpy as jnp
from jax import lax
from jax.experimental import pallas as pl
from jax.experimental.pallas import tpu as pltpu
from jax.sharding import PartitionSpec as P

GROUPS = 32
NCLIPS = 8
F32 = jnp.float32
BF16 = jnp.bfloat16
HIGHEST = lax.Precision.HIGHEST
VM = pl.BlockSpec(memory_space=pltpu.VMEM)
SM = pl.BlockSpec(memory_space=pltpu.SMEM)


ANY = pl.BlockSpec(memory_space=pl.ANY)


def after(value, *others):
    return lax.optimization_barrier((value, *others))[0]


def call(body, out_shape, in_specs, scratch=(), flops=0, nbytes=0, name=None, room=24):
    return pl.pallas_call(
        body,
        out_shape=out_shape,
        in_specs=in_specs,
        out_specs=jax.tree.map(lambda _: VM, out_shape),
        scratch_shapes=list(scratch),
        compiler_params=pltpu.CompilerParams(vmem_limit_bytes=room * 2**20),
        cost_estimate=pl.CostEstimate(flops=flops, bytes_accessed=nbytes, transcendentals=0),
        name=name,
    )


def fdot(a, b):
    return jnp.dot(a, b, precision=HIGHEST, preferred_element_type=F32)


def bdot(a, b):
    return jnp.dot(a, b, preferred_element_type=F32)


def ring(peers, by):
    return [(i, (i + by) % peers) for i in range(peers)]


def sibling(value):
    return lax.ppermute(value, "chan", ring(2, 1))


def sigmoid(v):
    return 1.0 / (1.0 + jnp.exp(-v))


def start_of(lengths, frame):
    begin = jnp.int32(0)
    end = jnp.int32(0)
    for k in range(NCLIPS):
        end = end + lengths[k]
        begin = jnp.where(end <= frame, end, begin)
    return begin


def clip_of(lengths, frame):
    number = jnp.zeros(frame.shape, jnp.int32)
    end = jnp.int32(0)
    for k in range(NCLIPS):
        end = end + lengths[k]
        number = number + jnp.where(end <= frame, 1, 0)
    return number


def per_clip(lengths, clip, scale):
    inverse = jnp.zeros(clip.shape, F32)
    for k in range(NCLIPS):
        length = jnp.full(clip.shape, lengths[k].astype(F32) * scale, F32)
        inverse = jnp.where(clip == k, 1.0 / length, inverse)
    return inverse


def iota(shape, dim):
    return lax.broadcasted_iota(jnp.int32, shape, dim)


def group_matrix(chans, size):
    return (iota((chans, chans), 0) // size == iota((chans, chans), 1) // size).astype(F32)


def pack_body(peers, cap, frames, grad, video, *outs):
    outs, sem = outs[:-1], outs[-1]
    slots = frames.shape[0]
    rows = grad.shape[1]
    copies = [
        pltpu.make_async_copy(
            video.at[slots - 2 + i],
            outs[1].at[pl.ds(cap * (rows + 1) + i * rows, rows)],
            sem.at[i],
        )
        for i in range(2)
    ]
    for copy in copies:
        copy.start()
    tm = lax.axis_index("tm")
    number = [frames[i] for i in range(slots)]
    step = [lax.rem(lax.div(n, slots) - tm + peers, peers) for n in number]
    rank = []
    for i in range(slots):
        r = jnp.int32(0)
        for j in range(i):
            r = r + jnp.where(step[j] == step[i], 1, 0)
        rank.append(r)
    for k in range(peers):
        for j in range(cap):
            at = j * (rows + 1)
            index = jnp.int32(0)
            local = jnp.int32(-1)
            for i in range(slots):
                hit = jnp.logical_and(step[i] == k, rank[i] == j)
                index = jnp.where(hit, i, index)
                local = jnp.where(hit, lax.rem(number[i], slots), local)
            outs[k][at : at + rows] = grad[index]
            outs[k][at + rows] = jnp.full(grad.shape[2:], local.astype(F32), F32).astype(BF16)
    for copy in copies:
        copy.wait()


def stat_body(size, video, gain, bias, out):
    frames, rows, cols, chans = video.shape
    cells = rows * cols
    average = group_matrix(chans, size) * (1.0 / size)
    sums = [
        jnp.sum(video[t].astype(F32).reshape(cells, chans), axis=0, keepdims=True)
        for t in range(frames)
    ]
    mean = fdot(jnp.concatenate(sums, axis=0) * (1.0 / cells), average)
    squares = []
    for t in range(frames):
        apart = video[t].astype(F32).reshape(cells, chans) - mean[t : t + 1]
        squares.append(jnp.sum(apart * apart, axis=0, keepdims=True))
    var = fdot(jnp.concatenate(squares, axis=0) * (1.0 / cells), average)
    rest = jnp.concatenate(
        [gain[...], bias[...], jnp.zeros((6, chans), F32)], axis=0
    )
    whole = jnp.concatenate([mean, var, rest], axis=0)
    for i in range(out.shape[0]):
        out[i] = whole


def turn_body(weight, out):
    for i in range(9):
        for col in range(3):
            out[i, col * 256 : (col + 1) * 256] = weight[i, col * 256 : (col + 1) * 256].T


def table_body(lengths, got, out):
    peers, bands = got.shape[:2]
    frames = (got.shape[3] - 8) // 2
    first = lax.axis_index("tm") * frames
    count = peers * frames
    clip = clip_of(lengths, iota((count, count), 1))
    inverse = per_clip(lengths, clip, 1.0)
    same = jnp.where(clip_of(lengths, iota((count, count), 0)) == clip, inverse, 0.0)
    near = jnp.clip(first - 2 + iota((16, count), 0), 0, count - 1)
    clip = clip_of(lengths, iota((16, count), 1))
    inverse = per_clip(lengths, clip, 1.0)
    picked = jnp.where(clip_of(lengths, near) == clip, inverse, 0.0)
    for c in range(2):
        mean = [
            jnp.concatenate([got[t, h, c, :frames] for t in range(peers)], axis=0)
            for h in range(bands)
        ]
        var = [
            jnp.concatenate([got[t, h, c, frames : 2 * frames] for t in range(peers)], axis=0)
            for h in range(bands)
        ]
        average = sum(mean[1:], mean[0]) * (1.0 / bands)
        clip_mean = fdot(same, average)
        spread = jnp.zeros_like(average)
        for h in range(bands):
            apart = mean[h] - clip_mean
            spread = spread + (var[h] + apart * apart)
        out[c, :16] = fdot(picked, average)
        out[c, 16:32] = lax.rsqrt(fdot(picked, spread * (1.0 / bands)) + 1e-06)
        out[c, 32:] = got[0, 0, c, 2 * frames :]


def shifts(value):
    length = value.shape[0]
    column = lax.rem(iota(value.shape, 0), 16)
    before = jnp.where(column == 0, 0.0, pltpu.roll(value, 1, 0))
    after = jnp.where(column == 15, 0.0, pltpu.roll(value, length - 1, 0))
    return before, after


def weight_body(peers, bands, cap, block, *refs):
    refs = list(refs)
    lengths, table = refs.pop(0), refs.pop(0)
    take = lambda n: [refs.pop(0) for _ in range(n)]
    own, sib, prev_sib = take(bands), take(bands), take(bands)
    ups = [take(peers) for _ in range(bands)]
    outs = take(peers)
    active, upright = refs
    frames, rows, cols, chans = own[0].shape
    cells = rows * cols
    width = peers * block
    tm, h, c = lax.axis_index("tm"), lax.axis_index("height"), lax.axis_index("chan")
    first = tm * frames
    band = [lax.rem(h - m + bands, bands) for m in range(bands)]
    place = iota((chans, width), 1)
    wanted = (lax.rem(tm + lax.div(place, block), peers) * bands + h) * block + lax.rem(place, block)
    channel = iota((chans, width), 0)
    pick_own = (c * chans + channel == wanted).astype(F32)
    pick_sib = ((1 - c) * chans + channel == wanted).astype(F32)
    lookup = fdot(table[c], pick_own) + fdot(table[1 - c], pick_sib)
    pick_own, pick_sib = pick_own.astype(BF16), pick_sib.astype(BF16)
    mean, inv = lookup[:16], lookup[16:32]
    scale = inv * lookup[32:33]
    bias = lookup[33:34]
    active[:, 0] = jnp.zeros((active.shape[0], cols, 3 * width), BF16)
    active[:, bands * rows + 1] = jnp.zeros((active.shape[0], cols, 3 * width), BF16)
    for f in range(frames + 2):
        for m in range(bands):
            if f < 2:
                at = cap * (rows + 1) + f * rows
                a, b = ups[m][1][at : at + rows], prev_sib[m][at : at + rows]
            else:
                a, b = own[m][f - 2], sib[m][f - 2]
            x = bdot(a.reshape(cells, chans), pick_own) + bdot(b.reshape(cells, chans), pick_sib)
            v = (x - mean[f : f + 1]) * scale[f : f + 1] + bias
            v = v * sigmoid(v)
            before, after = shifts(v)
            at = pl.ds(band[m] * rows + 1, rows)
            active[f, at, :, :width] = before.astype(BF16).reshape(rows, cols, width)
            active[f, at, :, width : 2 * width] = v.astype(BF16).reshape(rows, cols, width)
            active[f, at, :, 2 * width :] = after.astype(BF16).reshape(rows, cols, width)
    for k in range(peers):
        for j in range(cap):
            at = j * (rows + 1)
            local = jnp.max(ups[0][k][at + rows].astype(F32)).astype(jnp.int32)

            @pl.when(local >= 0)
            def _():
                for m in range(bands):
                    u = ups[m][k][at : at + rows].reshape(cells, chans)
                    upright[local, m] = u.T

    begin = [start_of(lengths, first + t) for t in range(frames)]

    def tap(i, carry):
        a = lax.div(i, 3)
        b = lax.rem(i, 3)
        total = jnp.zeros((chans, 3 * width), F32)
        for t in range(frames):
            s = jnp.maximum(first + t - 2 + a, begin[t]) - (first - 2)
            for m in range(bands):
                patch = active[s, pl.ds(band[m] * rows + b, rows)].reshape(cells, 3 * width)
                total = total + bdot(upright[t, m], patch)
        for col in range(3):
            piece = total[:, col * width : (col + 1) * width].T
            for k in range(peers):
                outs[k][i * 3 + col] = piece[k * block : (k + 1) * block].astype(outs[k].dtype)
        return carry

    lax.fori_loop(0, 9, tap, 0)


def forward_body(bands, skip, lengths, table, weight, *refs):
    own, sib, above_own, above_sib, below_own, below_sib = refs[:6]
    prev_own, prev_sib = refs[6:8]
    far_prev = refs[8:12]
    keep, give, active = refs[12:]
    frames, rows, cols, chans = own.shape
    half = rows // 2
    tm, h, c = lax.axis_index("tm"), lax.axis_index("height"), lax.axis_index("chan")
    first = tm * frames
    outer = jnp.logical_or(
        jnp.logical_and(c == 0, h > 0), jnp.logical_and(c == 1, h < bands - 1)
    )
    begin = [start_of(lengths, first + t) for t in range(frames)]

    def put(f, at, lines, value_own, value_sib, ok):
        a, b = value_own.astype(F32), value_sib.astype(F32)
        for side, x in enumerate((jnp.where(c == 0, a, b), jnp.where(c == 0, b, a))):
            mean = table[side, f : f + 1]
            scale = table[side, 16 + f : 17 + f] * table[side, 32:33]
            v = (x - mean) * scale + table[side, 33:34]
            v = v * sigmoid(v)
            if ok is not None:
                v = jnp.where(ok, v, 0.0)
            before, after = shifts(v)
            for n, w in enumerate((before, v, after)):
                lane = n * 2 * chans + side * chans
                active[f, at, :, lane : lane + chans] = w.astype(BF16).reshape(lines, cols, chans)

    def edge(up, down):
        return jnp.where(c == 0, up.astype(F32), down.astype(F32))

    for f in range(frames + 2):
        if f < 2:
            base = skip + f * rows
            near = pl.ds(base + (half - 1) * c, half + 1)
            here = [v[near] for v in (prev_own, prev_sib)]
            up = [v[base + rows - 1] for v in far_prev[:2]]
            down = [v[base] for v in far_prev[2:]]
        else:
            near = pl.ds((half - 1) * c, half + 1)
            here = [v[f - 2, near] for v in (own, sib)]
            up = [v[f - 2, rows - 1] for v in (above_own, above_sib)]
            down = [v[f - 2, 0] for v in (below_own, below_sib)]
        here = [v.reshape((half + 1) * cols, chans) for v in here]
        put(f, pl.ds(1 - c, half + 1), half + 1, here[0], here[1], None)
        put(
            f, pl.ds((half + 1) * c, 1), 1,
            edge(up[0], down[0]), edge(up[1], down[1]), outer,
        )
    batch = 4
    for t0 in range(0, frames, batch):
        mixed = [jnp.zeros((half * cols, 2 * chans), F32) for _ in range(batch)]
        for a in range(3):
            for b in range(3):
                w = weight[a * 3 + b]
                for q in range(batch):
                    t = t0 + q
                    s = jnp.maximum(first + t - 2 + a, begin[t]) - (first - 2)
                    patch = active[s, b : b + half].reshape(half * cols, 6 * chans)
                    mixed[q] = mixed[q] + bdot(patch, w)
        for q in range(batch):
            t = t0 + q
            mine = pl.ds(c * half, half)
            left, right = mixed[q][:, :chans], mixed[q][:, chans:]
            shape = (half, cols, chans)
            for out, value, x in (
                (keep, jnp.where(c == 0, left, right), own[t, mine]),
                (give, jnp.where(c == 0, right, left), sib[t, mine]),
            ):
                x = x.reshape(half * cols, chans).astype(F32)
                out[t] = (x + value).astype(BF16).reshape(shape)


def order_body(peers, bands, cap, *refs):
    own, above, below = refs[:peers], refs[peers : 2 * peers], refs[2 * peers : 3 * peers]
    out, first = refs[3 * peers :]
    rows = out.shape[1] - 2
    h = lax.axis_index("height")
    for k in range(peers):
        for j in range(cap):
            at = j * (rows + 1)
            local = jnp.max(own[k][at + rows].astype(F32)).astype(jnp.int32)

            @pl.when(local >= 0)
            def _():
                out[local, 1 : rows + 1] = own[k][at : at + rows]
                top = above[k][at + rows - 1].astype(F32)
                bottom = below[k][at].astype(F32)
                out[local, 0] = jnp.where(h > 0, top, 0.0).astype(BF16)
                out[local, rows + 1] = jnp.where(h < bands - 1, bottom, 0.0).astype(BF16)

    first[...] = out[:2]


def backward_body(peers, lengths, table, weight, own, sib, up, up_sib, next_own, next_sib, *refs):
    keep, give, sums, spatial, total = refs
    frames, rows, cols, chans = own.shape
    half = rows // 2
    cells = half * cols
    tm, c = lax.axis_index("tm"), lax.axis_index("chan")
    first = tm * frames
    for f in range(frames + 2):
        a, b, g = (up, up_sib, f) if f < frames else (next_own, next_sib, f - frames)
        a = a[g, pl.ds(c * half, half + 2)].reshape(cells + 2 * cols, chans).astype(F32)
        b = b[g, pl.ds(c * half, half + 2)].reshape(cells + 2 * cols, chans).astype(F32)
        for side, v in enumerate((jnp.where(c == 0, a, b), jnp.where(c == 0, b, a))):
            before, after = shifts(v)
            for n, w in enumerate((after, v, before)):
                at = n * 2 * chans + side * chans
                spatial[f, :, :, at : at + chans] = w.astype(BF16).reshape(half + 2, cols, chans)
    total[...] = jnp.zeros_like(total)

    def frame(t, carry):
        begin = start_of(lengths, first + t)
        for a in range(3):
            s = jnp.maximum(first + t - 2 + a, begin) - first

            @pl.when(jnp.logical_and(s >= 0, s < frames))
            def _():
                grad = jnp.zeros((cells, 2 * chans), F32)
                for b in range(3):
                    patch = spatial[t, 2 - b : 2 - b + half].reshape(cells, 6 * chans)
                    grad = grad + bdot(patch, weight[a * 3 + b])
                total[s] += grad

        return carry

    lax.fori_loop(0, frames + 2, frame, 0)
    mine = pl.ds(c * half, half)
    member = (
        clip_of(lengths, first + iota((NCLIPS, frames), 1)) == iota((NCLIPS, frames), 0)
    ).astype(F32)
    for side in range(2):
        firsts, seconds = [], []
        for t in range(frames):
            a, b = own[t, mine].astype(F32), sib[t, mine].astype(F32)
            x = jnp.where((c == 0) == (side == 0), a, b).reshape(cells, chans)
            hat = (x - table[side, t + 2 : t + 3]) * table[side, t + 18 : t + 19]
            v = hat * table[side, 32:33] + table[side, 33:34]
            s = sigmoid(v)
            grad = total[t, :, side * chans : (side + 1) * chans] * s * (1.0 + v * (1.0 - s))
            total[t, :, side * chans : (side + 1) * chans] = grad
            firsts.append(jnp.sum(grad, axis=0, keepdims=True))
            seconds.append(jnp.sum(grad * hat, axis=0, keepdims=True))
        whole = jnp.concatenate(
            [
                fdot(member, jnp.concatenate(firsts, axis=0)),
                fdot(member, jnp.concatenate(seconds, axis=0)),
            ],
            axis=0,
        )
        for i in range(sums.shape[0] // 2):
            sums[2 * i + side] = whole
    for t in range(frames):
        left, right = total[t, :, :chans], total[t, :, chans:]
        keep[t] = jnp.where(c == 0, left, right)
        give[t] = jnp.where(c == 0, right, left)


def finish_body(size, bands, lengths, table, got, video, keep, other, up, out, small):
    frames, rows, cols, chans = video.shape
    half = rows // 2
    cells = half * cols
    tm, c = lax.axis_index("tm"), lax.axis_index("chan")
    first_frame = tm * frames
    whole = jnp.sum(got[...], axis=0)
    gain = table[c, 32:33]
    small[0:1] = jnp.sum(whole[NCLIPS:], axis=0, keepdims=True)
    small[1:2] = jnp.sum(whole[:NCLIPS], axis=0, keepdims=True)
    small[2:] = jnp.zeros((6, chans), F32)
    group = group_matrix(chans, size)
    clip = iota((frames, NCLIPS), 1)
    inverse = per_clip(lengths, clip, float(rows * bands * cols * size))
    spread = jnp.where(clip_of(lengths, first_frame + iota((frames, NCLIPS), 0)) == clip, inverse, 0.0)
    first = fdot(spread, fdot(whole[:NCLIPS] * gain, group))
    second = fdot(spread, fdot(whole[NCLIPS:] * gain, group))
    for t in range(frames):
        inv = table[c, t + 18 : t + 19]
        for grads, at in ((keep, c * half), (other, (1 - c) * half)):
            x = video[t, pl.ds(at, half)].reshape(cells, chans).astype(F32)
            hat = (x - table[c, t + 2 : t + 3]) * inv
            part = inv * (grads[t] * gain - first[t : t + 1] - hat * second[t : t + 1])
            u = up[t, pl.ds(at + 1, half)].reshape(cells, chans).astype(F32)
            out[t, pl.ds(at, half)] = (u + part).astype(BF16).reshape(half, cols, chans)


def per_device(
    clip_video, norm_gain, norm_bias, conv_weight, clip_lengths, packed_frame, packed_grad
):
    frames, rows, cols, chans = clip_video.shape
    full = conv_weight.shape[3]
    peers = lax.axis_size("tm")
    bands = lax.axis_size("height")
    c = lax.axis_index("chan")
    size = full // GROUPS
    cap = max(1, frames // peers)
    block = full // (peers * bands)
    width = peers * block
    half = rows // 2
    everyone = ("tm", "height", "chan")
    devices = peers * bands * 2
    sds = jax.ShapeDtypeStruct

    skip = cap * (rows + 1)
    pieces = call(
        functools.partial(pack_body, peers, cap),
        [
            sds((skip + (2 * rows if k == 1 else 0), cols, chans), BF16)
            for k in range(peers)
        ],
        [SM, VM, ANY],
        [pltpu.SemaphoreType.DMA((2,))],
        nbytes=2**20, name="pack",
    )(packed_frame, packed_grad, clip_video)
    ups = [[pieces[0]] + [lax.ppermute(pieces[k], "tm", ring(peers, k)) for k in range(1, peers)]]

    stats = call(
        functools.partial(stat_body, size),
        sds((devices, 2 * frames + 8, chans), F32), [VM, VM, VM],
        nbytes=2**20, name="stat",
    )(after(clip_video, pieces[0]), norm_gain[None], norm_bias[None])

    own = [clip_video]
    for m in range(1, bands):
        own.append(lax.ppermute(clip_video, "height", ring(bands, m)))
    sib = [sibling(v) for v in own]
    for m in range(1, bands):
        ready = [after(v, stats) if k == 0 else after(v, stats, own[m]) for k, v in enumerate(ups[0])]
        ups.append([lax.ppermute(v, "height", ring(bands, m)) for v in ready])
    prev_sib = [sibling(v[1]) for v in ups]

    got = lax.all_to_all(stats, everyone, 0, 0)
    got = got.reshape(peers, bands, 2, 2 * frames + 8, chans)
    weight = conv_weight.reshape(9, 3 * full, full)
    turned = call(
        turn_body, sds(weight.shape, BF16), [VM], nbytes=8 * 2**20, name="turn"
    )(weight)
    table = call(
        table_body, sds((2, 40, chans), F32), [SM, VM], nbytes=2**18, name="table"
    )(clip_lengths, after(got, turned))

    grads = call(
        functools.partial(weight_body, peers, bands, cap, block),
        [sds((27, block, chans), F32)] + [sds((27, block, chans), BF16)] * (peers - 1),
        [SM] + [VM] * (1 + 3 * bands + peers * bands),
        [
            pltpu.VMEM((frames + 2, bands * rows + 2, cols, 3 * width), BF16),
            pltpu.VMEM((frames, bands, chans, rows * cols), BF16),
        ],
        flops=8 * 10**9, nbytes=6 * 2**20, name="weight",
    )(
        clip_lengths, table, *own, *sib, *prev_sib,
        *[v for band in ups for v in band],
    )
    far = bands - 1
    up, up_first = call(
        functools.partial(order_body, peers, bands, cap),
        [sds((frames, rows + 2, cols, chans), BF16), sds((2, rows + 2, cols, chans), BF16)],
        [VM] * (3 * peers),
        nbytes=2 * 2**20, name="order",
    )(*ups[0], *ups[1], *ups[far])
    up_sib = sibling(up)
    next_own = lax.ppermute(up_first, "tm", [(t + 1, t) for t in range(peers - 1)])
    next_sib = sibling(next_own)
    part = sds((frames, half * cols, chans), F32)
    keep, give, sums = call(
        functools.partial(backward_body, peers),
        [part, part, sds((devices, 2 * NCLIPS, chans), F32)],
        [SM] + [VM] * 8,
        [
            pltpu.VMEM((frames + 2, half + 2, cols, 6 * chans), BF16),
            pltpu.VMEM((frames, half * cols, 2 * chans), F32),
        ],
        flops=8 * 10**9, nbytes=6 * 2**20, name="backward",
    )(clip_lengths, table, after(turned, grads[0]), clip_video, sib[0], up, up_sib, next_own, next_sib)
    totals = lax.all_to_all(sums, everyone, 0, 0)
    other = sibling(give)

    part = sds((frames, half, cols, chans), BF16)
    block_keep, block_give = call(
        functools.partial(forward_body, bands, skip),
        [part, part],
        [SM] + [VM] * 14,
        [pltpu.VMEM((frames + 2, half + 2, cols, 6 * chans), BF16)],
        flops=8 * 10**9, nbytes=6 * 2**20, name="forward",
    )(
        clip_lengths, table, after(weight, sums), own[0], sib[0], own[1], sib[1], own[far], sib[far],
        ups[0][1], prev_sib[0], ups[1][1], prev_sib[1], ups[far][1], prev_sib[far],
    )
    block_other = sibling(block_give)
    block_out = jnp.where(
        c == 0,
        jnp.concatenate([block_keep, block_other], axis=1),
        jnp.concatenate([block_other, block_keep], axis=1),
    )

    video_grad, small = call(
        functools.partial(finish_body, size, bands),
        [sds(clip_video.shape, BF16), sds((8, chans), F32)],
        [SM] + [VM] * 6,
        nbytes=3 * 2**20, name="finish",
    )(clip_lengths, table, totals, clip_video, keep, other, up)
    weight_grad = after(grads[0], small)
    for k in range(1, peers):
        weight_grad = weight_grad + lax.ppermute(grads[k], "tm", ring(peers, k)).astype(F32)
    weight_grad = weight_grad.reshape(3, 3, 3, block, chans)
    return (block_out, video_grad, weight_grad, small[0], small[1])


def solution(mesh):
    placed = (
        P(("groups", "tm"), "height", None, "chan"),
        P("chan"),
        P("chan"),
        P(),
        P("groups"),
        P(("groups", "tm")),
        P(("groups", "tm"), "height", None, "chan"),
    )
    return jax.shard_map(
        per_device,
        mesh=mesh,
        in_specs=placed,
        out_specs=(
            P(("groups", "tm"), "height", None, "chan"),
            P(("groups", "tm"), "height", None, "chan"),
            P("groups", None, None, ("tm", "height"), "chan"),
            P(("groups", "chan")),
            P(("groups", "chan")),
        ),
        check_vma=False,
    )
```

```python
import functools
import jax
import jax.numpy as jnp
from jax import lax
from jax.experimental import pallas as pl
from jax.experimental.pallas import tpu as pltpu
from jax.sharding import PartitionSpec as P

GROUPS = 32
NCLIPS = 8
F32 = jnp.float32
BF16 = jnp.bfloat16
HIGHEST = lax.Precision.HIGHEST
VM = pl.BlockSpec(memory_space=pltpu.VMEM)
SM = pl.BlockSpec(memory_space=pltpu.SMEM)


ANY = pl.BlockSpec(memory_space=pl.ANY)


def after(value, *others):
    return lax.optimization_barrier((value, *others))[0]


def call(body, out_shape, in_specs, scratch=(), name=None, room=24, where=VM, work=1024):
    return pl.pallas_call(
        body,
        out_shape=out_shape,
        in_specs=in_specs,
        out_specs=jax.tree.map(lambda _: where, out_shape),
        scratch_shapes=list(scratch),
        compiler_params=pltpu.CompilerParams(vmem_limit_bytes=room * 2**20),
        cost_estimate=pl.CostEstimate(flops=work, bytes_accessed=1024, transcendentals=0),
        name=name,
    )


def fdot(a, b):
    return jnp.dot(a, b, precision=HIGHEST, preferred_element_type=F32)


def bdot(a, b):
    return jnp.dot(a, b, preferred_element_type=F32)


def ring(peers, by):
    return [(i, (i + by) % peers) for i in range(peers)]


def sibling(value):
    return lax.ppermute(value, "chan", ring(2, 1))


def sigmoid(v):
    return 1.0 / (1.0 + jnp.exp(-v))


def start_of(lengths, frame):
    begin = jnp.int32(0)
    end = jnp.int32(0)
    for k in range(NCLIPS):
        end = end + lengths[k]
        begin = jnp.where(end <= frame, end, begin)
    return begin


def clip_of(lengths, frame):
    number = jnp.zeros(frame.shape, jnp.int32)
    end = jnp.int32(0)
    for k in range(NCLIPS):
        end = end + lengths[k]
        number = number + jnp.where(end <= frame, 1, 0)
    return number


def per_clip(lengths, clip, scale):
    inverse = jnp.zeros(clip.shape, F32)
    for k in range(NCLIPS):
        length = jnp.full(clip.shape, lengths[k].astype(F32) * scale, F32)
        inverse = jnp.where(clip == k, 1.0 / length, inverse)
    return inverse


def iota(shape, dim):
    return lax.broadcasted_iota(jnp.int32, shape, dim)


def group_matrix(chans, size):
    return (iota((chans, chans), 0) // size == iota((chans, chans), 1) // size).astype(F32)


def pack_body(peers, cap, frames, grad, video, *refs):
    outs, names, sem = refs[:peers], refs[peers], refs[peers + 1]
    slots = frames.shape[0]
    rows = grad.shape[1]
    tm = lax.axis_index("tm")
    number = [frames[i] for i in range(slots)]
    step = [lax.rem(lax.div(n, slots) - tm + peers, peers) for n in number]
    rank = []
    for i in range(slots):
        r = jnp.int32(0)
        for j in range(i):
            r = r + jnp.where(step[j] == step[i], 1, 0)
        rank.append(r)
    copies = []
    for k in range(peers):
        for j in range(cap):
            at = j * (rows + 1)
            index = jnp.int32(0)
            local = jnp.int32(-1)
            for i in range(slots):
                hit = jnp.logical_and(step[i] == k, rank[i] == j)
                index = jnp.where(hit, i, index)
                local = jnp.where(hit, lax.rem(number[i], slots), local)
            n = 2 * (k * cap + j)
            names[k * cap + j] = jnp.full(grad.shape[2:], local.astype(F32), F32).astype(BF16)
            copies += [
                pltpu.make_async_copy(grad.at[index], outs[k].at[pl.ds(at, rows)], sem.at[n]),
                pltpu.make_async_copy(
                    names.at[pl.ds(k * cap + j, 1)], outs[k].at[pl.ds(at + rows, 1)], sem.at[n + 1]
                ),
            ]
            copies[-2].start()
            copies[-1].start()
    for i in range(2):
        copies.append(
            pltpu.make_async_copy(
                video.at[slots - 2 + i],
                outs[1].at[pl.ds(cap * (rows + 1) + i * rows, rows)],
                sem.at[2 * peers * cap + i],
            )
        )
        copies[-1].start()
    for copy in copies:
        copy.wait()


def named(piece, rows, cap):
    return [
        jnp.max(piece[j * (rows + 1) + rows].astype(F32)).astype(jnp.int32) for j in range(cap)
    ]


def stat_body(size, video, gain, bias, out):
    frames, rows, cols, chans = video.shape
    cells = rows * cols
    average = group_matrix(chans, size) * (1.0 / size)
    sums = [
        jnp.sum(video[t].astype(F32).reshape(cells, chans), axis=0, keepdims=True)
        for t in range(frames)
    ]
    mean = fdot(jnp.concatenate(sums, axis=0) * (1.0 / cells), average)
    squares = []
    for t in range(frames):
        apart = video[t].astype(F32).reshape(cells, chans) - mean[t : t + 1]
        squares.append(jnp.sum(apart * apart, axis=0, keepdims=True))
    var = fdot(jnp.concatenate(squares, axis=0) * (1.0 / cells), average)
    rest = jnp.concatenate(
        [gain[...], bias[...], jnp.zeros((6, chans), F32)], axis=0
    )
    whole = jnp.concatenate([mean, var, rest], axis=0)
    for i in range(out.shape[0]):
        out[i] = whole


def turn_body(weight, out):
    for i in range(9):
        for col in range(3):
            out[i, col * 256 : (col + 1) * 256] = weight[i, col * 256 : (col + 1) * 256].T


def table_body(lengths, got, out):
    peers, bands = got.shape[:2]
    frames = (got.shape[3] - 8) // 2
    first = lax.axis_index("tm") * frames
    count = peers * frames
    clip = clip_of(lengths, iota((count, count), 1))
    inverse = per_clip(lengths, clip, 1.0)
    same = jnp.where(clip_of(lengths, iota((count, count), 0)) == clip, inverse, 0.0)
    near = jnp.clip(first - 2 + iota((16, count), 0), 0, count - 1)
    clip = clip_of(lengths, iota((16, count), 1))
    inverse = per_clip(lengths, clip, 1.0)
    picked = jnp.where(clip_of(lengths, near) == clip, inverse, 0.0)
    for c in range(2):
        mean = [
            jnp.concatenate([got[t, h, c, :frames] for t in range(peers)], axis=0)
            for h in range(bands)
        ]
        var = [
            jnp.concatenate([got[t, h, c, frames : 2 * frames] for t in range(peers)], axis=0)
            for h in range(bands)
        ]
        average = sum(mean[1:], mean[0]) * (1.0 / bands)
        clip_mean = fdot(same, average)
        spread = jnp.zeros_like(average)
        for h in range(bands):
            apart = mean[h] - clip_mean
            spread = spread + (var[h] + apart * apart)
        out[c, :16] = fdot(picked, average)
        out[c, 16:32] = lax.rsqrt(fdot(picked, spread * (1.0 / bands)) + 1e-06)
        out[c, 32:] = got[0, 0, c, 2 * frames :]


def shifts(value):
    length = value.shape[0]
    column = lax.rem(iota(value.shape, 0), 16)
    before = jnp.where(column == 0, 0.0, pltpu.roll(value, 1, 0))
    after = jnp.where(column == 15, 0.0, pltpu.roll(value, length - 1, 0))
    return before, after


def weight_body(peers, bands, cap, block, *refs):
    refs = list(refs)
    lengths, table = refs.pop(0), refs.pop(0)
    take = lambda n: [refs.pop(0) for _ in range(n)]
    own, sib, prev_sib = take(bands), take(bands), take(bands)
    ups = [take(peers) for _ in range(bands)]
    outs = take(peers)
    active, upright = refs
    frames, rows, cols, chans = own[0].shape
    cells = rows * cols
    width = peers * block
    tm, h, c = lax.axis_index("tm"), lax.axis_index("height"), lax.axis_index("chan")
    first = tm * frames
    band = [lax.rem(h - m + bands, bands) for m in range(bands)]
    place = iota((chans, width), 1)
    wanted = (lax.rem(tm + lax.div(place, block), peers) * bands + h) * block + lax.rem(place, block)
    channel = iota((chans, width), 0)
    pick_own = (c * chans + channel == wanted).astype(F32)
    pick_sib = ((1 - c) * chans + channel == wanted).astype(F32)
    lookup = fdot(table[c], pick_own) + fdot(table[1 - c], pick_sib)
    pick_own, pick_sib = pick_own.astype(BF16), pick_sib.astype(BF16)
    mean, inv = lookup[:16], lookup[16:32]
    scale = inv * lookup[32:33]
    bias = lookup[33:34]
    names = [named(ups[0][k], rows, cap) for k in range(peers)]
    for col in range(3):
        active[col, :, 0] = jnp.zeros((frames + 2, cols, width), BF16)
        active[col, :, bands * rows + 1] = jnp.zeros((frames + 2, cols, width), BF16)
    for f in range(frames + 2):
        for m in range(bands):
            if f < 2:
                at = cap * (rows + 1) + f * rows
                a, b = ups[m][1][at : at + rows], prev_sib[m][at : at + rows]
            else:
                a, b = own[m][f - 2], sib[m][f - 2]
            x = bdot(a.reshape(cells, chans), pick_own) + bdot(b.reshape(cells, chans), pick_sib)
            v = (x - mean[f : f + 1]) * scale[f : f + 1] + bias
            v = v * sigmoid(v)
            before, after = shifts(v)
            at = pl.ds(band[m] * rows + 1, rows)
            for col, moved in enumerate((before, v, after)):
                active[col, f, at] = moved.astype(BF16).reshape(rows, cols, width)
    for k in range(peers):
        for j in range(cap):
            at = j * (rows + 1)
            local = names[k][j]

            @pl.when(local >= 0)
            def _():
                for m in range(bands):
                    u = ups[m][k][at : at + rows].reshape(cells, chans)
                    upright[local, m] = u.T

    begin = [start_of(lengths, first + t) for t in range(frames)]

    def taps(i, count):
        where = []
        for n in range(count):
            tap = 2 * i + n
            a = lax.div(tap, 9)
            where.append((a, lax.rem(lax.div(tap, 3), 3), lax.rem(tap, 3)))
        total = jnp.zeros((chans, count * width), F32)
        for t in range(frames):
            for m in range(bands):
                patch = []
                for a, b, col in where:
                    s = jnp.maximum(first + t - 2 + a, begin[t]) - (first - 2)
                    lines = active[col, s, pl.ds(band[m] * rows + b, rows)]
                    patch.append(lines.reshape(cells, width))
                patch = jnp.concatenate(patch, axis=1) if count > 1 else patch[0]
                total = total + bdot(upright[t, m], patch)
        for n in range(count):
            piece = total[:, n * width : (n + 1) * width].T
            for k in range(peers):
                outs[k][2 * i + n] = piece[k * block : (k + 1) * block].astype(outs[k].dtype)

    def pair(i, carry):
        taps(i, 2)
        return carry

    lax.fori_loop(0, 13, pair, 0)
    taps(jnp.int32(13), 1)


def forward_body(bands, skip, lengths, table, weight, *refs):
    own, sib, above_own, above_sib, below_own, below_sib = refs[:6]
    prev_own, prev_sib = refs[6:8]
    far_prev = refs[8:12]
    keep, give, active = refs[12:]
    frames, rows, cols, chans = own.shape
    half = rows // 2
    tm, h, c = lax.axis_index("tm"), lax.axis_index("height"), lax.axis_index("chan")
    first = tm * frames
    outer = jnp.logical_or(
        jnp.logical_and(c == 0, h > 0), jnp.logical_and(c == 1, h < bands - 1)
    )
    begin = [start_of(lengths, first + t) for t in range(frames)]

    def put(f, at, lines, value_own, value_sib, ok):
        a, b = value_own.astype(F32), value_sib.astype(F32)
        for side, x in enumerate((jnp.where(c == 0, a, b), jnp.where(c == 0, b, a))):
            mean = table[side, f : f + 1]
            scale = table[side, 16 + f : 17 + f] * table[side, 32:33]
            v = (x - mean) * scale + table[side, 33:34]
            v = v * sigmoid(v)
            if ok is not None:
                v = jnp.where(ok, v, 0.0)
            before, after = shifts(v)
            for n, w in enumerate((before, v, after)):
                lane = n * 2 * chans + side * chans
                active[f, at, :, lane : lane + chans] = w.astype(BF16).reshape(lines, cols, chans)

    def edge(up, down):
        return jnp.where(c == 0, up.astype(F32), down.astype(F32))

    for f in range(frames + 2):
        if f < 2:
            base = skip + f * rows
            near = pl.ds(base + (half - 1) * c, half + 1)
            here = [v[near] for v in (prev_own, prev_sib)]
            up = [v[base + rows - 1] for v in far_prev[:2]]
            down = [v[base] for v in far_prev[2:]]
        else:
            near = pl.ds((half - 1) * c, half + 1)
            here = [v[f - 2, near] for v in (own, sib)]
            up = [v[f - 2, rows - 1] for v in (above_own, above_sib)]
            down = [v[f - 2, 0] for v in (below_own, below_sib)]
        here = [v.reshape((half + 1) * cols, chans) for v in here]
        put(f, pl.ds(1 - c, half + 1), half + 1, here[0], here[1], None)
        put(
            f, pl.ds((half + 1) * c, 1), 1,
            edge(up[0], down[0]), edge(up[1], down[1]), outer,
        )
    batch = 4
    for t0 in range(0, frames, batch):
        mixed = [jnp.zeros((half * cols, 2 * chans), F32) for _ in range(batch)]
        for a in range(3):
            for b in range(3):
                w = weight[a * 3 + b]
                for q in range(batch):
                    t = t0 + q
                    s = jnp.maximum(first + t - 2 + a, begin[t]) - (first - 2)
                    patch = active[s, b : b + half].reshape(half * cols, 6 * chans)
                    mixed[q] = mixed[q] + bdot(patch, w)
        for q in range(batch):
            t = t0 + q
            mine = pl.ds(c * half, half)
            left, right = mixed[q][:, :chans], mixed[q][:, chans:]
            shape = (half, cols, chans)
            for out, value, x in (
                (keep, jnp.where(c == 0, left, right), own[t, mine]),
                (give, jnp.where(c == 0, right, left), sib[t, mine]),
            ):
                x = x.reshape(half * cols, chans).astype(F32)
                out[t] = (x + value).astype(BF16).reshape(shape)


def order_body(peers, bands, cap, *refs):
    own, above, below = refs[:peers], refs[peers : 2 * peers], refs[2 * peers : 3 * peers]
    out, first = refs[3 * peers :]
    rows = out.shape[1] - 2
    h = lax.axis_index("height")
    names = [named(own[k], rows, cap) for k in range(peers)]
    for k in range(peers):
        for j in range(cap):
            at = j * (rows + 1)
            local = names[k][j]

            @pl.when(local >= 0)
            def _():
                out[local, 1 : rows + 1] = own[k][at : at + rows]
                top = above[k][at + rows - 1].astype(F32)
                bottom = below[k][at].astype(F32)
                out[local, 0] = jnp.where(h > 0, top, 0.0).astype(BF16)
                out[local, rows + 1] = jnp.where(h < bands - 1, bottom, 0.0).astype(BF16)

    first[...] = out[:2]


def backward_body(peers, lengths, table, weight, own, sib, up, up_sib, next_own, next_sib, *refs):
    keep, give, sums, spatial, total = refs
    frames, rows, cols, chans = own.shape
    half = rows // 2
    cells = half * cols
    tm, c = lax.axis_index("tm"), lax.axis_index("chan")
    first = tm * frames
    for f in range(frames + 2):
        a, b, g = (up, up_sib, f) if f < frames else (next_own, next_sib, f - frames)
        a = a[g, pl.ds(c * half, half + 2)].reshape(cells + 2 * cols, chans).astype(F32)
        b = b[g, pl.ds(c * half, half + 2)].reshape(cells + 2 * cols, chans).astype(F32)
        for side, v in enumerate((jnp.where(c == 0, a, b), jnp.where(c == 0, b, a))):
            before, after = shifts(v)
            for n, w in enumerate((after, v, before)):
                at = n * 2 * chans + side * chans
                spatial[f, :, :, at : at + chans] = w.astype(BF16).reshape(half + 2, cols, chans)
    total[...] = jnp.zeros_like(total)

    begin = [start_of(lengths, first + t) for t in range(frames + 2)]
    for a in range(3):
        last = frames + 2 - a
        for low, high in ((0, last // 2), (last // 2, last)):
            grads = [jnp.zeros((cells, 2 * chans), F32) for _ in range(low, high)]
            for b in range(3):
                w = weight[a * 3 + b]
                for t in range(low, high):
                    patch = spatial[t, 2 - b : 2 - b + half].reshape(cells, 6 * chans)
                    grads[t - low] = grads[t - low] + bdot(patch, w)
            for t in range(low, high):
                s = jnp.maximum(first + t - 2 + a, begin[t]) - first
                s = jnp.where(jnp.logical_and(s >= 0, s < frames), s, frames)
                total[s] += grads[t - low]
    mine = pl.ds(c * half, half)
    member = (
        clip_of(lengths, first + iota((NCLIPS, frames), 1)) == iota((NCLIPS, frames), 0)
    ).astype(F32)
    for side in range(2):
        firsts, seconds = [], []
        for t in range(frames):
            a, b = own[t, mine].astype(F32), sib[t, mine].astype(F32)
            x = jnp.where((c == 0) == (side == 0), a, b).reshape(cells, chans)
            hat = (x - table[side, t + 2 : t + 3]) * table[side, t + 18 : t + 19]
            v = hat * table[side, 32:33] + table[side, 33:34]
            s = sigmoid(v)
            grad = total[t, :, side * chans : (side + 1) * chans] * s * (1.0 + v * (1.0 - s))
            total[t, :, side * chans : (side + 1) * chans] = grad
            firsts.append(jnp.sum(grad, axis=0, keepdims=True))
            seconds.append(jnp.sum(grad * hat, axis=0, keepdims=True))
        whole = jnp.concatenate(
            [
                fdot(member, jnp.concatenate(firsts, axis=0)),
                fdot(member, jnp.concatenate(seconds, axis=0)),
            ],
            axis=0,
        )
        for i in range(sums.shape[0] // 2):
            sums[2 * i + side] = whole
    for t in range(frames):
        left, right = total[t, :, :chans], total[t, :, chans:]
        keep[t] = jnp.where(c == 0, left, right)
        give[t] = jnp.where(c == 0, right, left)


def collect_body(own, *refs):
    terms, out = refs[:-1], refs[-1]
    for tap in range(own.shape[0]):
        total = own[tap]
        for term in terms:
            total = total + term[tap].astype(F32)
        out[tap] = total


def finish_body(size, bands, lengths, table, got, video, keep, other, up, out, small):
    frames, rows, cols, chans = video.shape
    half = rows // 2
    cells = half * cols
    tm, c = lax.axis_index("tm"), lax.axis_index("chan")
    first_frame = tm * frames
    whole = jnp.sum(got[...], axis=0)
    gain = table[c, 32:33]
    small[0:1] = jnp.sum(whole[NCLIPS:], axis=0, keepdims=True)
    small[1:2] = jnp.sum(whole[:NCLIPS], axis=0, keepdims=True)
    small[2:] = jnp.zeros((6, chans), F32)
    group = group_matrix(chans, size)
    clip = iota((frames, NCLIPS), 1)
    inverse = per_clip(lengths, clip, float(rows * bands * cols * size))
    spread = jnp.where(clip_of(lengths, first_frame + iota((frames, NCLIPS), 0)) == clip, inverse, 0.0)
    first = fdot(spread, fdot(whole[:NCLIPS] * gain, group))
    second = fdot(spread, fdot(whole[NCLIPS:] * gain, group))
    for t in range(frames):
        inv = table[c, t + 18 : t + 19]
        for grads, at in ((keep, c * half), (other, (1 - c) * half)):
            x = video[t, pl.ds(at, half)].reshape(cells, chans).astype(F32)
            hat = (x - table[c, t + 2 : t + 3]) * inv
            part = inv * (grads[t] * gain - first[t : t + 1] - hat * second[t : t + 1])
            u = up[t, pl.ds(at + 1, half)].reshape(cells, chans).astype(F32)
            out[t, pl.ds(at, half)] = (u + part).astype(BF16).reshape(half, cols, chans)


def per_device(
    clip_video, norm_gain, norm_bias, conv_weight, clip_lengths, packed_frame, packed_grad
):
    frames, rows, cols, chans = clip_video.shape
    full = conv_weight.shape[3]
    peers = lax.axis_size("tm")
    bands = lax.axis_size("height")
    c = lax.axis_index("chan")
    size = full // GROUPS
    cap = max(1, frames // peers)
    block = full // (peers * bands)
    width = peers * block
    half = rows // 2
    everyone = ("tm", "height", "chan")
    devices = peers * bands * 2
    sds = jax.ShapeDtypeStruct

    skip = cap * (rows + 1)
    pieces = call(
        functools.partial(pack_body, peers, cap),
        [
            sds((skip + (2 * rows if k == 1 else 0), cols, chans), BF16)
            for k in range(peers)
        ],
        [SM, ANY, ANY],
        [
            pltpu.VMEM((peers * cap, cols, chans), BF16),
            pltpu.SemaphoreType.DMA((2 * peers * cap + 2,)),
        ],
        name="pack", where=ANY,
    )(packed_frame, packed_grad, clip_video)
    ups = [[pieces[0]] + [lax.ppermute(pieces[k], "tm", ring(peers, k)) for k in range(1, peers)]]

    stats = call(
        functools.partial(stat_body, size),
        sds((devices, 2 * frames + 8, chans), F32), [VM, VM, VM],
        name="stat",
    )(after(clip_video, pieces[0]), norm_gain[None], norm_bias[None])

    got = lax.all_to_all(stats, everyone, 0, 0)
    got = got.reshape(peers, bands, 2, 2 * frames + 8, chans)

    own = [clip_video]
    for m in range(1, bands):
        own.append(lax.ppermute(after(clip_video, pieces[0]), "height", ring(bands, m)))
    sib = [sibling(v) for v in own]
    for m in range(1, bands):
        ups.append([lax.ppermute(after(v, got), "height", ring(bands, m)) for v in ups[0]])
    prev_sib = [sibling(v[1]) for v in ups]

    weight = conv_weight.reshape(9, 3 * full, full)
    turned = call(
        turn_body, sds(weight.shape, BF16), [VM], name="turn"
    )(weight)
    table = call(
        table_body, sds((2, 40, chans), F32), [SM, VM], name="table"
    )(clip_lengths, after(got, turned))

    grads = call(
        functools.partial(weight_body, peers, bands, cap, block),
        [sds((27, block, chans), F32)] + [sds((27, block, chans), BF16)] * (peers - 1),
        [SM] + [VM] * (1 + 3 * bands + peers * bands),
        [
            pltpu.VMEM((3, frames + 2, bands * rows + 2, cols, width), BF16),
            pltpu.VMEM((frames, bands, chans, rows * cols), BF16),
        ],
        name="weight",
    )(
        clip_lengths, table, *own, *sib, *prev_sib,
        *[v for band in ups for v in band],
    )
    far = bands - 1
    up, up_first = call(
        functools.partial(order_body, peers, bands, cap),
        [sds((frames, rows + 2, cols, chans), BF16), sds((2, rows + 2, cols, chans), BF16)],
        [VM] * (3 * peers),
        name="order",
    )(*ups[0], *ups[1], *ups[far])
    up_sib = sibling(up)
    next_own = lax.ppermute(up_first, "tm", [(t + 1, t) for t in range(peers - 1)])
    next_sib = sibling(next_own)
    part = sds((frames, half * cols, chans), F32)
    keep, give, sums = call(
        functools.partial(backward_body, peers),
        [part, part, sds((devices, 2 * NCLIPS, chans), F32)],
        [SM] + [VM] * 8,
        [
            pltpu.VMEM((frames + 2, half + 2, cols, 6 * chans), BF16),
            pltpu.VMEM((frames + 1, half * cols, 2 * chans), F32),
        ],
        name="backward",
    )(clip_lengths, table, after(turned, grads[0]), clip_video, sib[0], up, up_sib, next_own, next_sib)
    totals = lax.all_to_all(sums, everyone, 0, 0)
    other = sibling(give)

    part = sds((frames, half, cols, chans), BF16)
    block_keep, block_give = call(
        functools.partial(forward_body, bands, skip),
        [part, part],
        [SM] + [VM] * 14,
        [pltpu.VMEM((frames + 2, half + 2, cols, 6 * chans), BF16)],
        name="forward",
    )(
        clip_lengths, table, after(weight, sums), own[0], sib[0], own[1], sib[1], own[far], sib[far],
        ups[0][1], prev_sib[0], ups[1][1], prev_sib[1], ups[far][1], prev_sib[far],
    )
    block_other = sibling(block_give)
    block_out = jnp.where(
        c == 0,
        jnp.concatenate([block_keep, block_other], axis=1),
        jnp.concatenate([block_other, block_keep], axis=1),
    )

    terms = [lax.ppermute(grads[k], "tm", ring(peers, k)) for k in range(1, peers)]
    weight_grad = call(
        collect_body, sds((27, block, chans), F32), [VM] * peers, name="collect", work=10**13
    )(after(grads[0], block_out), *terms)
    weight_grad = weight_grad.reshape(3, 3, 3, block, chans)

    video_grad, small = call(
        functools.partial(finish_body, size, bands),
        [sds(clip_video.shape, BF16), sds((8, chans), F32)],
        [SM] + [VM] * 6,
        name="finish",
    )(clip_lengths, table, after(totals, weight_grad), clip_video, keep, other, up)
    return (block_out, video_grad, weight_grad, small[0], small[1])


def solution(mesh):
    placed = (
        P(("groups", "tm"), "height", None, "chan"),
        P("chan"),
        P("chan"),
        P(),
        P("groups"),
        P(("groups", "tm")),
        P(("groups", "tm"), "height", None, "chan"),
    )
    return jax.shard_map(
        per_device,
        mesh=mesh,
        in_specs=placed,
        out_specs=(
            P(("groups", "tm"), "height", None, "chan"),
            P(("groups", "tm"), "height", None, "chan"),
            P("groups", None, None, ("tm", "height"), "chan"),
            P(("groups", "chan")),
            P(("groups", "chan")),
        ),
        check_vma=False,
    )
```

```python
import functools
import jax
import jax.numpy as jnp
from jax import lax
from jax.experimental import pallas as pl
from jax.experimental.pallas import tpu as pltpu
from jax.sharding import PartitionSpec as P

GROUPS = 32
NCLIPS = 8
F32 = jnp.float32
BF16 = jnp.bfloat16
HIGHEST = lax.Precision.HIGHEST
VM = pl.BlockSpec(memory_space=pltpu.VMEM)
SM = pl.BlockSpec(memory_space=pltpu.SMEM)


ANY = pl.BlockSpec(memory_space=pl.ANY)
HB = pl.BlockSpec(memory_space=pltpu.HBM)


def after(value, *others):
    return lax.optimization_barrier((value, *others))[0]


def call(body, out_shape, in_specs, scratch=(), name=None, room=20, where=VM, work=1024):
    return pl.pallas_call(
        body,
        out_shape=out_shape,
        in_specs=in_specs,
        out_specs=jax.tree.map(lambda _: where, out_shape),
        scratch_shapes=list(scratch),
        compiler_params=pltpu.CompilerParams(vmem_limit_bytes=room * 2**20),
        cost_estimate=pl.CostEstimate(flops=work, bytes_accessed=1024, transcendentals=0),
        name=name,
    )


def fdot(a, b):
    return jnp.dot(a, b, precision=HIGHEST, preferred_element_type=F32)


def bdot(a, b):
    return jnp.dot(a, b, preferred_element_type=F32)


def ring(peers, by):
    return [(i, (i + by) % peers) for i in range(peers)]


def sibling(value):
    return lax.ppermute(value, "chan", ring(2, 1))


def sigmoid(v):
    return 1.0 / (1.0 + jnp.exp(-v))


def start_of(lengths, frame):
    begin = jnp.int32(0)
    end = jnp.int32(0)
    for k in range(NCLIPS):
        end = end + lengths[k]
        begin = jnp.where(end <= frame, end, begin)
    return begin


def clip_of(lengths, frame):
    number = jnp.zeros(frame.shape, jnp.int32)
    end = jnp.int32(0)
    for k in range(NCLIPS):
        end = end + lengths[k]
        number = number + jnp.where(end <= frame, 1, 0)
    return number


def per_clip(lengths, clip, scale):
    inverse = jnp.zeros(clip.shape, F32)
    for k in range(NCLIPS):
        length = jnp.full(clip.shape, lengths[k].astype(F32) * scale, F32)
        inverse = jnp.where(clip == k, 1.0 / length, inverse)
    return inverse


def iota(shape, dim):
    return lax.broadcasted_iota(jnp.int32, shape, dim)


def group_matrix(chans, size):
    return (iota((chans, chans), 0) // size == iota((chans, chans), 1) // size).astype(F32)


def split(value):
    parts = []
    for _ in range(3):
        part = value.astype(BF16)
        parts.append(part)
        value = value - part.astype(F32)
    return parts


def pack_body(peers, cap, size, frames, grad, video_far, *refs):
    outs = refs[:peers]
    names, video, stats, sem, far, done = refs[peers:]
    slots, rows, cols, chans = grad.shape
    cells = rows * cols
    loads = [
        pltpu.make_async_copy(video_far.at[t], video.at[t], far.at[t]) for t in range(slots)
    ]
    for load in loads:
        load.start()
    tm = lax.axis_index("tm")
    number = [frames[i] for i in range(slots)]
    step = [lax.rem(lax.div(n, slots) - tm + peers, peers) for n in number]
    rank = []
    for i in range(slots):
        r = jnp.int32(0)
        for j in range(i):
            r = r + jnp.where(step[j] == step[i], 1, 0)
        rank.append(r)
    copies = []
    for k in range(peers):
        for j in range(cap):
            at = j * (rows + 1)
            index = jnp.int32(0)
            local = jnp.int32(-1)
            for i in range(slots):
                hit = jnp.logical_and(step[i] == k, rank[i] == j)
                index = jnp.where(hit, i, index)
                local = jnp.where(hit, lax.rem(number[i], slots), local)
            n = 2 * (k * cap + j)
            names[k * cap + j] = jnp.full(grad.shape[2:], local.astype(F32), F32).astype(BF16)
            copies += [
                pltpu.make_async_copy(grad.at[index], outs[k].at[pl.ds(at, rows)], sem.at[n]),
                pltpu.make_async_copy(
                    names.at[pl.ds(k * cap + j, 1)], outs[k].at[pl.ds(at + rows, 1)], sem.at[n + 1]
                ),
            ]
            copies[-2].start()
            copies[-1].start()
    base = cap * (rows + 1)
    for i in range(2):
        copies.append(
            pltpu.make_async_copy(
                video_far.at[slots - 2 + i],
                outs[1].at[pl.ds(base + 3 + i * rows, rows)],
                sem.at[2 * peers * cap + i],
            )
        )
        copies[-1].start()
    average = group_matrix(chans, size) * (1.0 / size)
    sums = []
    for t in range(slots):
        loads[t].wait()
        sums.append(jnp.sum(video[t].astype(F32).reshape(cells, chans), axis=0, keepdims=True))
    mean = fdot(jnp.concatenate(sums, axis=0) * (1.0 / cells), average)
    squares = []
    for t in range(slots):
        apart = video[t].astype(F32).reshape(cells, chans) - mean[t : t + 1]
        squares.append(jnp.sum(apart * apart, axis=0, keepdims=True))
    var = fdot(jnp.concatenate(squares, axis=0) * (1.0 / cells), average)
    for n, part in enumerate(split(jnp.concatenate([mean, var], axis=0))):
        stats[n] = part
    for k in range(peers):
        copies.append(pltpu.make_async_copy(stats, outs[k].at[pl.ds(base, 3)], done.at[k]))
        copies[-1].start()
    for copy in copies:
        copy.wait()


def named(piece, rows, cap):
    return [
        jnp.max(piece[j * (rows + 1) + rows].astype(F32)).astype(jnp.int32) for j in range(cap)
    ]


def turn_body(weight, out):
    for i in range(9):
        for col in range(3):
            out[i, col * 256 : (col + 1) * 256] = weight[i, col * 256 : (col + 1) * 256].T


def shifts(value):
    length = value.shape[0]
    column = lax.rem(iota(value.shape, 0), 16)
    before = jnp.where(column == 0, 0.0, pltpu.roll(value, 1, 0))
    after = jnp.where(column == 15, 0.0, pltpu.roll(value, length - 1, 0))
    return before, after


def weight_body(peers, bands, cap, block, *refs):
    refs = list(refs)
    lengths, table, table_sib = [refs.pop(0) for _ in range(3)]
    take = lambda n: [refs.pop(0) for _ in range(n)]
    own, sib, prev_sib = take(bands), take(bands), take(bands)
    ups = [take(peers) for _ in range(bands)]
    outs = take(peers)
    active, upright = refs
    frames, rows, cols, chans = own[0].shape
    cells = rows * cols
    width = peers * block
    tm, h, c = lax.axis_index("tm"), lax.axis_index("height"), lax.axis_index("chan")
    first = tm * frames
    band = [lax.rem(h - m + bands, bands) for m in range(bands)]
    place = iota((chans, width), 1)
    wanted = (lax.rem(tm + lax.div(place, block), peers) * bands + h) * block + lax.rem(place, block)
    channel = iota((chans, width), 0)
    pick_own = (c * chans + channel == wanted).astype(F32)
    pick_sib = ((1 - c) * chans + channel == wanted).astype(F32)
    lookup = fdot(table[...], pick_own) + fdot(table_sib[...], pick_sib)
    pick_own, pick_sib = pick_own.astype(BF16), pick_sib.astype(BF16)
    mean, inv = lookup[:16], lookup[16:32]
    scale = inv * lookup[32:33]
    bias = lookup[33:34]
    names = [named(ups[0][k], rows, cap) for k in range(peers)]
    for col in range(3):
        active[col, :, 0] = jnp.zeros((frames + 2, cols, width), BF16)
        active[col, :, bands * rows + 1] = jnp.zeros((frames + 2, cols, width), BF16)
    for f in range(frames + 2):
        for m in range(bands):
            if f < 2:
                at = cap * (rows + 1) + 3 + f * rows
                a, b = ups[m][1][at : at + rows], prev_sib[m][at : at + rows]
            else:
                a, b = own[m][f - 2], sib[m][f - 2]
            x = bdot(a.reshape(cells, chans), pick_own) + bdot(b.reshape(cells, chans), pick_sib)
            v = (x - mean[f : f + 1]) * scale[f : f + 1] + bias
            v = v * sigmoid(v)
            before, after = shifts(v)
            at = pl.ds(band[m] * rows + 1, rows)
            for col, moved in enumerate((before, v, after)):
                active[col, f, at] = moved.astype(BF16).reshape(rows, cols, width)
    for k in range(peers):
        for j in range(cap):
            at = j * (rows + 1)
            local = names[k][j]

            @pl.when(local >= 0)
            def _():
                for m in range(bands):
                    u = ups[m][k][at : at + rows].reshape(cells, chans)
                    upright[local, m] = u.T

    begin = [start_of(lengths, first + t) for t in range(frames)]

    def taps(i, count):
        where = []
        for n in range(count):
            tap = 2 * i + n
            a = lax.div(tap, 9)
            where.append((a, lax.rem(lax.div(tap, 3), 3), lax.rem(tap, 3)))
        total = jnp.zeros((chans, count * width), F32)
        for t in range(frames):
            for m in range(bands):
                patch = []
                for a, b, col in where:
                    s = jnp.maximum(first + t - 2 + a, begin[t]) - (first - 2)
                    lines = active[col, s, pl.ds(band[m] * rows + b, rows)]
                    patch.append(lines.reshape(cells, width))
                patch = jnp.concatenate(patch, axis=1) if count > 1 else patch[0]
                total = total + bdot(upright[t, m], patch)
        for n in range(count):
            piece = total[:, n * width : (n + 1) * width].T
            for k in range(peers):
                outs[k][2 * i + n] = piece[k * block : (k + 1) * block].astype(outs[k].dtype)

    def pair(i, carry):
        taps(i, 2)
        return carry

    lax.fori_loop(0, 13, pair, 0)
    taps(jnp.int32(13), 1)


def both(c, table, table_sib):
    return (
        jnp.where(c == 0, table[...], table_sib[...]),
        jnp.where(c == 0, table_sib[...], table[...]),
    )


def forward_body(bands, skip, lengths, table, table_sib, weight_far, *refs):
    core, above, below = refs[:2], refs[2:4], refs[4:6]
    before, before_above, before_below = refs[6:8], refs[8:10], refs[10:12]
    keep, give, active, here, weight, sem = refs[12:]
    frames, rows, cols, chans = core[0].shape
    half = rows // 2
    tm, h, c = lax.axis_index("tm"), lax.axis_index("height"), lax.axis_index("chan")
    first = tm * frames
    load = pltpu.make_async_copy(weight_far, weight, sem.at[12])
    near, place = pl.ds((half - 1) * c, half + 1), pl.ds(1 - c, half + 1)
    outside = pl.ds((half + 1) * c, 1)
    waits = []
    for n in range(2):
        waits.append(
            pltpu.make_async_copy(
                core[n].at[:, near], here.at[n, pl.ds(2, frames), place], sem.at[6 * n]
            )
        )
        waits[-1].start()
        for f in range(2):
            line = skip + f * rows
            waits.append(
                pltpu.make_async_copy(
                    before[n].at[pl.ds(line + (half - 1) * c, half + 1)],
                    here.at[n, f, place],
                    sem.at[6 * n + 1 + f],
                )
            )
            waits[-1].start()
        for side, rim, rim_before, row in (
            (0, above[n], before_above[n], rows - 1),
            (1, below[n], before_below[n], 0),
        ):
            edges = [
                pltpu.make_async_copy(
                    rim.at[:, pl.ds(row, 1)],
                    here.at[n, pl.ds(2, frames), outside],
                    sem.at[6 * n + 3],
                )
            ]
            for f in range(2):
                edges.append(
                    pltpu.make_async_copy(
                        rim_before.at[pl.ds(skip + f * rows + row, 1)],
                        here.at[n, f, outside],
                        sem.at[6 * n + 4 + f],
                    )
                )

            @pl.when(c == side)
            def _():
                for edge in edges:
                    edge.start()

        waits += edges
    load.start()
    for wait in waits:
        wait.wait()
    outer = jnp.logical_or(
        jnp.logical_and(c == 0, h > 0), jnp.logical_and(c == 1, h < bands - 1)
    )
    begin = [start_of(lengths, first + t) for t in range(frames)]
    tables = both(c, table, table_sib)
    cells = (half + 2) * cols
    line = iota((cells, chans), 0)
    rim = jnp.logical_or(
        jnp.logical_and(line < cols, c == 0), jnp.logical_and(line >= cells - cols, c == 1)
    )
    ok = jnp.logical_or(jnp.logical_not(rim), outer)
    for f in range(frames + 2):
        a, b = [here[n, f].reshape(cells, chans).astype(F32) for n in range(2)]
        for side, x in enumerate((jnp.where(c == 0, a, b), jnp.where(c == 0, b, a))):
            info = tables[side]
            scale = info[16 + f : 17 + f] * info[32:33]
            v = (x - info[f : f + 1]) * scale + info[33:34]
            v = jnp.where(ok, v * sigmoid(v), 0.0)
            left, right = shifts(v)
            for n, w in enumerate((left, v, right)):
                lane = n * 2 * chans + side * chans
                active[f, :, :, lane : lane + chans] = w.astype(BF16).reshape(half + 2, cols, chans)
    load.wait()
    batch = 4
    for t0 in range(0, frames, batch):
        mixed = [jnp.zeros((half * cols, 2 * chans), F32) for _ in range(batch)]
        for a in range(3):
            for b in range(3):
                w = weight[a * 3 + b]
                for q in range(batch):
                    t = t0 + q
                    s = jnp.maximum(first + t - 2 + a, begin[t]) - (first - 2)
                    patch = active[s, b : b + half].reshape(half * cols, 6 * chans)
                    mixed[q] = mixed[q] + bdot(patch, w)
        for q in range(batch):
            t = t0 + q
            mine = slice(1, half + 1)
            left, right = mixed[q][:, :chans], mixed[q][:, chans:]
            shape = (half, cols, chans)
            for out, value, x in (
                (keep, jnp.where(c == 0, left, right), here[0, t + 2, mine]),
                (give, jnp.where(c == 0, right, left), here[1, t + 2, mine]),
            ):
                x = x.reshape(half * cols, chans).astype(F32)
                out[t] = (x + value).astype(BF16).reshape(shape)


def order_body(peers, bands, cap, lengths, gain, bias, *refs):
    pieces = [refs[m * peers : (m + 1) * peers] for m in range(bands)]
    out, first, table = refs[bands * peers :]
    own, above, below = pieces[0], pieces[1], pieces[bands - 1]
    frames = out.shape[0]
    base = cap * (out.shape[1] - 1)
    tm = lax.axis_index("tm")
    count = peers * frames

    def frame_of(index):
        slab = lax.rem(tm - lax.div(index, frames) + peers, peers)
        return slab * frames + lax.rem(index, frames)

    means, spreads = [], []
    for m in range(bands):
        stats = [
            sum(piece[base + n].astype(F32) for n in (2, 1, 0)) for piece in pieces[m]
        ]
        means.append(jnp.concatenate([v[:frames] for v in stats], axis=0))
        spreads.append(jnp.concatenate([v[frames:] for v in stats], axis=0))
    clip = clip_of(lengths, frame_of(iota((count, count), 1)))
    inverse = per_clip(lengths, clip, 1.0)
    same = jnp.where(clip_of(lengths, frame_of(iota((count, count), 0))) == clip, inverse, 0.0)
    near = jnp.clip(tm * frames - 2 + iota((16, count), 0), 0, count - 1)
    picked = jnp.where(clip_of(lengths, near) == clip[:16], inverse[:16], 0.0)
    average = sum(means[1:], means[0]) * (1.0 / bands)
    clip_mean = fdot(same, average)
    spread = jnp.zeros_like(average)
    for m in range(bands):
        apart = means[m] - clip_mean
        spread = spread + (spreads[m] + apart * apart)
    table[:16] = fdot(picked, average)
    table[16:32] = lax.rsqrt(fdot(picked, spread * (1.0 / bands)) + 1e-06)
    table[32:33] = gain[...]
    table[33:34] = bias[...]
    table[34:] = jnp.zeros((6, table.shape[1]), F32)
    rows = out.shape[1] - 2
    h = lax.axis_index("height")
    names = [named(own[k], rows, cap) for k in range(peers)]
    for k in range(peers):
        for j in range(cap):
            at = j * (rows + 1)
            local = names[k][j]

            @pl.when(local >= 0)
            def _():
                out[local, 1 : rows + 1] = own[k][at : at + rows]
                top = above[k][at + rows - 1].astype(F32)
                bottom = below[k][at].astype(F32)
                out[local, 0] = jnp.where(h > 0, top, 0.0).astype(BF16)
                out[local, rows + 1] = jnp.where(h < bands - 1, bottom, 0.0).astype(BF16)

    first[...] = out[:2]


def backward_body(peers, lengths, table, table_sib, weight, own, sib, up, up_sib, next_own, next_sib, *refs):
    keep, give, sums, spatial, total = refs
    frames, rows, cols, chans = own.shape
    half = rows // 2
    cells = half * cols
    tm, c = lax.axis_index("tm"), lax.axis_index("chan")
    first = tm * frames
    for f in range(frames + 2):
        a, b, g = (up, up_sib, f) if f < frames else (next_own, next_sib, f - frames)
        a = a[g, pl.ds(c * half, half + 2)].reshape(cells + 2 * cols, chans).astype(F32)
        b = b[g, pl.ds(c * half, half + 2)].reshape(cells + 2 * cols, chans).astype(F32)
        for side, v in enumerate((jnp.where(c == 0, a, b), jnp.where(c == 0, b, a))):
            before, after = shifts(v)
            for n, w in enumerate((after, v, before)):
                at = n * 2 * chans + side * chans
                spatial[f, :, :, at : at + chans] = w.astype(BF16).reshape(half + 2, cols, chans)
    total[...] = jnp.zeros_like(total)
    tables = both(c, table, table_sib)

    begin = [start_of(lengths, first + t) for t in range(frames + 2)]
    for a in range(3):
        last = frames + 2 - a
        for low, high in ((0, last // 2), (last // 2, last)):
            grads = [jnp.zeros((cells, 2 * chans), F32) for _ in range(low, high)]
            for b in range(3):
                w = weight[a * 3 + b]
                for t in range(low, high):
                    patch = spatial[t, 2 - b : 2 - b + half].reshape(cells, 6 * chans)
                    grads[t - low] = grads[t - low] + bdot(patch, w)
            for t in range(low, high):
                s = jnp.maximum(first + t - 2 + a, begin[t]) - first
                s = jnp.where(jnp.logical_and(s >= 0, s < frames), s, frames)
                total[s] += grads[t - low]
    mine = pl.ds(c * half, half)
    member = (
        clip_of(lengths, first + iota((NCLIPS, frames), 1)) == iota((NCLIPS, frames), 0)
    ).astype(F32)
    for side in range(2):
        firsts, seconds = [], []
        for t in range(frames):
            a, b = own[t, mine].astype(F32), sib[t, mine].astype(F32)
            x = jnp.where((c == 0) == (side == 0), a, b).reshape(cells, chans)
            info = tables[side]
            hat = (x - info[t + 2 : t + 3]) * info[t + 18 : t + 19]
            v = hat * info[32:33] + info[33:34]
            s = sigmoid(v)
            grad = total[t, :, side * chans : (side + 1) * chans] * s * (1.0 + v * (1.0 - s))
            total[t, :, side * chans : (side + 1) * chans] = grad
            firsts.append(jnp.sum(grad, axis=0, keepdims=True))
            seconds.append(jnp.sum(grad * hat, axis=0, keepdims=True))
        whole = jnp.concatenate(
            [
                fdot(member, jnp.concatenate(firsts, axis=0)),
                fdot(member, jnp.concatenate(seconds, axis=0)),
            ],
            axis=0,
        )
        for i in range(sums.shape[0] // 2):
            sums[2 * i + side] = whole
    for t in range(frames):
        left, right = total[t, :, :chans], total[t, :, chans:]
        keep[t] = jnp.where(c == 0, left, right)
        give[t] = jnp.where(c == 0, right, left)


def collect_body(own, *refs):
    terms, out = refs[:-1], refs[-1]
    for tap in range(own.shape[0]):
        total = own[tap]
        for term in terms:
            total = total + term[tap].astype(F32)
        out[tap] = total


def finish_body(size, bands, lengths, table, got, video, keep, other, up, out, small):
    frames, rows, cols, chans = video.shape
    half = rows // 2
    cells = half * cols
    tm, c = lax.axis_index("tm"), lax.axis_index("chan")
    first_frame = tm * frames
    whole = jnp.sum(got[...], axis=0)
    gain = table[32:33]
    small[0:1] = jnp.sum(whole[NCLIPS:], axis=0, keepdims=True)
    small[1:2] = jnp.sum(whole[:NCLIPS], axis=0, keepdims=True)
    small[2:] = jnp.zeros((6, chans), F32)
    group = group_matrix(chans, size)
    clip = iota((frames, NCLIPS), 1)
    inverse = per_clip(lengths, clip, float(rows * bands * cols * size))
    spread = jnp.where(clip_of(lengths, first_frame + iota((frames, NCLIPS), 0)) == clip, inverse, 0.0)
    first = fdot(spread, fdot(whole[:NCLIPS] * gain, group))
    second = fdot(spread, fdot(whole[NCLIPS:] * gain, group))
    for t in range(frames):
        inv = table[t + 18 : t + 19]
        for grads, at in ((keep, c * half), (other, (1 - c) * half)):
            x = video[t, pl.ds(at, half)].reshape(cells, chans).astype(F32)
            hat = (x - table[t + 2 : t + 3]) * inv
            part = inv * (grads[t] * gain - first[t : t + 1] - hat * second[t : t + 1])
            u = up[t, pl.ds(at + 1, half)].reshape(cells, chans).astype(F32)
            out[t, pl.ds(at, half)] = (u + part).astype(BF16).reshape(half, cols, chans)


def per_device(
    clip_video, norm_gain, norm_bias, conv_weight, clip_lengths, packed_frame, packed_grad
):
    frames, rows, cols, chans = clip_video.shape
    full = conv_weight.shape[3]
    peers = lax.axis_size("tm")
    bands = lax.axis_size("height")
    c = lax.axis_index("chan")
    size = full // GROUPS
    cap = max(1, frames // peers)
    block = full // (peers * bands)
    width = peers * block
    half = rows // 2
    everyone = ("tm", "height", "chan")
    devices = peers * bands * 2
    sds = jax.ShapeDtypeStruct

    skip = cap * (rows + 1) + 3
    pieces = call(
        functools.partial(pack_body, peers, cap, size),
        [
            sds((skip + (2 * rows if k == 1 else 0), cols, chans), BF16)
            for k in range(peers)
        ],
        [SM, HB, HB],
        [
            pltpu.VMEM((peers * cap, cols, chans), BF16),
            pltpu.VMEM(clip_video.shape, BF16),
            pltpu.VMEM((3, 2 * frames, chans), BF16),
            pltpu.SemaphoreType.DMA((2 * peers * cap + 2,)),
            pltpu.SemaphoreType.DMA((frames,)),
            pltpu.SemaphoreType.DMA((peers,)),
        ],
        name="pack", where=ANY,
    )(packed_frame, packed_grad, clip_video)
    ups = [[pieces[0]] + [lax.ppermute(pieces[k], "tm", ring(peers, k)) for k in range(1, peers)]]

    own = [clip_video]
    for m in range(1, bands):
        own.append(lax.ppermute(after(clip_video, pieces[0]), "height", ring(bands, m)))
    sib = [sibling(v) for v in own]
    for m in range(1, bands):
        ready = [v if k == 0 else after(v, own[m]) for k, v in enumerate(ups[0])]
        ups.append([lax.ppermute(v, "height", ring(bands, m)) for v in ready])
    prev_sib = [sibling(v[1]) for v in ups]

    weight = conv_weight.reshape(9, 3 * full, full)
    turned = call(
        turn_body, sds(weight.shape, BF16), [VM], name="turn"
    )(weight)

    up, up_first, table = call(
        functools.partial(order_body, peers, bands, cap),
        [
            sds((frames, rows + 2, cols, chans), BF16),
            sds((2, rows + 2, cols, chans), BF16),
            sds((40, chans), F32),
        ],
        [SM] + [VM] * (2 + bands * peers),
        name="order",
    )(
        clip_lengths, norm_gain[None], norm_bias[None], after(ups[0][0], turned),
        *ups[0][1:], *[v for band in ups[1:] for v in band],
    )
    table_sib = sibling(table)

    grads = call(
        functools.partial(weight_body, peers, bands, cap, block),
        [sds((27, block, chans), F32)] + [sds((27, block, chans), BF16)] * (peers - 1),
        [SM] + [VM] * (2 + 3 * bands + peers * bands),
        [
            pltpu.VMEM((3, frames + 2, bands * rows + 2, cols, width), BF16),
            pltpu.VMEM((frames, bands, chans, rows * cols), BF16),
        ],
        name="weight",
    )(
        clip_lengths, table, table_sib, *own, *sib, *prev_sib,
        *[v for band in ups for v in band],
    )
    far = bands - 1
    up_sib = sibling(up)
    next_own = lax.ppermute(up_first, "tm", [(t + 1, t) for t in range(peers - 1)])
    next_sib = sibling(next_own)
    part = sds((frames, half * cols, chans), F32)
    keep, give, sums = call(
        functools.partial(backward_body, peers),
        [part, part, sds((devices, 2 * NCLIPS, chans), F32)],
        [SM] + [VM] * 9,
        [
            pltpu.VMEM((frames + 2, half + 2, cols, 6 * chans), BF16),
            pltpu.VMEM((frames + 1, half * cols, 2 * chans), F32),
        ],
        name="backward",
    )(clip_lengths, table, table_sib, after(turned, grads[0]), clip_video, sib[0], up, up_sib, next_own, next_sib)
    totals = lax.all_to_all(sums, everyone, 0, 0)
    other = sibling(give)

    part = sds((frames, half, cols, chans), BF16)
    block_keep, block_give = call(
        functools.partial(forward_body, bands, skip),
        [part, part],
        [SM, VM, VM] + [HB] * 13,
        [
            pltpu.VMEM((frames + 2, half + 2, cols, 6 * chans), BF16),
            pltpu.VMEM((2, frames + 2, half + 2, cols, chans), BF16),
            pltpu.VMEM(weight.shape, BF16),
            pltpu.SemaphoreType.DMA((13,)),
        ],
        name="forward",
    )(
        clip_lengths, table, table_sib, after(weight, sums), own[0], sib[0], own[1], sib[1], own[far], sib[far],
        ups[0][1], prev_sib[0], ups[1][1], prev_sib[1], ups[far][1], prev_sib[far],
    )
    terms = [lax.ppermute(grads[k], "tm", ring(peers, k)) for k in range(1, peers)]
    weight_grad = call(
        collect_body, sds((27, block, chans), F32), [VM] * peers, name="collect", work=10**13
    )(after(grads[0], block_give), *terms)
    weight_grad = weight_grad.reshape(3, 3, 3, block, chans)

    video_grad, small = call(
        functools.partial(finish_body, size, bands),
        [sds(clip_video.shape, BF16), sds((8, chans), F32)],
        [SM] + [VM] * 6,
        name="finish",
    )(clip_lengths, table, after(totals, weight_grad), clip_video, keep, other, up)
    block_other = sibling(after(block_give, small))
    block_out = jnp.where(
        c == 0,
        jnp.concatenate([block_keep, block_other], axis=1),
        jnp.concatenate([block_other, block_keep], axis=1),
    )
    return (block_out, video_grad, weight_grad, small[0], small[1])


def solution(mesh):
    placed = (
        P(("groups", "tm"), "height", None, "chan"),
        P("chan"),
        P("chan"),
        P(),
        P("groups"),
        P(("groups", "tm")),
        P(("groups", "tm"), "height", None, "chan"),
    )
    return jax.shard_map(
        per_device,
        mesh=mesh,
        in_specs=placed,
        out_specs=(
            P(("groups", "tm"), "height", None, "chan"),
            P(("groups", "tm"), "height", None, "chan"),
            P("groups", None, None, ("tm", "height"), "chan"),
            P(("groups", "chan")),
            P(("groups", "chan")),
        ),
        check_vma=False,
    )
```

```python
import functools
import jax
import jax.numpy as jnp
from jax import lax
from jax.experimental import pallas as pl
from jax.experimental.pallas import tpu as pltpu
from jax.sharding import PartitionSpec as P

GROUPS = 32
NCLIPS = 8
F32 = jnp.float32
BF16 = jnp.bfloat16
HIGHEST = lax.Precision.HIGHEST
VM = pl.BlockSpec(memory_space=pltpu.VMEM)
SM = pl.BlockSpec(memory_space=pltpu.SMEM)


ANY = pl.BlockSpec(memory_space=pl.ANY)
HB = pl.BlockSpec(memory_space=pltpu.HBM)


def after(value, *others):
    return lax.optimization_barrier((value, *others))[0]


def call(body, out_shape, in_specs, scratch=(), name=None, room=20, where=VM, work=1024):
    return pl.pallas_call(
        body,
        out_shape=out_shape,
        in_specs=in_specs,
        out_specs=jax.tree.map(lambda _: where, out_shape),
        scratch_shapes=list(scratch),
        compiler_params=pltpu.CompilerParams(vmem_limit_bytes=room * 2**20),
        cost_estimate=pl.CostEstimate(flops=work, bytes_accessed=1024, transcendentals=0),
        name=name,
    )


def far_away(*values):
    return [pltpu.with_memory_space_constraint(v, pltpu.HBM) for v in values]


def fdot(a, b):
    return jnp.dot(a, b, precision=HIGHEST, preferred_element_type=F32)


def bdot(a, b):
    return jnp.dot(a, b, preferred_element_type=F32)


def ring(peers, by):
    return [(i, (i + by) % peers) for i in range(peers)]


def sibling(value):
    return lax.ppermute(value, "chan", ring(2, 1))


def sigmoid(v):
    return 1.0 / (1.0 + jnp.exp(-v))


def start_of(lengths, frame):
    begin = jnp.int32(0)
    end = jnp.int32(0)
    for k in range(NCLIPS):
        end = end + lengths[k]
        begin = jnp.where(end <= frame, end, begin)
    return begin


def clip_of(lengths, frame):
    number = jnp.zeros(frame.shape, jnp.int32)
    end = jnp.int32(0)
    for k in range(NCLIPS):
        end = end + lengths[k]
        number = number + jnp.where(end <= frame, 1, 0)
    return number


def per_clip(lengths, clip, scale):
    inverse = jnp.zeros(clip.shape, F32)
    for k in range(NCLIPS):
        length = jnp.full(clip.shape, lengths[k].astype(F32) * scale, F32)
        inverse = jnp.where(clip == k, 1.0 / length, inverse)
    return inverse


def iota(shape, dim):
    return lax.broadcasted_iota(jnp.int32, shape, dim)


def group_matrix(chans, size):
    return (iota((chans, chans), 0) // size == iota((chans, chans), 1) // size).astype(F32)


def split(value):
    parts = []
    for _ in range(3):
        part = value.astype(BF16)
        parts.append(part)
        value = value - part.astype(F32)
    return parts


def pack_body(peers, cap, size, frames, grad, video_far, *refs):
    outs = refs[:peers]
    names, video, stats, sem, far, done = refs[peers:]
    slots, rows, cols, chans = grad.shape
    cells = rows * cols
    loads = [
        pltpu.make_async_copy(video_far.at[t], video.at[t], far.at[t]) for t in range(slots)
    ]
    for load in loads:
        load.start()
    tm = lax.axis_index("tm")
    number = [frames[i] for i in range(slots)]
    step = [lax.rem(lax.div(n, slots) - tm + peers, peers) for n in number]
    rank = []
    for i in range(slots):
        r = jnp.int32(0)
        for j in range(i):
            r = r + jnp.where(step[j] == step[i], 1, 0)
        rank.append(r)
    copies = []
    for k in range(peers):
        for j in range(cap):
            at = j * (rows + 1)
            index = jnp.int32(0)
            local = jnp.int32(-1)
            for i in range(slots):
                hit = jnp.logical_and(step[i] == k, rank[i] == j)
                index = jnp.where(hit, i, index)
                local = jnp.where(hit, lax.rem(number[i], slots), local)
            n = 2 * (k * cap + j)
            names[k * cap + j] = jnp.full(grad.shape[2:], local.astype(F32), F32).astype(BF16)
            copies += [
                pltpu.make_async_copy(grad.at[index], outs[k].at[pl.ds(at, rows)], sem.at[n]),
                pltpu.make_async_copy(
                    names.at[pl.ds(k * cap + j, 1)], outs[k].at[pl.ds(at + rows, 1)], sem.at[n + 1]
                ),
            ]
            copies[-2].start()
            copies[-1].start()
    base = cap * (rows + 1)
    for i in range(2):
        copies.append(
            pltpu.make_async_copy(
                video_far.at[slots - 2 + i],
                outs[1].at[pl.ds(base + 3 + i * rows, rows)],
                sem.at[2 * peers * cap + i],
            )
        )
        copies[-1].start()
    average = group_matrix(chans, size) * (1.0 / size)
    sums = []
    for t in range(slots):
        loads[t].wait()
        sums.append(jnp.sum(video[t].astype(F32).reshape(cells, chans), axis=0, keepdims=True))
    mean = fdot(jnp.concatenate(sums, axis=0) * (1.0 / cells), average)
    squares = []
    for t in range(slots):
        apart = video[t].astype(F32).reshape(cells, chans) - mean[t : t + 1]
        squares.append(jnp.sum(apart * apart, axis=0, keepdims=True))
    var = fdot(jnp.concatenate(squares, axis=0) * (1.0 / cells), average)
    for n, part in enumerate(split(jnp.concatenate([mean, var], axis=0))):
        stats[n] = part
    for k in range(peers):
        copies.append(pltpu.make_async_copy(stats, outs[k].at[pl.ds(base, 3)], done.at[k]))
        copies[-1].start()
    for copy in copies:
        copy.wait()


def named(piece, rows, cap):
    return [
        jnp.max(piece[j * (rows + 1) + rows].astype(F32)).astype(jnp.int32) for j in range(cap)
    ]


def turn_body(weight, out):
    for i in range(9):
        for col in range(3):
            out[i, col * 256 : (col + 1) * 256] = weight[i, col * 256 : (col + 1) * 256].T


def shifts(value):
    length = value.shape[0]
    column = lax.rem(iota(value.shape, 0), 16)
    before = jnp.where(column == 0, 0.0, pltpu.roll(value, 1, 0))
    after = jnp.where(column == 15, 0.0, pltpu.roll(value, length - 1, 0))
    return before, after


def weight_body(peers, bands, cap, block, *refs):
    refs = list(refs)
    lengths, table, table_sib = [refs.pop(0) for _ in range(3)]
    take = lambda n: [refs.pop(0) for _ in range(n)]
    own, sib, prev_sib = take(bands), take(bands), take(bands)
    ups = [take(peers) for _ in range(bands)]
    outs = take(peers)
    active, upright = refs
    frames, rows, cols, chans = own[0].shape
    cells = rows * cols
    width = peers * block
    tm, h, c = lax.axis_index("tm"), lax.axis_index("height"), lax.axis_index("chan")
    first = tm * frames
    band = [lax.rem(h - m + bands, bands) for m in range(bands)]
    place = iota((chans, width), 1)
    wanted = (lax.rem(tm + lax.div(place, block), peers) * bands + h) * block + lax.rem(place, block)
    channel = iota((chans, width), 0)
    pick_own = (c * chans + channel == wanted).astype(F32)
    pick_sib = ((1 - c) * chans + channel == wanted).astype(F32)
    lookup = fdot(table[...], pick_own) + fdot(table_sib[...], pick_sib)
    pick_own, pick_sib = pick_own.astype(BF16), pick_sib.astype(BF16)
    mean, inv = lookup[:16], lookup[16:32]
    scale = inv * lookup[32:33]
    bias = lookup[33:34]
    names = [named(ups[0][k], rows, cap) for k in range(peers)]
    for col in range(3):
        active[col, :, 0] = jnp.zeros((frames + 2, cols, width), BF16)
        active[col, :, bands * rows + 1] = jnp.zeros((frames + 2, cols, width), BF16)
    for f in range(frames + 2):
        for m in range(bands):
            if f < 2:
                at = cap * (rows + 1) + 3 + f * rows
                a, b = ups[m][1][at : at + rows], prev_sib[m][at : at + rows]
            else:
                a, b = own[m][f - 2], sib[m][f - 2]
            x = bdot(a.reshape(cells, chans), pick_own) + bdot(b.reshape(cells, chans), pick_sib)
            v = (x - mean[f : f + 1]) * scale[f : f + 1] + bias
            v = v * sigmoid(v)
            before, after = shifts(v)
            at = pl.ds(band[m] * rows + 1, rows)
            for col, moved in enumerate((before, v, after)):
                active[col, f, at] = moved.astype(BF16).reshape(rows, cols, width)
    for k in range(peers):
        for j in range(cap):
            at = j * (rows + 1)
            local = names[k][j]

            @pl.when(local >= 0)
            def _():
                for m in range(bands):
                    u = ups[m][k][at : at + rows].reshape(cells, chans)
                    upright[local, m] = u.T

    begin = [start_of(lengths, first + t) for t in range(frames)]

    def taps(i, count):
        where = []
        for n in range(count):
            tap = 2 * i + n
            a = lax.div(tap, 9)
            where.append((a, lax.rem(lax.div(tap, 3), 3), lax.rem(tap, 3)))
        total = jnp.zeros((chans, count * width), F32)
        for t in range(frames):
            for m in range(bands):
                patch = []
                for a, b, col in where:
                    s = jnp.maximum(first + t - 2 + a, begin[t]) - (first - 2)
                    lines = active[col, s, pl.ds(band[m] * rows + b, rows)]
                    patch.append(lines.reshape(cells, width))
                patch = jnp.concatenate(patch, axis=1) if count > 1 else patch[0]
                total = total + bdot(upright[t, m], patch)
        for n in range(count):
            piece = total[:, n * width : (n + 1) * width].T
            for k in range(peers):
                outs[k][2 * i + n] = piece[k * block : (k + 1) * block].astype(outs[k].dtype)

    def pair(i, carry):
        taps(i, 2)
        return carry

    lax.fori_loop(0, 13, pair, 0)
    taps(jnp.int32(13), 1)


def both(c, table, table_sib):
    return (
        jnp.where(c == 0, table[...], table_sib[...]),
        jnp.where(c == 0, table_sib[...], table[...]),
    )


def forward_body(bands, skip, lengths, table, table_sib, weight_far, *refs):
    core, above, below = refs[:2], refs[2:4], refs[4:6]
    before, before_above, before_below = refs[6:8], refs[8:10], refs[10:12]
    keep, give, active, here, weight, sem = refs[12:]
    frames, rows, cols, chans = core[0].shape
    half = rows // 2
    tm, h, c = lax.axis_index("tm"), lax.axis_index("height"), lax.axis_index("chan")
    first = tm * frames
    load = pltpu.make_async_copy(weight_far, weight, sem.at[12])
    near, place = pl.ds((half - 1) * c, half + 1), pl.ds(1 - c, half + 1)
    outside = pl.ds((half + 1) * c, 1)
    waits = []
    for n in range(2):
        waits.append(
            pltpu.make_async_copy(
                core[n].at[:, near], here.at[n, pl.ds(2, frames), place], sem.at[6 * n]
            )
        )
        waits[-1].start()
        for f in range(2):
            line = skip + f * rows
            waits.append(
                pltpu.make_async_copy(
                    before[n].at[pl.ds(line + (half - 1) * c, half + 1)],
                    here.at[n, f, place],
                    sem.at[6 * n + 1 + f],
                )
            )
            waits[-1].start()
        for side, rim, rim_before, row in (
            (0, above[n], before_above[n], rows - 1),
            (1, below[n], before_below[n], 0),
        ):
            edges = [
                pltpu.make_async_copy(
                    rim.at[:, pl.ds(row, 1)],
                    here.at[n, pl.ds(2, frames), outside],
                    sem.at[6 * n + 3],
                )
            ]
            for f in range(2):
                edges.append(
                    pltpu.make_async_copy(
                        rim_before.at[pl.ds(skip + f * rows + row, 1)],
                        here.at[n, f, outside],
                        sem.at[6 * n + 4 + f],
                    )
                )

            @pl.when(c == side)
            def _():
                for edge in edges:
                    edge.start()

        waits += edges
    load.start()
    for wait in waits:
        wait.wait()
    outer = jnp.logical_or(
        jnp.logical_and(c == 0, h > 0), jnp.logical_and(c == 1, h < bands - 1)
    )
    begin = [start_of(lengths, first + t) for t in range(frames)]
    tables = both(c, table, table_sib)
    cells = (half + 2) * cols
    line = iota((cells, chans), 0)
    rim = jnp.logical_or(
        jnp.logical_and(line < cols, c == 0), jnp.logical_and(line >= cells - cols, c == 1)
    )
    ok = jnp.logical_or(jnp.logical_not(rim), outer)
    for f in range(frames + 2):
        a, b = [here[n, f].reshape(cells, chans).astype(F32) for n in range(2)]
        for side, x in enumerate((jnp.where(c == 0, a, b), jnp.where(c == 0, b, a))):
            info = tables[side]
            scale = info[16 + f : 17 + f] * info[32:33]
            v = (x - info[f : f + 1]) * scale + info[33:34]
            v = jnp.where(ok, v * sigmoid(v), 0.0)
            left, right = shifts(v)
            for n, w in enumerate((left, v, right)):
                lane = n * 2 * chans + side * chans
                active[f, :, :, lane : lane + chans] = w.astype(BF16).reshape(half + 2, cols, chans)
    load.wait()
    batch = 4
    for t0 in range(0, frames, batch):
        mixed = [jnp.zeros((half * cols, 2 * chans), F32) for _ in range(batch)]
        for a in range(3):
            for b in range(3):
                w = weight[a * 3 + b]
                for q in range(batch):
                    t = t0 + q
                    s = jnp.maximum(first + t - 2 + a, begin[t]) - (first - 2)
                    patch = active[s, b : b + half].reshape(half * cols, 6 * chans)
                    mixed[q] = mixed[q] + bdot(patch, w)
        for q in range(batch):
            t = t0 + q
            mine = slice(1, half + 1)
            left, right = mixed[q][:, :chans], mixed[q][:, chans:]
            shape = (half, cols, chans)
            for out, value, x in (
                (keep, jnp.where(c == 0, left, right), here[0, t + 2, mine]),
                (give, jnp.where(c == 0, right, left), here[1, t + 2, mine]),
            ):
                x = x.reshape(half * cols, chans).astype(F32)
                out[t] = (x + value).astype(BF16).reshape(shape)


def order_body(peers, bands, cap, lengths, gain, bias, *refs):
    pieces = [refs[m * peers : (m + 1) * peers] for m in range(bands)]
    out, first, table = refs[bands * peers :]
    own, above, below = pieces[0], pieces[1], pieces[bands - 1]
    frames = out.shape[0]
    base = cap * (out.shape[1] - 1)
    tm = lax.axis_index("tm")
    count = peers * frames

    def frame_of(index):
        slab = lax.rem(tm - lax.div(index, frames) + peers, peers)
        return slab * frames + lax.rem(index, frames)

    means, spreads = [], []
    for m in range(bands):
        stats = [
            sum(piece[base + n].astype(F32) for n in (2, 1, 0)) for piece in pieces[m]
        ]
        means.append(jnp.concatenate([v[:frames] for v in stats], axis=0))
        spreads.append(jnp.concatenate([v[frames:] for v in stats], axis=0))
    clip = clip_of(lengths, frame_of(iota((count, count), 1)))
    inverse = per_clip(lengths, clip, 1.0)
    same = jnp.where(clip_of(lengths, frame_of(iota((count, count), 0))) == clip, inverse, 0.0)
    near = jnp.clip(tm * frames - 2 + iota((16, count), 0), 0, count - 1)
    picked = jnp.where(clip_of(lengths, near) == clip[:16], inverse[:16], 0.0)
    average = sum(means[1:], means[0]) * (1.0 / bands)
    clip_mean = fdot(same, average)
    spread = jnp.zeros_like(average)
    for m in range(bands):
        apart = means[m] - clip_mean
        spread = spread + (spreads[m] + apart * apart)
    table[:16] = fdot(picked, average)
    table[16:32] = lax.rsqrt(fdot(picked, spread * (1.0 / bands)) + 1e-06)
    table[32:33] = gain[...]
    table[33:34] = bias[...]
    table[34:] = jnp.zeros((6, table.shape[1]), F32)
    rows = out.shape[1] - 2
    h = lax.axis_index("height")
    names = [named(own[k], rows, cap) for k in range(peers)]
    for k in range(peers):
        for j in range(cap):
            at = j * (rows + 1)
            local = names[k][j]

            @pl.when(local >= 0)
            def _():
                out[local, 1 : rows + 1] = own[k][at : at + rows]
                top = above[k][at + rows - 1].astype(F32)
                bottom = below[k][at].astype(F32)
                out[local, 0] = jnp.where(h > 0, top, 0.0).astype(BF16)
                out[local, rows + 1] = jnp.where(h < bands - 1, bottom, 0.0).astype(BF16)

    first[...] = out[:2]


def backward_body(peers, lengths, table, table_sib, weight, own, sib, up, up_sib, next_own, next_sib, *refs):
    keep, give, sums, spatial, total = refs
    frames, rows, cols, chans = own.shape
    half = rows // 2
    cells = half * cols
    tm, c = lax.axis_index("tm"), lax.axis_index("chan")
    first = tm * frames
    for f in range(frames + 2):
        a, b, g = (up, up_sib, f) if f < frames else (next_own, next_sib, f - frames)
        a = a[g, pl.ds(c * half, half + 2)].reshape(cells + 2 * cols, chans).astype(F32)
        b = b[g, pl.ds(c * half, half + 2)].reshape(cells + 2 * cols, chans).astype(F32)
        for side, v in enumerate((jnp.where(c == 0, a, b), jnp.where(c == 0, b, a))):
            before, after = shifts(v)
            for n, w in enumerate((after, v, before)):
                at = n * 2 * chans + side * chans
                spatial[f, :, :, at : at + chans] = w.astype(BF16).reshape(half + 2, cols, chans)
    total[...] = jnp.zeros_like(total)
    tables = both(c, table, table_sib)

    begin = [start_of(lengths, first + t) for t in range(frames + 2)]
    for a in range(3):
        last = frames + 2 - a
        for low, high in ((0, last // 2), (last // 2, last)):
            grads = [jnp.zeros((cells, 2 * chans), F32) for _ in range(low, high)]
            for b in range(3):
                w = weight[a * 3 + b]
                for t in range(low, high):
                    patch = spatial[t, 2 - b : 2 - b + half].reshape(cells, 6 * chans)
                    grads[t - low] = grads[t - low] + bdot(patch, w)
            for t in range(low, high):
                s = jnp.maximum(first + t - 2 + a, begin[t]) - first
                s = jnp.where(jnp.logical_and(s >= 0, s < frames), s, frames)
                total[s] += grads[t - low]
    mine = pl.ds(c * half, half)
    member = (
        clip_of(lengths, first + iota((NCLIPS, frames), 1)) == iota((NCLIPS, frames), 0)
    ).astype(F32)
    for side in range(2):
        firsts, seconds = [], []
        for t in range(frames):
            a, b = own[t, mine].astype(F32), sib[t, mine].astype(F32)
            x = jnp.where((c == 0) == (side == 0), a, b).reshape(cells, chans)
            info = tables[side]
            hat = (x - info[t + 2 : t + 3]) * info[t + 18 : t + 19]
            v = hat * info[32:33] + info[33:34]
            s = sigmoid(v)
            grad = total[t, :, side * chans : (side + 1) * chans] * s * (1.0 + v * (1.0 - s))
            total[t, :, side * chans : (side + 1) * chans] = grad
            firsts.append(jnp.sum(grad, axis=0, keepdims=True))
            seconds.append(jnp.sum(grad * hat, axis=0, keepdims=True))
        whole = jnp.concatenate(
            [
                fdot(member, jnp.concatenate(firsts, axis=0)),
                fdot(member, jnp.concatenate(seconds, axis=0)),
            ],
            axis=0,
        )
        for i in range(sums.shape[0] // 2):
            sums[2 * i + side] = whole
    for t in range(frames):
        left, right = total[t, :, :chans], total[t, :, chans:]
        keep[t] = jnp.where(c == 0, left, right)
        give[t] = jnp.where(c == 0, right, left)


def collect_body(*refs):
    count = len(refs) // 2 - 1
    far, out, near, sem = refs[:count], refs[count], refs[count + 1 : -1], refs[-1]
    loads = [pltpu.make_async_copy(far[n], near[n], sem.at[n]) for n in range(count)]
    for load in loads:
        load.start()
    for load in loads:
        load.wait()
    for tap in range(out.shape[0]):
        total = near[0][tap]
        for term in near[1:]:
            total = total + term[tap].astype(F32)
        out[tap] = total


def finish_body(size, bands, lengths, table, got, video, keep_far, other, up, block_keep, block_other, out, block, small, keep, sem):
    load = pltpu.make_async_copy(keep_far, keep, sem)
    load.start()
    frames, rows, cols, chans = video.shape
    half = rows // 2
    cells = half * cols
    tm, c = lax.axis_index("tm"), lax.axis_index("chan")
    first_frame = tm * frames
    whole = jnp.sum(got[...], axis=0)
    gain = table[32:33]
    small[0:1] = jnp.sum(whole[NCLIPS:], axis=0, keepdims=True)
    small[1:2] = jnp.sum(whole[:NCLIPS], axis=0, keepdims=True)
    small[2:] = jnp.zeros((6, chans), F32)
    group = group_matrix(chans, size)
    clip = iota((frames, NCLIPS), 1)
    inverse = per_clip(lengths, clip, float(rows * bands * cols * size))
    spread = jnp.where(clip_of(lengths, first_frame + iota((frames, NCLIPS), 0)) == clip, inverse, 0.0)
    first = fdot(spread, fdot(whole[:NCLIPS] * gain, group))
    second = fdot(spread, fdot(whole[NCLIPS:] * gain, group))
    load.wait()
    for t in range(frames):
        block[t, pl.ds(c * half, half)] = block_keep[t]
        block[t, pl.ds((1 - c) * half, half)] = block_other[t]
        inv = table[t + 18 : t + 19]
        for grads, at in ((keep, c * half), (other, (1 - c) * half)):
            x = video[t, pl.ds(at, half)].reshape(cells, chans).astype(F32)
            hat = (x - table[t + 2 : t + 3]) * inv
            part = inv * (grads[t] * gain - first[t : t + 1] - hat * second[t : t + 1])
            u = up[t, pl.ds(at + 1, half)].reshape(cells, chans).astype(F32)
            out[t, pl.ds(at, half)] = (u + part).astype(BF16).reshape(half, cols, chans)


def per_device(
    clip_video, norm_gain, norm_bias, conv_weight, clip_lengths, packed_frame, packed_grad
):
    frames, rows, cols, chans = clip_video.shape
    full = conv_weight.shape[3]
    peers = lax.axis_size("tm")
    bands = lax.axis_size("height")
    c = lax.axis_index("chan")
    size = full // GROUPS
    cap = max(1, frames // peers)
    block = full // (peers * bands)
    width = peers * block
    half = rows // 2
    everyone = ("tm", "height", "chan")
    devices = peers * bands * 2
    sds = jax.ShapeDtypeStruct

    skip = cap * (rows + 1) + 3
    pieces = call(
        functools.partial(pack_body, peers, cap, size),
        [
            sds((skip + (2 * rows if k == 1 else 0), cols, chans), BF16)
            for k in range(peers)
        ],
        [SM, HB, HB],
        [
            pltpu.VMEM((peers * cap, cols, chans), BF16),
            pltpu.VMEM(clip_video.shape, BF16),
            pltpu.VMEM((3, 2 * frames, chans), BF16),
            pltpu.SemaphoreType.DMA((2 * peers * cap + 2,)),
            pltpu.SemaphoreType.DMA((frames,)),
            pltpu.SemaphoreType.DMA((peers,)),
        ],
        name="pack", where=ANY,
    )(packed_frame, *far_away(packed_grad, clip_video))
    ups = [[pieces[0]] + [lax.ppermute(pieces[k], "tm", ring(peers, k)) for k in range(1, peers)]]

    own = [clip_video]
    for m in range(1, bands):
        own.append(lax.ppermute(after(clip_video, pieces[0]), "height", ring(bands, m)))
    sib = [sibling(v) for v in own]
    for m in range(1, bands):
        ready = [v if k == 0 else after(v, own[m]) for k, v in enumerate(ups[0])]
        ups.append([lax.ppermute(v, "height", ring(bands, m)) for v in ready])
    prev_sib = [sibling(v[1]) for v in ups]

    weight = conv_weight.reshape(9, 3 * full, full)
    turned = call(
        turn_body, sds(weight.shape, BF16), [VM], name="turn"
    )(weight)

    up, up_first, table = call(
        functools.partial(order_body, peers, bands, cap),
        [
            sds((frames, rows + 2, cols, chans), BF16),
            sds((2, rows + 2, cols, chans), BF16),
            sds((40, chans), F32),
        ],
        [SM] + [VM] * (2 + bands * peers),
        name="order",
    )(
        clip_lengths, norm_gain[None], norm_bias[None], after(ups[0][0], turned),
        *ups[0][1:], *[v for band in ups[1:] for v in band],
    )
    table_sib = sibling(table)

    grads = call(
        functools.partial(weight_body, peers, bands, cap, block),
        [sds((27, block, chans), F32)] + [sds((27, block, chans), BF16)] * (peers - 1),
        [SM] + [VM] * (2 + 3 * bands + peers * bands),
        [
            pltpu.VMEM((3, frames + 2, bands * rows + 2, cols, width), BF16),
            pltpu.VMEM((frames, bands, chans, rows * cols), BF16),
        ],
        name="weight",
    )(
        clip_lengths, table, table_sib, *own, *sib, *prev_sib,
        *[v for band in ups for v in band],
    )
    far = bands - 1
    up_sib = sibling(up)
    next_own = lax.ppermute(up_first, "tm", [(t + 1, t) for t in range(peers - 1)])
    next_sib = sibling(next_own)
    part = sds((frames, half * cols, chans), F32)
    keep, give, sums = call(
        functools.partial(backward_body, peers),
        [part, part, sds((devices, 2 * NCLIPS, chans), F32)],
        [SM] + [VM] * 9,
        [
            pltpu.VMEM((frames + 2, half + 2, cols, 6 * chans), BF16),
            pltpu.VMEM((frames + 1, half * cols, 2 * chans), F32),
        ],
        name="backward",
    )(clip_lengths, table, table_sib, after(turned, grads[0]), clip_video, sib[0], up, up_sib, next_own, next_sib)
    totals = lax.all_to_all(sums, everyone, 0, 0)
    other = sibling(give)

    part = sds((frames, half, cols, chans), BF16)
    block_keep, block_give = call(
        functools.partial(forward_body, bands, skip),
        [part, part],
        [SM, VM, VM] + [HB] * 13,
        [
            pltpu.VMEM((frames + 2, half + 2, cols, 6 * chans), BF16),
            pltpu.VMEM((2, frames + 2, half + 2, cols, chans), BF16),
            pltpu.VMEM(weight.shape, BF16),
            pltpu.SemaphoreType.DMA((13,)),
        ],
        name="forward",
    )(
        clip_lengths, table, table_sib, *far_away(
            after(weight, sums), own[0], sib[0], own[1], sib[1], own[far], sib[far],
            ups[0][1], prev_sib[0], ups[1][1], prev_sib[1], ups[far][1], prev_sib[far],
        ),
    )
    terms = [lax.ppermute(grads[k], "tm", ring(peers, k)) for k in range(1, peers)]
    weight_grad = call(
        collect_body, sds((27, block, chans), F32), [HB] * peers,
        [pltpu.VMEM((27, block, chans), F32)]
        + [pltpu.VMEM((27, block, chans), BF16)] * (peers - 1)
        + [pltpu.SemaphoreType.DMA((peers,))],
        name="collect", work=10**13,
    )(*far_away(after(grads[0], block_give), *terms))
    weight_grad = weight_grad.reshape(3, 3, 3, block, chans)

    block_other = sibling(after(block_give, terms[-1]))
    video_grad, block_out, small = call(
        functools.partial(finish_body, size, bands),
        [sds(clip_video.shape, BF16)] * 2 + [sds((8, chans), F32)],
        [SM] + [VM] * 3 + [HB] + [VM] * 4,
        [pltpu.VMEM((frames, half * cols, chans), F32), pltpu.SemaphoreType.DMA],
        name="finish",
    )(clip_lengths, table, after(totals, weight_grad), clip_video, *far_away(keep), other, up, block_keep, block_other)
    return (block_out, video_grad, weight_grad, small[0], small[1])


def solution(mesh):
    placed = (
        P(("groups", "tm"), "height", None, "chan"),
        P("chan"),
        P("chan"),
        P(),
        P("groups"),
        P(("groups", "tm")),
        P(("groups", "tm"), "height", None, "chan"),
    )
    return jax.shard_map(
        per_device,
        mesh=mesh,
        in_specs=placed,
        out_specs=(
            P(("groups", "tm"), "height", None, "chan"),
            P(("groups", "tm"), "height", None, "chan"),
            P("groups", None, None, ("tm", "height"), "chan"),
            P(("groups", "chan")),
            P(("groups", "chan")),
        ),
        check_vma=False,
    )
```

```python
import functools
import jax
import jax.numpy as jnp
from jax import lax
from jax.experimental import pallas as pl
from jax.experimental.pallas import tpu as pltpu
from jax.sharding import PartitionSpec as P

GROUPS = 32
NCLIPS = 8
F32 = jnp.float32
BF16 = jnp.bfloat16
HIGHEST = lax.Precision.HIGHEST
VM = pl.BlockSpec(memory_space=pltpu.VMEM)
SM = pl.BlockSpec(memory_space=pltpu.SMEM)


ANY = pl.BlockSpec(memory_space=pl.ANY)
HB = pl.BlockSpec(memory_space=pltpu.HBM)


def after(value, *others):
    return lax.optimization_barrier((value, *others))[0]


def call(body, out_shape, in_specs, scratch=(), name=None, room=20, where=VM, work=1024):
    return pl.pallas_call(
        body,
        out_shape=out_shape,
        in_specs=in_specs,
        out_specs=jax.tree.map(lambda _: where, out_shape),
        scratch_shapes=list(scratch),
        compiler_params=pltpu.CompilerParams(vmem_limit_bytes=room * 2**20),
        cost_estimate=pl.CostEstimate(flops=work, bytes_accessed=1024, transcendentals=0),
        name=name,
    )


def far_away(*values):
    return [pltpu.with_memory_space_constraint(v, pltpu.HBM) for v in values]


def fdot(a, b):
    return jnp.dot(a, b, precision=HIGHEST, preferred_element_type=F32)


def bdot(a, b):
    return jnp.dot(a, b, preferred_element_type=F32)


def ring(peers, by):
    return [(i, (i + by) % peers) for i in range(peers)]


def sibling(value):
    return lax.ppermute(value, "chan", ring(2, 1))


def sigmoid(v):
    return 1.0 / (1.0 + jnp.exp(-v))


def start_of(lengths, frame):
    begin = jnp.int32(0)
    end = jnp.int32(0)
    for k in range(NCLIPS):
        end = end + lengths[k]
        begin = jnp.where(end <= frame, end, begin)
    return begin


def clip_of(lengths, frame):
    number = jnp.zeros(frame.shape, jnp.int32)
    end = jnp.int32(0)
    for k in range(NCLIPS):
        end = end + lengths[k]
        number = number + jnp.where(end <= frame, 1, 0)
    return number


def per_clip(lengths, clip, scale):
    inverse = jnp.zeros(clip.shape, F32)
    for k in range(NCLIPS):
        length = jnp.full(clip.shape, lengths[k].astype(F32) * scale, F32)
        inverse = jnp.where(clip == k, 1.0 / length, inverse)
    return inverse


def iota(shape, dim):
    return lax.broadcasted_iota(jnp.int32, shape, dim)


def group_matrix(chans, size):
    return (iota((chans, chans), 0) // size == iota((chans, chans), 1) // size).astype(F32)


def split(value):
    parts = []
    for _ in range(3):
        part = value.astype(BF16)
        parts.append(part)
        value = value - part.astype(F32)
    return parts


def pack_body(peers, cap, size, frames, grad, video_far, *refs):
    outs = refs[:peers]
    names, video, stats, sem, far, done = refs[peers:]
    slots, rows, cols, chans = grad.shape
    cells = rows * cols
    loads = [
        pltpu.make_async_copy(video_far.at[t], video.at[t], far.at[t]) for t in range(slots)
    ]
    for load in loads:
        load.start()
    tm = lax.axis_index("tm")
    number = [frames[i] for i in range(slots)]
    step = [lax.rem(lax.div(n, slots) - tm + peers, peers) for n in number]
    rank = []
    for i in range(slots):
        r = jnp.int32(0)
        for j in range(i):
            r = r + jnp.where(step[j] == step[i], 1, 0)
        rank.append(r)
    copies = []
    for k in range(peers):
        for j in range(cap):
            at = j * (rows + 1)
            index = jnp.int32(0)
            local = jnp.int32(-1)
            for i in range(slots):
                hit = jnp.logical_and(step[i] == k, rank[i] == j)
                index = jnp.where(hit, i, index)
                local = jnp.where(hit, lax.rem(number[i], slots), local)
            n = 2 * (k * cap + j)
            names[k * cap + j] = jnp.full(grad.shape[2:], local.astype(F32), F32).astype(BF16)
            copies += [
                pltpu.make_async_copy(grad.at[index], outs[k].at[pl.ds(at, rows)], sem.at[n]),
                pltpu.make_async_copy(
                    names.at[pl.ds(k * cap + j, 1)], outs[k].at[pl.ds(at + rows, 1)], sem.at[n + 1]
                ),
            ]
            copies[-2].start()
            copies[-1].start()
    base = cap * (rows + 1)
    average = group_matrix(chans, size) * (1.0 / size)
    sums = []
    for t in range(slots):
        loads[t].wait()
        sums.append(jnp.sum(video[t].astype(F32).reshape(cells, chans), axis=0, keepdims=True))
    mean = fdot(jnp.concatenate(sums, axis=0) * (1.0 / cells), average)
    squares = []
    for t in range(slots):
        apart = video[t].astype(F32).reshape(cells, chans) - mean[t : t + 1]
        squares.append(jnp.sum(apart * apart, axis=0, keepdims=True))
    var = fdot(jnp.concatenate(squares, axis=0) * (1.0 / cells), average)
    for n, part in enumerate(split(jnp.concatenate([mean, var], axis=0))):
        stats[n] = part
    for k in range(peers):
        copies.append(pltpu.make_async_copy(stats, outs[k].at[pl.ds(base, 3)], done.at[k]))
        copies[-1].start()
    for copy in copies:
        copy.wait()


def named(piece, rows, cap):
    return [
        jnp.max(piece[j * (rows + 1) + rows].astype(F32)).astype(jnp.int32) for j in range(cap)
    ]


def turn_body(weight, out):
    for i in range(9):
        for col in range(3):
            out[i, col * 256 : (col + 1) * 256] = weight[i, col * 256 : (col + 1) * 256].T


def shifts(value):
    length = value.shape[0]
    column = lax.rem(iota(value.shape, 0), 16)
    before = jnp.where(column == 0, 0.0, pltpu.roll(value, 1, 0))
    after = jnp.where(column == 15, 0.0, pltpu.roll(value, length - 1, 0))
    return before, after


def weight_body(peers, bands, cap, block, *refs):
    refs = list(refs)
    lengths, table, table_sib = [refs.pop(0) for _ in range(3)]
    take = lambda n: [refs.pop(0) for _ in range(n)]
    own, sib = take(bands), take(bands)
    prev, prev_sib = take(2)
    ups = [take(peers) for _ in range(bands)]
    outs = take(peers)
    active, upright = refs
    frames, rows, cols, chans = own[0].shape
    cells = rows * cols
    width = peers * block
    tm, h, c = lax.axis_index("tm"), lax.axis_index("height"), lax.axis_index("chan")
    first = tm * frames
    band = [lax.rem(h - m + bands, bands) for m in range(bands)]
    place = iota((chans, width), 1)
    wanted = (lax.rem(tm + lax.div(place, block), peers) * bands + h) * block + lax.rem(place, block)
    channel = iota((chans, width), 0)
    pick_own = (c * chans + channel == wanted).astype(F32)
    pick_sib = ((1 - c) * chans + channel == wanted).astype(F32)
    lookup = fdot(table[...], pick_own) + fdot(table_sib[...], pick_sib)
    pick_own, pick_sib = pick_own.astype(BF16), pick_sib.astype(BF16)
    mean, inv = lookup[:16], lookup[16:32]
    scale = inv * lookup[32:33]
    bias = lookup[33:34]
    names = [named(ups[0][k], rows, cap) for k in range(peers)]
    for col in range(3):
        active[col, :, 0] = jnp.zeros((frames + 2, cols, width), BF16)
        active[col, :, bands * rows + 1] = jnp.zeros((frames + 2, cols, width), BF16)
    for f in range(frames + 2):
        for m in range(bands):
            if f < 2:
                at = (2 * m + f) * rows
                a, b = prev[at : at + rows], prev_sib[at : at + rows]
            else:
                a, b = own[m][f - 2], sib[m][f - 2]
            x = bdot(a.reshape(cells, chans), pick_own) + bdot(b.reshape(cells, chans), pick_sib)
            v = (x - mean[f : f + 1]) * scale[f : f + 1] + bias
            v = v * sigmoid(v)
            before, after = shifts(v)
            at = pl.ds(band[m] * rows + 1, rows)
            for col, moved in enumerate((before, v, after)):
                active[col, f, at] = moved.astype(BF16).reshape(rows, cols, width)
    for k in range(peers):
        for j in range(cap):
            at = j * (rows + 1)
            local = names[k][j]

            @pl.when(local >= 0)
            def _():
                for m in range(bands):
                    u = ups[m][k][at : at + rows].reshape(cells, chans)
                    upright[local, m] = u.T

    begin = [start_of(lengths, first + t) for t in range(frames)]

    def taps(i, count):
        where = []
        for n in range(count):
            tap = 2 * i + n
            a = lax.div(tap, 9)
            where.append((a, lax.rem(lax.div(tap, 3), 3), lax.rem(tap, 3)))
        total = jnp.zeros((chans, count * width), F32)
        for t in range(frames):
            for m in range(bands):
                patch = []
                for a, b, col in where:
                    s = jnp.maximum(first + t - 2 + a, begin[t]) - (first - 2)
                    lines = active[col, s, pl.ds(band[m] * rows + b, rows)]
                    patch.append(lines.reshape(cells, width))
                patch = jnp.concatenate(patch, axis=1) if count > 1 else patch[0]
                total = total + bdot(upright[t, m], patch)
        for n in range(count):
            piece = total[:, n * width : (n + 1) * width].T
            for k in range(peers):
                outs[k][2 * i + n] = piece[k * block : (k + 1) * block].astype(outs[k].dtype)

    def pair(i, carry):
        taps(i, 2)
        return carry

    lax.fori_loop(0, 13, pair, 0)
    taps(jnp.int32(13), 1)


def both(c, table, table_sib):
    return (
        jnp.where(c == 0, table[...], table_sib[...]),
        jnp.where(c == 0, table_sib[...], table[...]),
    )


def forward_body(bands, lengths, table, table_sib, weight_far, *refs):
    core, above, below = refs[:2], refs[2:4], refs[4:6]
    before = refs[6:8]
    keep, give, active, here, weight, sem = refs[8:]
    frames, rows, cols, chans = core[0].shape
    half = rows // 2
    tm, h, c = lax.axis_index("tm"), lax.axis_index("height"), lax.axis_index("chan")
    first = tm * frames
    load = pltpu.make_async_copy(weight_far, weight, sem.at[12])
    near, place = pl.ds((half - 1) * c, half + 1), pl.ds(1 - c, half + 1)
    outside = pl.ds((half + 1) * c, 1)
    waits = []
    for n in range(2):
        waits.append(
            pltpu.make_async_copy(
                core[n].at[:, near], here.at[n, pl.ds(2, frames), place], sem.at[6 * n]
            )
        )
        waits[-1].start()
        for f in range(2):
            line = f * rows
            waits.append(
                pltpu.make_async_copy(
                    before[n].at[pl.ds(line + (half - 1) * c, half + 1)],
                    here.at[n, f, place],
                    sem.at[6 * n + 1 + f],
                )
            )
            waits[-1].start()
        for side, rim, row, line in (
            (0, above[n], rows - 1, 2 * rows),
            (1, below[n], 0, 2 * (bands - 1) * rows),
        ):
            edges = [
                pltpu.make_async_copy(
                    rim.at[:, pl.ds(row, 1)],
                    here.at[n, pl.ds(2, frames), outside],
                    sem.at[6 * n + 3],
                )
            ]
            for f in range(2):
                edges.append(
                    pltpu.make_async_copy(
                        before[n].at[pl.ds(line + f * rows + row, 1)],
                        here.at[n, f, outside],
                        sem.at[6 * n + 4 + f],
                    )
                )

            @pl.when(c == side)
            def _():
                for edge in edges:
                    edge.start()

        waits += edges
    load.start()
    for wait in waits:
        wait.wait()
    outer = jnp.logical_or(
        jnp.logical_and(c == 0, h > 0), jnp.logical_and(c == 1, h < bands - 1)
    )
    begin = [start_of(lengths, first + t) for t in range(frames)]
    tables = both(c, table, table_sib)
    cells = (half + 2) * cols
    line = iota((cells, chans), 0)
    rim = jnp.logical_or(
        jnp.logical_and(line < cols, c == 0), jnp.logical_and(line >= cells - cols, c == 1)
    )
    ok = jnp.logical_or(jnp.logical_not(rim), outer)
    for f in range(frames + 2):
        a, b = [here[n, f].reshape(cells, chans).astype(F32) for n in range(2)]
        for side, x in enumerate((jnp.where(c == 0, a, b), jnp.where(c == 0, b, a))):
            info = tables[side]
            scale = info[16 + f : 17 + f] * info[32:33]
            v = (x - info[f : f + 1]) * scale + info[33:34]
            v = jnp.where(ok, v * sigmoid(v), 0.0)
            left, right = shifts(v)
            for n, w in enumerate((left, v, right)):
                lane = n * 2 * chans + side * chans
                active[f, :, :, lane : lane + chans] = w.astype(BF16).reshape(half + 2, cols, chans)
    load.wait()
    batch = 4
    for t0 in range(0, frames, batch):
        mixed = [jnp.zeros((half * cols, 2 * chans), F32) for _ in range(batch)]
        for a in range(3):
            for b in range(3):
                w = weight[a * 3 + b]
                for q in range(batch):
                    t = t0 + q
                    s = jnp.maximum(first + t - 2 + a, begin[t]) - (first - 2)
                    patch = active[s, b : b + half].reshape(half * cols, 6 * chans)
                    mixed[q] = mixed[q] + bdot(patch, w)
        for q in range(batch):
            t = t0 + q
            mine = slice(1, half + 1)
            left, right = mixed[q][:, :chans], mixed[q][:, chans:]
            shape = (half, cols, chans)
            for out, value, x in (
                (keep, jnp.where(c == 0, left, right), here[0, t + 2, mine]),
                (give, jnp.where(c == 0, right, left), here[1, t + 2, mine]),
            ):
                x = x.reshape(half * cols, chans).astype(F32)
                out[t] = (x + value).astype(BF16).reshape(shape)


def order_body(peers, bands, cap, lengths, gain, bias, *refs):
    pieces = [refs[m * peers : (m + 1) * peers] for m in range(bands)]
    out, first, table = refs[bands * peers :]
    own, above, below = pieces[0], pieces[1], pieces[bands - 1]
    frames = out.shape[0]
    base = cap * (out.shape[1] - 1)
    tm = lax.axis_index("tm")
    count = peers * frames

    def frame_of(index):
        slab = lax.rem(tm - lax.div(index, frames) + peers, peers)
        return slab * frames + lax.rem(index, frames)

    means, spreads = [], []
    for m in range(bands):
        stats = [
            sum(piece[base + n].astype(F32) for n in (2, 1, 0)) for piece in pieces[m]
        ]
        means.append(jnp.concatenate([v[:frames] for v in stats], axis=0))
        spreads.append(jnp.concatenate([v[frames:] for v in stats], axis=0))
    clip = clip_of(lengths, frame_of(iota((count, count), 1)))
    inverse = per_clip(lengths, clip, 1.0)
    same = jnp.where(clip_of(lengths, frame_of(iota((count, count), 0))) == clip, inverse, 0.0)
    near = jnp.clip(tm * frames - 2 + iota((16, count), 0), 0, count - 1)
    picked = jnp.where(clip_of(lengths, near) == clip[:16], inverse[:16], 0.0)
    average = sum(means[1:], means[0]) * (1.0 / bands)
    clip_mean = fdot(same, average)
    spread = jnp.zeros_like(average)
    for m in range(bands):
        apart = means[m] - clip_mean
        spread = spread + (spreads[m] + apart * apart)
    table[:16] = fdot(picked, average)
    table[16:32] = lax.rsqrt(fdot(picked, spread * (1.0 / bands)) + 1e-06)
    table[32:33] = gain[...]
    table[33:34] = bias[...]
    table[34:] = jnp.zeros((6, table.shape[1]), F32)
    rows = out.shape[1] - 2
    h = lax.axis_index("height")
    names = [named(own[k], rows, cap) for k in range(peers)]
    for k in range(peers):
        for j in range(cap):
            at = j * (rows + 1)
            local = names[k][j]

            @pl.when(local >= 0)
            def _():
                out[local, 1 : rows + 1] = own[k][at : at + rows]
                top = above[k][at + rows - 1].astype(F32)
                bottom = below[k][at].astype(F32)
                out[local, 0] = jnp.where(h > 0, top, 0.0).astype(BF16)
                out[local, rows + 1] = jnp.where(h < bands - 1, bottom, 0.0).astype(BF16)

    first[...] = out[:2]


def backward_body(peers, lengths, table, table_sib, weight, own, sib, up, up_sib, next_own, next_sib, *refs):
    keep, give, sums, spatial, total = refs
    frames, rows, cols, chans = own.shape
    half = rows // 2
    cells = half * cols
    tm, c = lax.axis_index("tm"), lax.axis_index("chan")
    first = tm * frames
    for f in range(frames + 2):
        a, b, g = (up, up_sib, f) if f < frames else (next_own, next_sib, f - frames)
        a = a[g, pl.ds(c * half, half + 2)].reshape(cells + 2 * cols, chans).astype(F32)
        b = b[g, pl.ds(c * half, half + 2)].reshape(cells + 2 * cols, chans).astype(F32)
        for side, v in enumerate((jnp.where(c == 0, a, b), jnp.where(c == 0, b, a))):
            before, after = shifts(v)
            for n, w in enumerate((after, v, before)):
                at = n * 2 * chans + side * chans
                spatial[f, :, :, at : at + chans] = w.astype(BF16).reshape(half + 2, cols, chans)
    total[...] = jnp.zeros_like(total)
    tables = both(c, table, table_sib)

    begin = [start_of(lengths, first + t) for t in range(frames + 2)]
    for a in range(3):
        last = frames + 2 - a
        for low, high in ((0, last // 2), (last // 2, last)):
            grads = [jnp.zeros((cells, 2 * chans), F32) for _ in range(low, high)]
            for b in range(3):
                w = weight[a * 3 + b]
                for t in range(low, high):
                    patch = spatial[t, 2 - b : 2 - b + half].reshape(cells, 6 * chans)
                    grads[t - low] = grads[t - low] + bdot(patch, w)
            for t in range(low, high):
                s = jnp.maximum(first + t - 2 + a, begin[t]) - first
                s = jnp.where(jnp.logical_and(s >= 0, s < frames), s, frames)
                total[s] += grads[t - low]
    mine = pl.ds(c * half, half)
    member = (
        clip_of(lengths, first + iota((NCLIPS, frames), 1)) == iota((NCLIPS, frames), 0)
    ).astype(F32)
    for side in range(2):
        firsts, seconds = [], []
        for t in range(frames):
            a, b = own[t, mine].astype(F32), sib[t, mine].astype(F32)
            x = jnp.where((c == 0) == (side == 0), a, b).reshape(cells, chans)
            info = tables[side]
            hat = (x - info[t + 2 : t + 3]) * info[t + 18 : t + 19]
            v = hat * info[32:33] + info[33:34]
            s = sigmoid(v)
            grad = total[t, :, side * chans : (side + 1) * chans] * s * (1.0 + v * (1.0 - s))
            total[t, :, side * chans : (side + 1) * chans] = grad
            firsts.append(jnp.sum(grad, axis=0, keepdims=True))
            seconds.append(jnp.sum(grad * hat, axis=0, keepdims=True))
        whole = jnp.concatenate(
            [
                fdot(member, jnp.concatenate(firsts, axis=0)),
                fdot(member, jnp.concatenate(seconds, axis=0)),
            ],
            axis=0,
        )
        for i in range(sums.shape[0] // 2):
            sums[2 * i + side] = whole
    for t in range(frames):
        left, right = total[t, :, :chans], total[t, :, chans:]
        keep[t] = jnp.where(c == 0, left, right)
        give[t] = jnp.where(c == 0, right, left)


def collect_body(*refs):
    count = len(refs) // 2 - 1
    far, out, near, sem = refs[:count], refs[count], refs[count + 1 : -1], refs[-1]
    loads = [pltpu.make_async_copy(far[n], near[n], sem.at[n]) for n in range(count)]
    for load in loads:
        load.start()
    for load in loads:
        load.wait()
    for tap in range(out.shape[0]):
        total = near[0][tap]
        for term in near[1:]:
            total = total + term[tap].astype(F32)
        out[tap] = total


def finish_body(size, bands, lengths, table, got, video, keep_far, other, up, block_keep, block_other, out, block, small, keep, sem):
    load = pltpu.make_async_copy(keep_far, keep, sem)
    load.start()
    frames, rows, cols, chans = video.shape
    half = rows // 2
    cells = half * cols
    tm, c = lax.axis_index("tm"), lax.axis_index("chan")
    first_frame = tm * frames
    whole = jnp.sum(got[...], axis=0)
    gain = table[32:33]
    small[0:1] = jnp.sum(whole[NCLIPS:], axis=0, keepdims=True)
    small[1:2] = jnp.sum(whole[:NCLIPS], axis=0, keepdims=True)
    small[2:] = jnp.zeros((6, chans), F32)
    group = group_matrix(chans, size)
    clip = iota((frames, NCLIPS), 1)
    inverse = per_clip(lengths, clip, float(rows * bands * cols * size))
    spread = jnp.where(clip_of(lengths, first_frame + iota((frames, NCLIPS), 0)) == clip, inverse, 0.0)
    first = fdot(spread, fdot(whole[:NCLIPS] * gain, group))
    second = fdot(spread, fdot(whole[NCLIPS:] * gain, group))
    load.wait()
    for t in range(frames):
        block[t, pl.ds(c * half, half)] = block_keep[t]
        block[t, pl.ds((1 - c) * half, half)] = block_other[t]
        inv = table[t + 18 : t + 19]
        for grads, at in ((keep, c * half), (other, (1 - c) * half)):
            x = video[t, pl.ds(at, half)].reshape(cells, chans).astype(F32)
            hat = (x - table[t + 2 : t + 3]) * inv
            part = inv * (grads[t] * gain - first[t : t + 1] - hat * second[t : t + 1])
            u = up[t, pl.ds(at + 1, half)].reshape(cells, chans).astype(F32)
            out[t, pl.ds(at, half)] = (u + part).astype(BF16).reshape(half, cols, chans)


def per_device(
    clip_video, norm_gain, norm_bias, conv_weight, clip_lengths, packed_frame, packed_grad
):
    frames, rows, cols, chans = clip_video.shape
    full = conv_weight.shape[3]
    peers = lax.axis_size("tm")
    bands = lax.axis_size("height")
    c = lax.axis_index("chan")
    size = full // GROUPS
    cap = max(1, frames // peers)
    block = full // (peers * bands)
    width = peers * block
    half = rows // 2
    everyone = ("tm", "height", "chan")
    devices = peers * bands * 2
    sds = jax.ShapeDtypeStruct

    pieces = call(
        functools.partial(pack_body, peers, cap, size),
        [sds((cap * (rows + 1) + 3, cols, chans), BF16)] * peers,
        [SM, HB, HB],
        [
            pltpu.VMEM((peers * cap, cols, chans), BF16),
            pltpu.VMEM(clip_video.shape, BF16),
            pltpu.VMEM((3, 2 * frames, chans), BF16),
            pltpu.SemaphoreType.DMA((2 * peers * cap,)),
            pltpu.SemaphoreType.DMA((frames,)),
            pltpu.SemaphoreType.DMA((peers,)),
        ],
        name="pack", where=ANY,
    )(packed_frame, *far_away(packed_grad, clip_video))
    ups = [[pieces[0]] + [lax.ppermute(pieces[k], "tm", ring(peers, k)) for k in range(1, peers)]]

    own = [clip_video]
    for m in range(1, bands):
        own.append(lax.ppermute(after(clip_video, pieces[0]), "height", ring(bands, m)))
    sib = [sibling(v) for v in own]
    for m in range(1, bands):
        ready = [v for k, v in enumerate(ups[0])]
        ups.append([lax.ppermute(v, "height", ring(bands, m)) for v in ready])
    prev = jnp.concatenate([v[frames - 2 :] for v in own], axis=0)
    prev = prev.reshape(2 * bands * rows, cols, chans)
    prev = lax.ppermute(prev, "tm", [(t, t + 1) for t in range(peers - 1)])
    prev_sib = sibling(prev)

    weight = conv_weight.reshape(9, 3 * full, full)
    turned = call(
        turn_body, sds(weight.shape, BF16), [VM], name="turn"
    )(weight)

    up, up_first, table = call(
        functools.partial(order_body, peers, bands, cap),
        [
            sds((frames, rows + 2, cols, chans), BF16),
            sds((2, rows + 2, cols, chans), BF16),
            sds((40, chans), F32),
        ],
        [SM] + [VM] * (2 + bands * peers),
        name="order",
    )(
        clip_lengths, norm_gain[None], norm_bias[None], after(ups[0][0], turned),
        *ups[0][1:], *[v for band in ups[1:] for v in band],
    )
    table_sib = sibling(table)

    grads = call(
        functools.partial(weight_body, peers, bands, cap, block),
        [sds((27, block, chans), F32)] + [sds((27, block, chans), BF16)] * (peers - 1),
        [SM] + [VM] * (4 + 2 * bands + peers * bands),
        [
            pltpu.VMEM((3, frames + 2, bands * rows + 2, cols, width), BF16),
            pltpu.VMEM((frames, bands, chans, rows * cols), BF16),
        ],
        name="weight",
    )(
        clip_lengths, table, table_sib, *own, *sib, prev, prev_sib,
        *[v for band in ups for v in band],
    )
    far = bands - 1
    up_sib = sibling(up)
    next_own = lax.ppermute(up_first, "tm", [(t + 1, t) for t in range(peers - 1)])
    next_sib = sibling(next_own)
    part = sds((frames, half * cols, chans), F32)
    keep, give, sums = call(
        functools.partial(backward_body, peers),
        [part, part, sds((devices, 2 * NCLIPS, chans), F32)],
        [SM] + [VM] * 9,
        [
            pltpu.VMEM((frames + 2, half + 2, cols, 6 * chans), BF16),
            pltpu.VMEM((frames + 1, half * cols, 2 * chans), F32),
        ],
        name="backward",
    )(clip_lengths, table, table_sib, after(turned, grads[0]), clip_video, sib[0], up, up_sib, next_own, next_sib)
    totals = lax.all_to_all(sums, everyone, 0, 0)
    other = sibling(give)

    part = sds((frames, half, cols, chans), BF16)
    block_keep, block_give = call(
        functools.partial(forward_body, bands),
        [part, part],
        [SM, VM, VM] + [HB] * 9,
        [
            pltpu.VMEM((frames + 2, half + 2, cols, 6 * chans), BF16),
            pltpu.VMEM((2, frames + 2, half + 2, cols, chans), BF16),
            pltpu.VMEM(weight.shape, BF16),
            pltpu.SemaphoreType.DMA((13,)),
        ],
        name="forward",
    )(
        clip_lengths, table, table_sib, *far_away(
            after(weight, sums), own[0], sib[0], own[1], sib[1], own[far], sib[far],
            prev, prev_sib,
        ),
    )
    terms = [lax.ppermute(grads[k], "tm", ring(peers, k)) for k in range(1, peers)]
    weight_grad = call(
        collect_body, sds((27, block, chans), F32), [HB] * peers,
        [pltpu.VMEM((27, block, chans), F32)]
        + [pltpu.VMEM((27, block, chans), BF16)] * (peers - 1)
        + [pltpu.SemaphoreType.DMA((peers,))],
        name="collect", work=10**13,
    )(*far_away(after(grads[0], block_give), *terms))
    weight_grad = weight_grad.reshape(3, 3, 3, block, chans)

    block_other = sibling(after(block_give, terms[-1]))
    video_grad, block_out, small = call(
        functools.partial(finish_body, size, bands),
        [sds(clip_video.shape, BF16)] * 2 + [sds((8, chans), F32)],
        [SM] + [VM] * 3 + [HB] + [VM] * 4,
        [pltpu.VMEM((frames, half * cols, chans), F32), pltpu.SemaphoreType.DMA],
        name="finish",
    )(clip_lengths, table, after(totals, weight_grad), clip_video, *far_away(keep), other, up, block_keep, block_other)
    return (block_out, video_grad, weight_grad, small[0], small[1])


def solution(mesh):
    placed = (
        P(("groups", "tm"), "height", None, "chan"),
        P("chan"),
        P("chan"),
        P(),
        P("groups"),
        P(("groups", "tm")),
        P(("groups", "tm"), "height", None, "chan"),
    )
    return jax.shard_map(
        per_device,
        mesh=mesh,
        in_specs=placed,
        out_specs=(
            P(("groups", "tm"), "height", None, "chan"),
            P(("groups", "tm"), "height", None, "chan"),
            P("groups", None, None, ("tm", "height"), "chan"),
            P(("groups", "chan")),
            P(("groups", "chan")),
        ),
        check_vma=False,
    )
```

```python
import functools
import jax
import jax.numpy as jnp
from jax import lax
from jax.experimental import pallas as pl
from jax.experimental.pallas import tpu as pltpu
from jax.sharding import PartitionSpec as P

GROUPS = 32
NCLIPS = 8
F32 = jnp.float32
BF16 = jnp.bfloat16
HIGHEST = lax.Precision.HIGHEST
VM = pl.BlockSpec(memory_space=pltpu.VMEM)
SM = pl.BlockSpec(memory_space=pltpu.SMEM)


ANY = pl.BlockSpec(memory_space=pl.ANY)
HB = pl.BlockSpec(memory_space=pltpu.HBM)


def after(value, *others):
    return lax.optimization_barrier((value, *others))[0]


def call(body, out_shape, in_specs, scratch=(), name=None, room=20, where=VM, work=1024):
    return pl.pallas_call(
        body,
        out_shape=out_shape,
        in_specs=in_specs,
        out_specs=where if isinstance(where, list) else jax.tree.map(lambda _: where, out_shape),
        scratch_shapes=list(scratch),
        compiler_params=pltpu.CompilerParams(vmem_limit_bytes=room * 2**20),
        cost_estimate=pl.CostEstimate(flops=work, bytes_accessed=1024, transcendentals=0),
        name=name,
    )


def far_away(*values):
    return [pltpu.with_memory_space_constraint(v, pltpu.HBM) for v in values]


def fdot(a, b):
    return jnp.dot(a, b, precision=HIGHEST, preferred_element_type=F32)


def bdot(a, b):
    return jnp.dot(a, b, preferred_element_type=F32)


def ring(peers, by):
    return [(i, (i + by) % peers) for i in range(peers)]


def sibling(value):
    return lax.ppermute(value, "chan", ring(2, 1))


def sigmoid(v):
    return 1.0 / (1.0 + jnp.exp(-v))


def start_of(lengths, frame):
    begin = jnp.int32(0)
    end = jnp.int32(0)
    for k in range(NCLIPS):
        end = end + lengths[k]
        begin = jnp.where(end <= frame, end, begin)
    return begin


def clip_of(lengths, frame):
    number = jnp.zeros(frame.shape, jnp.int32)
    end = jnp.int32(0)
    for k in range(NCLIPS):
        end = end + lengths[k]
        number = number + jnp.where(end <= frame, 1, 0)
    return number


def per_clip(lengths, clip, scale):
    inverse = jnp.zeros(clip.shape, F32)
    for k in range(NCLIPS):
        length = jnp.full(clip.shape, lengths[k].astype(F32) * scale, F32)
        inverse = jnp.where(clip == k, 1.0 / length, inverse)
    return inverse


def iota(shape, dim):
    return lax.broadcasted_iota(jnp.int32, shape, dim)


def group_matrix(chans, size):
    return (iota((chans, chans), 0) // size == iota((chans, chans), 1) // size).astype(F32)


def split(value):
    parts = []
    for _ in range(3):
        part = value.astype(BF16)
        parts.append(part)
        value = value - part.astype(F32)
    return parts


def pack_body(peers, cap, size, frames, grad, video_far, *refs):
    outs = refs[:peers]
    names, video, stats, sem, far, done = refs[peers:]
    slots, rows, cols, chans = grad.shape
    cells = rows * cols
    loads = [
        pltpu.make_async_copy(video_far.at[t], video.at[t], far.at[t]) for t in range(slots)
    ]
    for load in loads:
        load.start()
    tm = lax.axis_index("tm")
    number = [frames[i] for i in range(slots)]
    step = [lax.rem(lax.div(n, slots) - tm + peers, peers) for n in number]
    rank = []
    for i in range(slots):
        r = jnp.int32(0)
        for j in range(i):
            r = r + jnp.where(step[j] == step[i], 1, 0)
        rank.append(r)
    copies = []
    for k in range(peers):
        for j in range(cap):
            at = j * (rows + 1)
            index = jnp.int32(0)
            local = jnp.int32(-1)
            for i in range(slots):
                hit = jnp.logical_and(step[i] == k, rank[i] == j)
                index = jnp.where(hit, i, index)
                local = jnp.where(hit, lax.rem(number[i], slots), local)
            n = 2 * (k * cap + j)
            names[k * cap + j] = jnp.full(grad.shape[2:], local.astype(F32), F32).astype(BF16)
            copies += [
                pltpu.make_async_copy(grad.at[index], outs[k].at[pl.ds(at, rows)], sem.at[n]),
                pltpu.make_async_copy(
                    names.at[pl.ds(k * cap + j, 1)], outs[k].at[pl.ds(at + rows, 1)], sem.at[n + 1]
                ),
            ]
            copies[-2].start()
            copies[-1].start()
    base = cap * (rows + 1)
    average = group_matrix(chans, size) * (1.0 / size)
    sums = []
    for t in range(slots):
        loads[t].wait()
        sums.append(jnp.sum(video[t].astype(F32).reshape(cells, chans), axis=0, keepdims=True))
    mean = fdot(jnp.concatenate(sums, axis=0) * (1.0 / cells), average)
    squares = []
    for t in range(slots):
        apart = video[t].astype(F32).reshape(cells, chans) - mean[t : t + 1]
        squares.append(jnp.sum(apart * apart, axis=0, keepdims=True))
    var = fdot(jnp.concatenate(squares, axis=0) * (1.0 / cells), average)
    for n, part in enumerate(split(jnp.concatenate([mean, var], axis=0))):
        stats[n] = part
    for k in range(peers):
        copies.append(pltpu.make_async_copy(stats, outs[k].at[pl.ds(base, 3)], done.at[k]))
        copies[-1].start()
    for copy in copies:
        copy.wait()


def named(piece, rows, cap):
    return [
        jnp.max(piece[j * (rows + 1) + rows].astype(F32)).astype(jnp.int32) for j in range(cap)
    ]


def turn_body(weight, out):
    for i in range(9):
        for col in range(3):
            out[i, col * 256 : (col + 1) * 256] = weight[i, col * 256 : (col + 1) * 256].T


def shifts(value):
    length = value.shape[0]
    column = lax.rem(iota(value.shape, 0), 16)
    before = jnp.where(column == 0, 0.0, pltpu.roll(value, 1, 0))
    after = jnp.where(column == 15, 0.0, pltpu.roll(value, length - 1, 0))
    return before, after


def weight_body(peers, bands, cap, block, *refs):
    refs = list(refs)
    lengths, table, table_sib = [refs.pop(0) for _ in range(3)]
    take = lambda n: [refs.pop(0) for _ in range(n)]
    own, sib = take(bands), take(bands)
    prev, prev_sib = take(2)
    ups = [take(peers) for _ in range(bands)]
    outs = take(peers)
    active, upright = refs
    frames, rows, cols, chans = own[0].shape
    cells = rows * cols
    width = peers * block
    tm, h, c = lax.axis_index("tm"), lax.axis_index("height"), lax.axis_index("chan")
    first = tm * frames
    band = [lax.rem(h - m + bands, bands) for m in range(bands)]
    place = iota((chans, width), 1)
    wanted = (lax.rem(tm + lax.div(place, block), peers) * bands + h) * block + lax.rem(place, block)
    channel = iota((chans, width), 0)
    pick_own = (c * chans + channel == wanted).astype(F32)
    pick_sib = ((1 - c) * chans + channel == wanted).astype(F32)
    lookup = fdot(table[...], pick_own) + fdot(table_sib[...], pick_sib)
    pick_own, pick_sib = pick_own.astype(BF16), pick_sib.astype(BF16)
    mean, inv = lookup[:16], lookup[16:32]
    scale = inv * lookup[32:33]
    bias = lookup[33:34]
    names = [named(ups[0][k], rows, cap) for k in range(peers)]
    for col in range(3):
        active[col, :, 0] = jnp.zeros((frames + 2, cols, width), BF16)
        active[col, :, bands * rows + 1] = jnp.zeros((frames + 2, cols, width), BF16)
    for f in range(frames + 2):
        for m in range(bands):
            if f < 2:
                at = (2 * m + f) * rows
                a, b = prev[at : at + rows], prev_sib[at : at + rows]
            else:
                a, b = own[m][f - 2], sib[m][f - 2]
            x = bdot(a.reshape(cells, chans), pick_own) + bdot(b.reshape(cells, chans), pick_sib)
            v = (x - mean[f : f + 1]) * scale[f : f + 1] + bias
            v = v * sigmoid(v)
            before, after = shifts(v)
            at = pl.ds(band[m] * rows + 1, rows)
            for col, moved in enumerate((before, v, after)):
                active[col, f, at] = moved.astype(BF16).reshape(rows, cols, width)
    for k in range(peers):
        for j in range(cap):
            at = j * (rows + 1)
            local = names[k][j]

            @pl.when(local >= 0)
            def _():
                for m in range(bands):
                    u = ups[m][k][at : at + rows].reshape(cells, chans)
                    upright[local, m] = u.T

    begin = [start_of(lengths, first + t) for t in range(frames)]

    def taps(i, count):
        where = []
        for n in range(count):
            tap = 2 * i + n
            a = lax.div(tap, 9)
            where.append((a, lax.rem(lax.div(tap, 3), 3), lax.rem(tap, 3)))
        total = jnp.zeros((chans, count * width), F32)
        for t in range(frames):
            for m in range(bands):
                patch = []
                for a, b, col in where:
                    s = jnp.maximum(first + t - 2 + a, begin[t]) - (first - 2)
                    lines = active[col, s, pl.ds(band[m] * rows + b, rows)]
                    patch.append(lines.reshape(cells, width))
                patch = jnp.concatenate(patch, axis=1) if count > 1 else patch[0]
                total = total + bdot(upright[t, m], patch)
        for n in range(count):
            piece = total[:, n * width : (n + 1) * width].T
            for k in range(peers):
                outs[k][2 * i + n] = piece[k * block : (k + 1) * block].astype(outs[k].dtype)

    def pair(i, carry):
        taps(i, 2)
        return carry

    lax.fori_loop(0, 13, pair, 0)
    taps(jnp.int32(13), 1)


def both(c, table, table_sib):
    return (
        jnp.where(c == 0, table[...], table_sib[...]),
        jnp.where(c == 0, table_sib[...], table[...]),
    )


def forward_body(bands, lengths, table, table_sib, weight_far, *refs):
    core, above, below = refs[:2], refs[2:4], refs[4:6]
    before = refs[6:8]
    keep, give, active, here, weight, sem = refs[8:]
    frames, rows, cols, chans = core[0].shape
    half = rows // 2
    tm, h, c = lax.axis_index("tm"), lax.axis_index("height"), lax.axis_index("chan")
    first = tm * frames
    load = pltpu.make_async_copy(weight_far, weight, sem.at[12])
    near, place = pl.ds((half - 1) * c, half + 1), pl.ds(1 - c, half + 1)
    outside = pl.ds((half + 1) * c, 1)
    waits = []
    for n in range(2):
        waits.append(
            pltpu.make_async_copy(
                core[n].at[:, near], here.at[n, pl.ds(2, frames), place], sem.at[6 * n]
            )
        )
        waits[-1].start()
        for f in range(2):
            line = f * rows
            waits.append(
                pltpu.make_async_copy(
                    before[n].at[pl.ds(line + (half - 1) * c, half + 1)],
                    here.at[n, f, place],
                    sem.at[6 * n + 1 + f],
                )
            )
            waits[-1].start()
        for side, rim, row, line in (
            (0, above[n], rows - 1, 2 * rows),
            (1, below[n], 0, 2 * (bands - 1) * rows),
        ):
            edges = [
                pltpu.make_async_copy(
                    rim.at[:, pl.ds(row, 1)],
                    here.at[n, pl.ds(2, frames), outside],
                    sem.at[6 * n + 3],
                )
            ]
            for f in range(2):
                edges.append(
                    pltpu.make_async_copy(
                        before[n].at[pl.ds(line + f * rows + row, 1)],
                        here.at[n, f, outside],
                        sem.at[6 * n + 4 + f],
                    )
                )

            @pl.when(c == side)
            def _():
                for edge in edges:
                    edge.start()

        waits += edges
    load.start()
    for wait in waits:
        wait.wait()
    outer = jnp.logical_or(
        jnp.logical_and(c == 0, h > 0), jnp.logical_and(c == 1, h < bands - 1)
    )
    begin = [start_of(lengths, first + t) for t in range(frames)]
    tables = both(c, table, table_sib)
    cells = (half + 2) * cols
    line = iota((cells, chans), 0)
    rim = jnp.logical_or(
        jnp.logical_and(line < cols, c == 0), jnp.logical_and(line >= cells - cols, c == 1)
    )
    ok = jnp.logical_or(jnp.logical_not(rim), outer)
    for f in range(frames + 2):
        a, b = [here[n, f].reshape(cells, chans).astype(F32) for n in range(2)]
        for side, x in enumerate((jnp.where(c == 0, a, b), jnp.where(c == 0, b, a))):
            info = tables[side]
            scale = info[16 + f : 17 + f] * info[32:33]
            v = (x - info[f : f + 1]) * scale + info[33:34]
            v = jnp.where(ok, v * sigmoid(v), 0.0)
            left, right = shifts(v)
            for n, w in enumerate((left, v, right)):
                lane = n * 2 * chans + side * chans
                active[f, :, :, lane : lane + chans] = w.astype(BF16).reshape(half + 2, cols, chans)
    load.wait()
    batch = 4
    for t0 in range(0, frames, batch):
        mixed = [jnp.zeros((half * cols, 2 * chans), F32) for _ in range(batch)]
        for a in range(3):
            for b in range(3):
                w = weight[a * 3 + b]
                for q in range(batch):
                    t = t0 + q
                    s = jnp.maximum(first + t - 2 + a, begin[t]) - (first - 2)
                    patch = active[s, b : b + half].reshape(half * cols, 6 * chans)
                    mixed[q] = mixed[q] + bdot(patch, w)
        for q in range(batch):
            t = t0 + q
            mine = slice(1, half + 1)
            left, right = mixed[q][:, :chans], mixed[q][:, chans:]
            shape = (half, cols, chans)
            for out, value, x in (
                (keep, jnp.where(c == 0, left, right), here[0, t + 2, mine]),
                (give, jnp.where(c == 0, right, left), here[1, t + 2, mine]),
            ):
                x = x.reshape(half * cols, chans).astype(F32)
                out[t] = (x + value).astype(BF16).reshape(shape)


def order_body(peers, bands, cap, lengths, gain, bias, *refs):
    pieces = [refs[m * peers : (m + 1) * peers] for m in range(bands)]
    out, first, table = refs[bands * peers :]
    own, above, below = pieces[0], pieces[1], pieces[bands - 1]
    frames = out.shape[0]
    base = cap * (out.shape[1] - 1)
    tm = lax.axis_index("tm")
    count = peers * frames

    def frame_of(index):
        slab = lax.rem(tm - lax.div(index, frames) + peers, peers)
        return slab * frames + lax.rem(index, frames)

    means, spreads = [], []
    for m in range(bands):
        stats = [
            sum(piece[base + n].astype(F32) for n in (2, 1, 0)) for piece in pieces[m]
        ]
        means.append(jnp.concatenate([v[:frames] for v in stats], axis=0))
        spreads.append(jnp.concatenate([v[frames:] for v in stats], axis=0))
    clip = clip_of(lengths, frame_of(iota((count, count), 1)))
    inverse = per_clip(lengths, clip, 1.0)
    same = jnp.where(clip_of(lengths, frame_of(iota((count, count), 0))) == clip, inverse, 0.0)
    near = jnp.clip(tm * frames - 2 + iota((16, count), 0), 0, count - 1)
    picked = jnp.where(clip_of(lengths, near) == clip[:16], inverse[:16], 0.0)
    average = sum(means[1:], means[0]) * (1.0 / bands)
    clip_mean = fdot(same, average)
    spread = jnp.zeros_like(average)
    for m in range(bands):
        apart = means[m] - clip_mean
        spread = spread + (spreads[m] + apart * apart)
    table[:16] = fdot(picked, average)
    table[16:32] = lax.rsqrt(fdot(picked, spread * (1.0 / bands)) + 1e-06)
    table[32:33] = gain[...]
    table[33:34] = bias[...]
    table[34:] = jnp.zeros((6, table.shape[1]), F32)
    rows = out.shape[1] - 2
    h = lax.axis_index("height")
    names = [named(own[k], rows, cap) for k in range(peers)]
    for k in range(peers):
        for j in range(cap):
            at = j * (rows + 1)
            local = names[k][j]

            @pl.when(local >= 0)
            def _():
                out[local, 1 : rows + 1] = own[k][at : at + rows]
                top = above[k][at + rows - 1].astype(F32)
                bottom = below[k][at].astype(F32)
                out[local, 0] = jnp.where(h > 0, top, 0.0).astype(BF16)
                out[local, rows + 1] = jnp.where(h < bands - 1, bottom, 0.0).astype(BF16)

    first[...] = out[:2]


def backward_body(peers, lengths, table, table_sib, weight, own, sib, up, up_sib, next_own, next_sib, *refs):
    keep, give, sums, spatial, total = refs
    frames, rows, cols, chans = own.shape
    half = rows // 2
    cells = half * cols
    tm, c = lax.axis_index("tm"), lax.axis_index("chan")
    first = tm * frames
    for f in range(frames + 2):
        a, b, g = (up, up_sib, f) if f < frames else (next_own, next_sib, f - frames)
        a = a[g, pl.ds(c * half, half + 2)].reshape(cells + 2 * cols, chans).astype(F32)
        b = b[g, pl.ds(c * half, half + 2)].reshape(cells + 2 * cols, chans).astype(F32)
        for side, v in enumerate((jnp.where(c == 0, a, b), jnp.where(c == 0, b, a))):
            before, after = shifts(v)
            for n, w in enumerate((after, v, before)):
                at = n * 2 * chans + side * chans
                spatial[f, :, :, at : at + chans] = w.astype(BF16).reshape(half + 2, cols, chans)
    total[...] = jnp.zeros_like(total)
    tables = both(c, table, table_sib)

    begin = [start_of(lengths, first + t) for t in range(frames + 2)]
    for a in range(3):
        last = frames + 2 - a
        for low, high in ((0, last // 2), (last // 2, last)):
            grads = [jnp.zeros((cells, 2 * chans), F32) for _ in range(low, high)]
            for b in range(3):
                w = weight[a * 3 + b]
                for t in range(low, high):
                    patch = spatial[t, 2 - b : 2 - b + half].reshape(cells, 6 * chans)
                    grads[t - low] = grads[t - low] + bdot(patch, w)
            for t in range(low, high):
                s = jnp.maximum(first + t - 2 + a, begin[t]) - first
                s = jnp.where(jnp.logical_and(s >= 0, s < frames), s, frames)
                total[s] += grads[t - low]
    mine = pl.ds(c * half, half)
    member = (
        clip_of(lengths, first + iota((NCLIPS, frames), 1)) == iota((NCLIPS, frames), 0)
    ).astype(F32)
    for side in range(2):
        firsts, seconds = [], []
        for t in range(frames):
            a, b = own[t, mine].astype(F32), sib[t, mine].astype(F32)
            x = jnp.where((c == 0) == (side == 0), a, b).reshape(cells, chans)
            info = tables[side]
            hat = (x - info[t + 2 : t + 3]) * info[t + 18 : t + 19]
            v = hat * info[32:33] + info[33:34]
            s = sigmoid(v)
            grad = total[t, :, side * chans : (side + 1) * chans] * s * (1.0 + v * (1.0 - s))
            total[t, :, side * chans : (side + 1) * chans] = grad
            firsts.append(jnp.sum(grad, axis=0, keepdims=True))
            seconds.append(jnp.sum(grad * hat, axis=0, keepdims=True))
        whole = jnp.concatenate(
            [
                fdot(member, jnp.concatenate(firsts, axis=0)),
                fdot(member, jnp.concatenate(seconds, axis=0)),
            ],
            axis=0,
        )
        for i in range(sums.shape[0] // 2):
            sums[2 * i + side] = whole
    for t in range(frames):
        left, right = total[t, :, :chans], total[t, :, chans:]
        keep[t] = jnp.where(c == 0, left, right)
        give[t] = jnp.where(c == 0, right, left)


def arrive_body(*refs):
    refs[-1][...] = jnp.zeros(refs[-1].shape, F32)


def finish_body(size, bands, count, lengths, table, got, token, video, other, up, *refs):
    block_keep, block_other, keep_far = refs[:3]
    terms_far = refs[3 : 3 + count]
    out_far, block, small, grad_far = refs[3 + count : 7 + count]
    keep, out, *terms, grad, sem, done = refs[7 + count :]
    frames, rows, cols, chans = video.shape
    half = rows // 2
    cells = half * cols
    tm, c = lax.axis_index("tm"), lax.axis_index("chan")
    loads = [pltpu.make_async_copy(keep_far, keep, sem.at[count])]
    for n in range(count):
        loads.append(pltpu.make_async_copy(terms_far[n], terms[n], sem.at[n]))
    stores = [
        pltpu.make_async_copy(block_keep, block.at[:, pl.ds(c * half, half)], done.at[frames]),
        pltpu.make_async_copy(
            block_other, block.at[:, pl.ds((1 - c) * half, half)], done.at[frames + 1]
        ),
    ]
    for copy in loads + stores:
        copy.start()
    first_frame = tm * frames
    whole = jnp.sum(got[...], axis=0)
    gain = table[32:33]
    small[0:1] = jnp.sum(whole[NCLIPS:], axis=0, keepdims=True)
    small[1:2] = jnp.sum(whole[:NCLIPS], axis=0, keepdims=True)
    small[2:] = jnp.zeros((6, chans), F32)
    group = group_matrix(chans, size)
    clip = iota((frames, NCLIPS), 1)
    inverse = per_clip(lengths, clip, float(rows * bands * cols * size))
    spread = jnp.where(clip_of(lengths, first_frame + iota((frames, NCLIPS), 0)) == clip, inverse, 0.0)
    first = fdot(spread, fdot(whole[:NCLIPS] * gain, group))
    second = fdot(spread, fdot(whole[NCLIPS:] * gain, group))
    loads[0].wait()
    for t in range(frames):
        inv = table[t + 18 : t + 19]
        for grads, at in ((keep, c * half), (other, (1 - c) * half)):
            x = video[t, pl.ds(at, half)].reshape(cells, chans).astype(F32)
            hat = (x - table[t + 2 : t + 3]) * inv
            part = inv * (grads[t] * gain - first[t : t + 1] - hat * second[t : t + 1])
            u = up[t, pl.ds(at + 1, half)].reshape(cells, chans).astype(F32)
            out[t, pl.ds(at, half)] = (u + part).astype(BF16).reshape(half, cols, chans)
        stores.append(pltpu.make_async_copy(out.at[t], out_far.at[t], done.at[t]))
        stores[-1].start()
    for load in loads[1:]:
        load.wait()
    for tap in range(grad.shape[0]):
        total = terms[0][tap]
        for term in terms[1:]:
            total = total + term[tap].astype(F32)
        grad[tap] = total
    stores.append(pltpu.make_async_copy(grad, grad_far, done.at[frames + 2]))
    stores[-1].start()
    for store in stores:
        store.wait()


def per_device(
    clip_video, norm_gain, norm_bias, conv_weight, clip_lengths, packed_frame, packed_grad
):
    frames, rows, cols, chans = clip_video.shape
    full = conv_weight.shape[3]
    peers = lax.axis_size("tm")
    bands = lax.axis_size("height")
    c = lax.axis_index("chan")
    size = full // GROUPS
    cap = max(1, frames // peers)
    block = full // (peers * bands)
    width = peers * block
    half = rows // 2
    everyone = ("tm", "height", "chan")
    devices = peers * bands * 2
    sds = jax.ShapeDtypeStruct

    pieces = call(
        functools.partial(pack_body, peers, cap, size),
        [sds((cap * (rows + 1) + 3, cols, chans), BF16)] * peers,
        [SM, HB, HB],
        [
            pltpu.VMEM((peers * cap, cols, chans), BF16),
            pltpu.VMEM(clip_video.shape, BF16),
            pltpu.VMEM((3, 2 * frames, chans), BF16),
            pltpu.SemaphoreType.DMA((2 * peers * cap,)),
            pltpu.SemaphoreType.DMA((frames,)),
            pltpu.SemaphoreType.DMA((peers,)),
        ],
        name="pack", where=ANY,
    )(packed_frame, *far_away(packed_grad, clip_video))
    ups = [[pieces[0]] + [lax.ppermute(pieces[k], "tm", ring(peers, k)) for k in range(1, peers)]]

    own = [clip_video]
    for m in range(1, bands):
        own.append(lax.ppermute(clip_video, "height", ring(bands, m)))
    sib = [sibling(v) for v in own]
    for m in range(1, bands):
        ready = [v for k, v in enumerate(ups[0])]
        ups.append([lax.ppermute(v, "height", ring(bands, m)) for v in ready])
    prev = jnp.concatenate([v[frames - 2 :] for v in own], axis=0)
    prev = prev.reshape(2 * bands * rows, cols, chans)
    prev = lax.ppermute(prev, "tm", [(t, t + 1) for t in range(peers - 1)])
    prev_sib = sibling(prev)

    weight = conv_weight.reshape(9, 3 * full, full)
    turned = call(
        turn_body, sds(weight.shape, BF16), [VM], name="turn"
    )(weight)

    up, up_first, table = call(
        functools.partial(order_body, peers, bands, cap),
        [
            sds((frames, rows + 2, cols, chans), BF16),
            sds((2, rows + 2, cols, chans), BF16),
            sds((40, chans), F32),
        ],
        [SM] + [VM] * (2 + bands * peers),
        name="order",
    )(
        clip_lengths, norm_gain[None], norm_bias[None], after(ups[0][0], turned),
        *ups[0][1:], *[v for band in ups[1:] for v in band],
    )
    table_sib = sibling(table)

    grads = call(
        functools.partial(weight_body, peers, bands, cap, block),
        [sds((27, block, chans), F32)] + [sds((27, block, chans), BF16)] * (peers - 1),
        [SM] + [VM] * (4 + 2 * bands + peers * bands),
        [
            pltpu.VMEM((3, frames + 2, bands * rows + 2, cols, width), BF16),
            pltpu.VMEM((frames, bands, chans, rows * cols), BF16),
        ],
        name="weight",
    )(
        clip_lengths, table, table_sib, *own, *sib, prev, prev_sib,
        *[v for band in ups for v in band],
    )
    far = bands - 1
    up_sib = sibling(up)
    next_own = lax.ppermute(up_first, "tm", [(t + 1, t) for t in range(peers - 1)])
    next_sib = sibling(next_own)
    part = sds((frames, half * cols, chans), F32)
    keep, give, sums = call(
        functools.partial(backward_body, peers),
        [part, part, sds((devices, 2 * NCLIPS, chans), F32)],
        [SM] + [VM] * 9,
        [
            pltpu.VMEM((frames + 2, half + 2, cols, 6 * chans), BF16),
            pltpu.VMEM((frames + 1, half * cols, 2 * chans), F32),
        ],
        name="backward",
    )(clip_lengths, table, table_sib, after(turned, grads[0]), clip_video, sib[0], up, up_sib, next_own, next_sib)
    totals = lax.all_to_all(sums, everyone, 0, 0)
    other = sibling(give)

    part = sds((frames, half, cols, chans), BF16)
    block_keep, block_give = call(
        functools.partial(forward_body, bands),
        [part, part],
        [SM, VM, VM] + [HB] * 9,
        [
            pltpu.VMEM((frames + 2, half + 2, cols, 6 * chans), BF16),
            pltpu.VMEM((2, frames + 2, half + 2, cols, chans), BF16),
            pltpu.VMEM(weight.shape, BF16),
            pltpu.SemaphoreType.DMA((13,)),
        ],
        name="forward",
    )(
        clip_lengths, table, table_sib, *far_away(
            after(weight, sums), own[0], sib[0], own[1], sib[1], own[far], sib[far],
            prev, prev_sib,
        ),
    )
    arrived = [lax.ppermute(grads[k], "tm", ring(peers, k)) for k in range(1, peers)]
    terms = far_away(after(grads[0], block_give), *arrived)
    token = call(
        arrive_body, sds((8, chans), F32), [HB] * peers, name="arrive", work=10**13
    )(*terms)
    block_other = sibling(after(block_give, arrived[-1]))
    video_grad, block_out, small, weight_grad = call(
        functools.partial(finish_body, size, bands, peers),
        [sds(clip_video.shape, BF16)] * 2
        + [sds((8, chans), F32), sds((27, block, chans), F32)],
        [SM] + [VM] * 8 + [HB] * (1 + peers),
        [
            pltpu.VMEM((frames, half * cols, chans), F32),
            pltpu.VMEM(clip_video.shape, BF16),
            pltpu.VMEM((27, block, chans), F32),
        ]
        + [pltpu.VMEM((27, block, chans), BF16)] * (peers - 1)
        + [
            pltpu.VMEM((27, block, chans), F32),
            pltpu.SemaphoreType.DMA((peers + 1,)),
            pltpu.SemaphoreType.DMA((frames + 3,)),
        ],
        name="finish", where=[ANY, ANY, VM, ANY],
    )(
        clip_lengths, table, totals, token, clip_video, other, up, block_keep, block_other,
        *far_away(keep), *terms,
    )
    weight_grad = weight_grad.reshape(3, 3, 3, block, chans)
    return (block_out, video_grad, weight_grad, small[0], small[1])


def solution(mesh):
    placed = (
        P(("groups", "tm"), "height", None, "chan"),
        P("chan"),
        P("chan"),
        P(),
        P("groups"),
        P(("groups", "tm")),
        P(("groups", "tm"), "height", None, "chan"),
    )
    return jax.shard_map(
        per_device,
        mesh=mesh,
        in_specs=placed,
        out_specs=(
            P(("groups", "tm"), "height", None, "chan"),
            P(("groups", "tm"), "height", None, "chan"),
            P("groups", None, None, ("tm", "height"), "chan"),
            P(("groups", "chan")),
            P(("groups", "chan")),
        ),
        check_vma=False,
    )
```

```python
import functools
import jax
import jax.numpy as jnp
from jax import lax
from jax.experimental import pallas as pl
from jax.experimental.pallas import tpu as pltpu
from jax.sharding import PartitionSpec as P

GROUPS = 32
NCLIPS = 8
F32 = jnp.float32
BF16 = jnp.bfloat16
HIGHEST = lax.Precision.HIGHEST
VM = pl.BlockSpec(memory_space=pltpu.VMEM)
SM = pl.BlockSpec(memory_space=pltpu.SMEM)


ANY = pl.BlockSpec(memory_space=pl.ANY)
HB = pl.BlockSpec(memory_space=pltpu.HBM)


def after(value, *others):
    return lax.optimization_barrier((value, *others))[0]


def call(body, out_shape, in_specs, scratch=(), name=None, room=20, where=VM, work=1024):
    return pl.pallas_call(
        body,
        out_shape=out_shape,
        in_specs=in_specs,
        out_specs=jax.tree.map(lambda _: where, out_shape),
        scratch_shapes=list(scratch),
        compiler_params=pltpu.CompilerParams(vmem_limit_bytes=room * 2**20),
        cost_estimate=pl.CostEstimate(flops=work, bytes_accessed=1024, transcendentals=0),
        name=name,
    )


def far_away(*values):
    return [pltpu.with_memory_space_constraint(v, pltpu.HBM) for v in values]


def fdot(a, b):
    return jnp.dot(a, b, precision=HIGHEST, preferred_element_type=F32)


def bdot(a, b):
    return jnp.dot(a, b, preferred_element_type=F32)


def ring(peers, by):
    return [(i, (i + by) % peers) for i in range(peers)]


def sibling(value):
    return lax.ppermute(value, "chan", ring(2, 1))


def sigmoid(v):
    return 1.0 / (1.0 + jnp.exp(-v))


def start_of(lengths, frame):
    begin = jnp.int32(0)
    end = jnp.int32(0)
    for k in range(NCLIPS):
        end = end + lengths[k]
        begin = jnp.where(end <= frame, end, begin)
    return begin


def clip_of(lengths, frame):
    number = jnp.zeros(frame.shape, jnp.int32)
    end = jnp.int32(0)
    for k in range(NCLIPS):
        end = end + lengths[k]
        number = number + jnp.where(end <= frame, 1, 0)
    return number


def per_clip(lengths, clip, scale):
    inverse = jnp.zeros(clip.shape, F32)
    for k in range(NCLIPS):
        length = jnp.full(clip.shape, lengths[k].astype(F32) * scale, F32)
        inverse = jnp.where(clip == k, 1.0 / length, inverse)
    return inverse


def iota(shape, dim):
    return lax.broadcasted_iota(jnp.int32, shape, dim)


def group_matrix(chans, size):
    return (iota((chans, chans), 0) // size == iota((chans, chans), 1) // size).astype(F32)


def split(value):
    parts = []
    for _ in range(3):
        part = value.astype(BF16)
        parts.append(part)
        value = value - part.astype(F32)
    return parts


def pack_body(peers, cap, size, frames, grad, video_far, *refs):
    outs = refs[:peers]
    names, video, stats, sem, far, done = refs[peers:]
    slots, rows, cols, chans = grad.shape
    cells = rows * cols
    loads = [
        pltpu.make_async_copy(video_far.at[t], video.at[t], far.at[t]) for t in range(slots)
    ]
    for load in loads:
        load.start()
    tm = lax.axis_index("tm")
    number = [frames[i] for i in range(slots)]
    step = [lax.rem(lax.div(n, slots) - tm + peers, peers) for n in number]
    rank = []
    for i in range(slots):
        r = jnp.int32(0)
        for j in range(i):
            r = r + jnp.where(step[j] == step[i], 1, 0)
        rank.append(r)
    copies = []
    for k in range(peers):
        for j in range(cap):
            at = j * (rows + 1)
            index = jnp.int32(0)
            local = jnp.int32(-1)
            for i in range(slots):
                hit = jnp.logical_and(step[i] == k, rank[i] == j)
                index = jnp.where(hit, i, index)
                local = jnp.where(hit, lax.rem(number[i], slots), local)
            n = 2 * (k * cap + j)
            names[k * cap + j] = jnp.full(grad.shape[2:], local.astype(F32), F32).astype(BF16)
            copies += [
                pltpu.make_async_copy(grad.at[index], outs[k].at[pl.ds(at, rows)], sem.at[n]),
                pltpu.make_async_copy(
                    names.at[pl.ds(k * cap + j, 1)], outs[k].at[pl.ds(at + rows, 1)], sem.at[n + 1]
                ),
            ]
            copies[-2].start()
            copies[-1].start()
    base = cap * (rows + 1)
    average = group_matrix(chans, size) * (1.0 / size)
    sums = []
    for t in range(slots):
        loads[t].wait()
        sums.append(jnp.sum(video[t].astype(F32).reshape(cells, chans), axis=0, keepdims=True))
    mean = fdot(jnp.concatenate(sums, axis=0) * (1.0 / cells), average)
    squares = []
    for t in range(slots):
        apart = video[t].astype(F32).reshape(cells, chans) - mean[t : t + 1]
        squares.append(jnp.sum(apart * apart, axis=0, keepdims=True))
    var = fdot(jnp.concatenate(squares, axis=0) * (1.0 / cells), average)
    for n, part in enumerate(split(jnp.concatenate([mean, var], axis=0))):
        stats[n] = part
    for k in range(peers):
        copies.append(pltpu.make_async_copy(stats, outs[k].at[pl.ds(base, 3)], done.at[k]))
        copies[-1].start()
    for copy in copies:
        copy.wait()


def named(piece, rows, cap):
    return [
        jnp.max(piece[j * (rows + 1) + rows].astype(F32)).astype(jnp.int32) for j in range(cap)
    ]


def turn_body(weight, out):
    for i in range(9):
        for col in range(3):
            out[i, col * 256 : (col + 1) * 256] = weight[i, col * 256 : (col + 1) * 256].T


def shifts(value):
    length = value.shape[0]
    column = lax.rem(iota(value.shape, 0), 16)
    before = jnp.where(column == 0, 0.0, pltpu.roll(value, 1, 0))
    after = jnp.where(column == 15, 0.0, pltpu.roll(value, length - 1, 0))
    return before, after


def weight_body(peers, bands, cap, block, *refs):
    refs = list(refs)
    lengths, table, table_sib = [refs.pop(0) for _ in range(3)]
    take = lambda n: [refs.pop(0) for _ in range(n)]
    own, sib = take(bands), take(bands)
    prev, prev_sib = take(2)
    ups = [take(peers) for _ in range(bands)]
    outs = take(peers)
    active, upright = refs
    frames, rows, cols, chans = own[0].shape
    cells = rows * cols
    width = peers * block
    tm, h, c = lax.axis_index("tm"), lax.axis_index("height"), lax.axis_index("chan")
    first = tm * frames
    band = [lax.rem(h - m + bands, bands) for m in range(bands)]
    place = iota((chans, width), 1)
    wanted = (lax.rem(tm + lax.div(place, block), peers) * bands + h) * block + lax.rem(place, block)
    channel = iota((chans, width), 0)
    pick_own = (c * chans + channel == wanted).astype(F32)
    pick_sib = ((1 - c) * chans + channel == wanted).astype(F32)
    lookup = fdot(table[...], pick_own) + fdot(table_sib[...], pick_sib)
    pick_own, pick_sib = pick_own.astype(BF16), pick_sib.astype(BF16)
    mean, inv = lookup[:16], lookup[16:32]
    scale = inv * lookup[32:33]
    bias = lookup[33:34]
    names = [named(ups[0][k], rows, cap) for k in range(peers)]
    for col in range(3):
        active[col, :, 0] = jnp.zeros((frames + 2, cols, width), BF16)
        active[col, :, bands * rows + 1] = jnp.zeros((frames + 2, cols, width), BF16)
    for f in range(frames + 2):
        for m in range(bands):
            if f < 2:
                at = (2 * m + f) * rows
                a, b = prev[at : at + rows], prev_sib[at : at + rows]
            else:
                a, b = own[m][f - 2], sib[m][f - 2]
            x = bdot(a.reshape(cells, chans), pick_own) + bdot(b.reshape(cells, chans), pick_sib)
            v = (x - mean[f : f + 1]) * scale[f : f + 1] + bias
            v = v * sigmoid(v)
            before, after = shifts(v)
            at = pl.ds(band[m] * rows + 1, rows)
            for col, moved in enumerate((before, v, after)):
                active[col, f, at] = moved.astype(BF16).reshape(rows, cols, width)
    for k in range(peers):
        for j in range(cap):
            at = j * (rows + 1)
            local = names[k][j]

            @pl.when(local >= 0)
            def _():
                for m in range(bands):
                    u = ups[m][k][at : at + rows].reshape(cells, chans)
                    at_lane = pl.multiple_of(band[m] * cells, cells)
                    upright[local, :, pl.ds(at_lane, cells)] = u.T

    begin = [start_of(lengths, first + t) for t in range(frames)]

    def taps(i, count):
        where = []
        for n in range(count):
            tap = 2 * i + n
            a = lax.div(tap, 9)
            where.append((a, lax.rem(lax.div(tap, 3), 3), lax.rem(tap, 3)))
        total = jnp.zeros((chans, count * width), F32)
        for t in range(frames):
            patch = []
            for a, b, col in where:
                s = jnp.maximum(first + t - 2 + a, begin[t]) - (first - 2)
                lines = active[col, s, pl.ds(b, bands * rows)]
                patch.append(lines.reshape(bands * cells, width))
            patch = jnp.concatenate(patch, axis=1) if count > 1 else patch[0]
            total = total + bdot(upright[t], patch)
        for n in range(count):
            piece = total[:, n * width : (n + 1) * width].T
            for k in range(peers):
                outs[k][2 * i + n] = piece[k * block : (k + 1) * block].astype(outs[k].dtype)

    def pair(i, carry):
        taps(i, 2)
        return carry

    lax.fori_loop(0, 13, pair, 0)
    taps(jnp.int32(13), 1)


def both(c, table, table_sib):
    return (
        jnp.where(c == 0, table[...], table_sib[...]),
        jnp.where(c == 0, table_sib[...], table[...]),
    )


def forward_body(bands, lengths, table, table_sib, weight_far, *refs):
    core, above, below = refs[:2], refs[2:4], refs[4:6]
    before = refs[6:8]
    keep, give, active, here, weight, sem = refs[8:]
    frames, rows, cols, chans = core[0].shape
    half = rows // 2
    tm, h, c = lax.axis_index("tm"), lax.axis_index("height"), lax.axis_index("chan")
    first = tm * frames
    load = pltpu.make_async_copy(weight_far, weight, sem.at[12])
    near, place = pl.ds((half - 1) * c, half + 1), pl.ds(1 - c, half + 1)
    outside = pl.ds((half + 1) * c, 1)
    waits = []
    for n in range(2):
        waits.append(
            pltpu.make_async_copy(
                core[n].at[:, near], here.at[n, pl.ds(2, frames), place], sem.at[6 * n]
            )
        )
        waits[-1].start()
        for f in range(2):
            line = f * rows
            waits.append(
                pltpu.make_async_copy(
                    before[n].at[pl.ds(line + (half - 1) * c, half + 1)],
                    here.at[n, f, place],
                    sem.at[6 * n + 1 + f],
                )
            )
            waits[-1].start()
        for side, rim, row, line in (
            (0, above[n], rows - 1, 2 * rows),
            (1, below[n], 0, 2 * (bands - 1) * rows),
        ):
            edges = [
                pltpu.make_async_copy(
                    rim.at[:, pl.ds(row, 1)],
                    here.at[n, pl.ds(2, frames), outside],
                    sem.at[6 * n + 3],
                )
            ]
            for f in range(2):
                edges.append(
                    pltpu.make_async_copy(
                        before[n].at[pl.ds(line + f * rows + row, 1)],
                        here.at[n, f, outside],
                        sem.at[6 * n + 4 + f],
                    )
                )

            @pl.when(c == side)
            def _():
                for edge in edges:
                    edge.start()

        waits += edges
    load.start()
    for wait in waits:
        wait.wait()
    outer = jnp.logical_or(
        jnp.logical_and(c == 0, h > 0), jnp.logical_and(c == 1, h < bands - 1)
    )
    begin = [start_of(lengths, first + t) for t in range(frames)]
    tables = both(c, table, table_sib)
    cells = (half + 2) * cols
    line = iota((cells, chans), 0)
    rim = jnp.logical_or(
        jnp.logical_and(line < cols, c == 0), jnp.logical_and(line >= cells - cols, c == 1)
    )
    ok = jnp.logical_or(jnp.logical_not(rim), outer)
    for f in range(frames + 2):
        a, b = [here[n, f].reshape(cells, chans).astype(F32) for n in range(2)]
        for side, x in enumerate((jnp.where(c == 0, a, b), jnp.where(c == 0, b, a))):
            info = tables[side]
            scale = info[16 + f : 17 + f] * info[32:33]
            v = (x - info[f : f + 1]) * scale + info[33:34]
            v = jnp.where(ok, v * sigmoid(v), 0.0)
            left, right = shifts(v)
            for n, w in enumerate((left, v, right)):
                lane = n * 2 * chans + side * chans
                active[f, :, :, lane : lane + chans] = w.astype(BF16).reshape(half + 2, cols, chans)
    load.wait()
    batch = 4
    for t0 in range(0, frames, batch):
        mixed = [jnp.zeros((half * cols, 2 * chans), F32) for _ in range(batch)]
        for a in range(3):
            for b in range(3):
                w = weight[a * 3 + b]
                for q in range(batch):
                    t = t0 + q
                    s = jnp.maximum(first + t - 2 + a, begin[t]) - (first - 2)
                    patch = active[s, b : b + half].reshape(half * cols, 6 * chans)
                    mixed[q] = mixed[q] + bdot(patch, w)
        for q in range(batch):
            t = t0 + q
            mine = slice(1, half + 1)
            left, right = mixed[q][:, :chans], mixed[q][:, chans:]
            shape = (half, cols, chans)
            for out, value, x in (
                (keep, jnp.where(c == 0, left, right), here[0, t + 2, mine]),
                (give, jnp.where(c == 0, right, left), here[1, t + 2, mine]),
            ):
                x = x.reshape(half * cols, chans).astype(F32)
                out[t] = (x + value).astype(BF16).reshape(shape)


def order_body(peers, bands, cap, lengths, gain, bias, *refs):
    pieces = [refs[m * peers : (m + 1) * peers] for m in range(bands)]
    out, first, table = refs[bands * peers :]
    own, above, below = pieces[0], pieces[1], pieces[bands - 1]
    frames = out.shape[0]
    base = cap * (out.shape[1] - 1)
    tm = lax.axis_index("tm")
    count = peers * frames

    def frame_of(index):
        slab = lax.rem(tm - lax.div(index, frames) + peers, peers)
        return slab * frames + lax.rem(index, frames)

    means, spreads = [], []
    for m in range(bands):
        stats = [
            sum(piece[base + n].astype(F32) for n in (2, 1, 0)) for piece in pieces[m]
        ]
        means.append(jnp.concatenate([v[:frames] for v in stats], axis=0))
        spreads.append(jnp.concatenate([v[frames:] for v in stats], axis=0))
    clip = clip_of(lengths, frame_of(iota((count, count), 1)))
    inverse = per_clip(lengths, clip, 1.0)
    same = jnp.where(clip_of(lengths, frame_of(iota((count, count), 0))) == clip, inverse, 0.0)
    near = jnp.clip(tm * frames - 2 + iota((16, count), 0), 0, count - 1)
    picked = jnp.where(clip_of(lengths, near) == clip[:16], inverse[:16], 0.0)
    average = sum(means[1:], means[0]) * (1.0 / bands)
    clip_mean = fdot(same, average)
    spread = jnp.zeros_like(average)
    for m in range(bands):
        apart = means[m] - clip_mean
        spread = spread + (spreads[m] + apart * apart)
    table[:16] = fdot(picked, average)
    table[16:32] = lax.rsqrt(fdot(picked, spread * (1.0 / bands)) + 1e-06)
    table[32:33] = gain[...]
    table[33:34] = bias[...]
    table[34:] = jnp.zeros((6, table.shape[1]), F32)
    rows = out.shape[1] - 2
    h = lax.axis_index("height")
    names = [named(own[k], rows, cap) for k in range(peers)]
    for k in range(peers):
        for j in range(cap):
            at = j * (rows + 1)
            local = names[k][j]

            @pl.when(local >= 0)
            def _():
                out[local, 1 : rows + 1] = own[k][at : at + rows]
                top = above[k][at + rows - 1].astype(F32)
                bottom = below[k][at].astype(F32)
                out[local, 0] = jnp.where(h > 0, top, 0.0).astype(BF16)
                out[local, rows + 1] = jnp.where(h < bands - 1, bottom, 0.0).astype(BF16)

    first[...] = out[:2]


def backward_body(peers, lengths, table, table_sib, weight, own, sib, up, up_sib, next_own, next_sib, *refs):
    keep, give, sums, spatial, total = refs
    frames, rows, cols, chans = own.shape
    half = rows // 2
    cells = half * cols
    tm, c = lax.axis_index("tm"), lax.axis_index("chan")
    first = tm * frames
    for f in range(frames + 2):
        a, b, g = (up, up_sib, f) if f < frames else (next_own, next_sib, f - frames)
        a = a[g, pl.ds(c * half, half + 2)].reshape(cells + 2 * cols, chans).astype(F32)
        b = b[g, pl.ds(c * half, half + 2)].reshape(cells + 2 * cols, chans).astype(F32)
        for side, v in enumerate((jnp.where(c == 0, a, b), jnp.where(c == 0, b, a))):
            before, after = shifts(v)
            for n, w in enumerate((after, v, before)):
                at = n * 2 * chans + side * chans
                spatial[f, :, :, at : at + chans] = w.astype(BF16).reshape(half + 2, cols, chans)
    total[...] = jnp.zeros_like(total)
    tables = both(c, table, table_sib)

    begin = [start_of(lengths, first + t) for t in range(frames + 2)]
    for a in range(3):
        last = frames + 2 - a
        for low, high in ((0, last // 2), (last // 2, last)):
            grads = [jnp.zeros((cells, 2 * chans), F32) for _ in range(low, high)]
            for b in range(3):
                w = weight[a * 3 + b]
                for t in range(low, high):
                    patch = spatial[t, 2 - b : 2 - b + half].reshape(cells, 6 * chans)
                    grads[t - low] = grads[t - low] + bdot(patch, w)
            for t in range(low, high):
                s = jnp.maximum(first + t - 2 + a, begin[t]) - first
                s = jnp.where(jnp.logical_and(s >= 0, s < frames), s, frames)
                total[s] += grads[t - low]
    mine = pl.ds(c * half, half)
    member = (
        clip_of(lengths, first + iota((NCLIPS, frames), 1)) == iota((NCLIPS, frames), 0)
    ).astype(F32)
    for side in range(2):
        firsts, seconds = [], []
        for t in range(frames):
            a, b = own[t, mine].astype(F32), sib[t, mine].astype(F32)
            x = jnp.where((c == 0) == (side == 0), a, b).reshape(cells, chans)
            info = tables[side]
            hat = (x - info[t + 2 : t + 3]) * info[t + 18 : t + 19]
            v = hat * info[32:33] + info[33:34]
            s = sigmoid(v)
            grad = total[t, :, side * chans : (side + 1) * chans] * s * (1.0 + v * (1.0 - s))
            total[t, :, side * chans : (side + 1) * chans] = grad
            firsts.append(jnp.sum(grad, axis=0, keepdims=True))
            seconds.append(jnp.sum(grad * hat, axis=0, keepdims=True))
        whole = jnp.concatenate(
            [
                fdot(member, jnp.concatenate(firsts, axis=0)),
                fdot(member, jnp.concatenate(seconds, axis=0)),
            ],
            axis=0,
        )
        for i in range(sums.shape[0] // 2):
            sums[2 * i + side] = whole
    for t in range(frames):
        left, right = total[t, :, :chans], total[t, :, chans:]
        keep[t] = jnp.where(c == 0, left, right)
        give[t] = jnp.where(c == 0, right, left)


def collect_body(*refs):
    count = len(refs) // 2 - 1
    far, out, near, sem = refs[:count], refs[count], refs[count + 1 : -1], refs[-1]
    loads = [pltpu.make_async_copy(far[n], near[n], sem.at[n]) for n in range(count)]
    for load in loads:
        load.start()
    for load in loads:
        load.wait()
    for tap in range(out.shape[0]):
        total = near[0][tap]
        for term in near[1:]:
            total = total + term[tap].astype(F32)
        out[tap] = total


def finish_body(size, bands, lengths, table, got, video, keep_far, other, up, block_keep, block_other, out, block, small, keep, sem):
    load = pltpu.make_async_copy(keep_far, keep, sem)
    load.start()
    frames, rows, cols, chans = video.shape
    half = rows // 2
    cells = half * cols
    tm, c = lax.axis_index("tm"), lax.axis_index("chan")
    first_frame = tm * frames
    whole = jnp.sum(got[...], axis=0)
    gain = table[32:33]
    small[0:1] = jnp.sum(whole[NCLIPS:], axis=0, keepdims=True)
    small[1:2] = jnp.sum(whole[:NCLIPS], axis=0, keepdims=True)
    small[2:] = jnp.zeros((6, chans), F32)
    group = group_matrix(chans, size)
    clip = iota((frames, NCLIPS), 1)
    inverse = per_clip(lengths, clip, float(rows * bands * cols * size))
    spread = jnp.where(clip_of(lengths, first_frame + iota((frames, NCLIPS), 0)) == clip, inverse, 0.0)
    first = fdot(spread, fdot(whole[:NCLIPS] * gain, group))
    second = fdot(spread, fdot(whole[NCLIPS:] * gain, group))
    load.wait()
    for t in range(frames):
        block[t, pl.ds(c * half, half)] = block_keep[t]
        block[t, pl.ds((1 - c) * half, half)] = block_other[t]
        inv = table[t + 18 : t + 19]
        for grads, at in ((keep, c * half), (other, (1 - c) * half)):
            x = video[t, pl.ds(at, half)].reshape(cells, chans).astype(F32)
            hat = (x - table[t + 2 : t + 3]) * inv
            part = inv * (grads[t] * gain - first[t : t + 1] - hat * second[t : t + 1])
            u = up[t, pl.ds(at + 1, half)].reshape(cells, chans).astype(F32)
            out[t, pl.ds(at, half)] = (u + part).astype(BF16).reshape(half, cols, chans)


def per_device(
    clip_video, norm_gain, norm_bias, conv_weight, clip_lengths, packed_frame, packed_grad
):
    frames, rows, cols, chans = clip_video.shape
    full = conv_weight.shape[3]
    peers = lax.axis_size("tm")
    bands = lax.axis_size("height")
    c = lax.axis_index("chan")
    size = full // GROUPS
    cap = max(1, frames // peers)
    block = full // (peers * bands)
    width = peers * block
    half = rows // 2
    everyone = ("tm", "height", "chan")
    devices = peers * bands * 2
    sds = jax.ShapeDtypeStruct

    pieces = call(
        functools.partial(pack_body, peers, cap, size),
        [sds((cap * (rows + 1) + 3, cols, chans), BF16)] * peers,
        [SM, HB, HB],
        [
            pltpu.VMEM((peers * cap, cols, chans), BF16),
            pltpu.VMEM(clip_video.shape, BF16),
            pltpu.VMEM((3, 2 * frames, chans), BF16),
            pltpu.SemaphoreType.DMA((2 * peers * cap,)),
            pltpu.SemaphoreType.DMA((frames,)),
            pltpu.SemaphoreType.DMA((peers,)),
        ],
        name="pack", where=ANY,
    )(packed_frame, *far_away(packed_grad, clip_video))
    ups = [[pieces[0]] + [lax.ppermute(pieces[k], "tm", ring(peers, k)) for k in range(1, peers)]]

    own = [clip_video]
    for m in range(1, bands):
        own.append(lax.ppermute(after(clip_video, pieces[0]), "height", ring(bands, m)))
    sib = [sibling(v) for v in own]
    for m in range(1, bands):
        ready = [v for k, v in enumerate(ups[0])]
        ups.append([lax.ppermute(v, "height", ring(bands, m)) for v in ready])
    prev = jnp.concatenate([v[frames - 2 :] for v in own], axis=0)
    prev = prev.reshape(2 * bands * rows, cols, chans)
    prev = lax.ppermute(prev, "tm", [(t, t + 1) for t in range(peers - 1)])
    prev_sib = sibling(prev)

    weight = conv_weight.reshape(9, 3 * full, full)
    turned = call(
        turn_body, sds(weight.shape, BF16), [VM], name="turn"
    )(weight)

    up, up_first, table = call(
        functools.partial(order_body, peers, bands, cap),
        [
            sds((frames, rows + 2, cols, chans), BF16),
            sds((2, rows + 2, cols, chans), BF16),
            sds((40, chans), F32),
        ],
        [SM] + [VM] * (2 + bands * peers),
        name="order",
    )(
        clip_lengths, norm_gain[None], norm_bias[None], after(ups[0][0], turned),
        *ups[0][1:], *[v for band in ups[1:] for v in band],
    )
    table_sib = sibling(table)

    grads = call(
        functools.partial(weight_body, peers, bands, cap, block),
        [sds((27, block, chans), F32)] + [sds((27, block, chans), BF16)] * (peers - 1),
        [SM] + [VM] * (4 + 2 * bands + peers * bands),
        [
            pltpu.VMEM((3, frames + 2, bands * rows + 2, cols, width), BF16),
            pltpu.VMEM((frames, chans, bands * rows * cols), BF16),
        ],
        name="weight",
    )(
        clip_lengths, table, table_sib, *own, *sib, prev, prev_sib,
        *[v for band in ups for v in band],
    )
    far = bands - 1
    up_sib = sibling(up)
    next_own = lax.ppermute(up_first, "tm", [(t + 1, t) for t in range(peers - 1)])
    next_sib = sibling(next_own)
    part = sds((frames, half * cols, chans), F32)
    keep, give, sums = call(
        functools.partial(backward_body, peers),
        [part, part, sds((devices, 2 * NCLIPS, chans), F32)],
        [SM] + [VM] * 9,
        [
            pltpu.VMEM((frames + 2, half + 2, cols, 6 * chans), BF16),
            pltpu.VMEM((frames + 1, half * cols, 2 * chans), F32),
        ],
        name="backward",
    )(clip_lengths, table, table_sib, after(turned, grads[0]), clip_video, sib[0], up, up_sib, next_own, next_sib)
    totals = lax.all_to_all(sums, everyone, 0, 0)
    other = sibling(give)

    part = sds((frames, half, cols, chans), BF16)
    block_keep, block_give = call(
        functools.partial(forward_body, bands),
        [part, part],
        [SM, VM, VM] + [HB] * 9,
        [
            pltpu.VMEM((frames + 2, half + 2, cols, 6 * chans), BF16),
            pltpu.VMEM((2, frames + 2, half + 2, cols, chans), BF16),
            pltpu.VMEM(weight.shape, BF16),
            pltpu.SemaphoreType.DMA((13,)),
        ],
        name="forward",
    )(
        clip_lengths, table, table_sib, *far_away(
            after(weight, sums), own[0], sib[0], own[1], sib[1], own[far], sib[far],
            prev, prev_sib,
        ),
    )
    terms = [lax.ppermute(grads[k], "tm", ring(peers, k)) for k in range(1, peers)]
    weight_grad = call(
        collect_body, sds((27, block, chans), F32), [HB] * peers,
        [pltpu.VMEM((27, block, chans), F32)]
        + [pltpu.VMEM((27, block, chans), BF16)] * (peers - 1)
        + [pltpu.SemaphoreType.DMA((peers,))],
        name="collect", work=10**13,
    )(*far_away(after(grads[0], block_give), *terms))
    weight_grad = weight_grad.reshape(3, 3, 3, block, chans)

    block_other = sibling(after(block_give, terms[-1]))
    video_grad, block_out, small = call(
        functools.partial(finish_body, size, bands),
        [sds(clip_video.shape, BF16)] * 2 + [sds((8, chans), F32)],
        [SM] + [VM] * 3 + [HB] + [VM] * 4,
        [pltpu.VMEM((frames, half * cols, chans), F32), pltpu.SemaphoreType.DMA],
        name="finish",
    )(clip_lengths, table, after(totals, weight_grad), clip_video, *far_away(keep), other, up, block_keep, block_other)
    return (block_out, video_grad, weight_grad, small[0], small[1])


def solution(mesh):
    placed = (
        P(("groups", "tm"), "height", None, "chan"),
        P("chan"),
        P("chan"),
        P(),
        P("groups"),
        P(("groups", "tm")),
        P(("groups", "tm"), "height", None, "chan"),
    )
    return jax.shard_map(
        per_device,
        mesh=mesh,
        in_specs=placed,
        out_specs=(
            P(("groups", "tm"), "height", None, "chan"),
            P(("groups", "tm"), "height", None, "chan"),
            P("groups", None, None, ("tm", "height"), "chan"),
            P(("groups", "chan")),
            P(("groups", "chan")),
        ),
        check_vma=False,
    )
```
